128 devices in a mesh: ctx: 16 (over y, x), mem: 4 (over z), half: 2 (over core).
Axes of the slice: x: 4, y: 4, z: 4, core: 2. Of those that a mesh axis runs over, the one named last changes fastest.
Arguments:
- tokens: bfloat16 [32768, 2048], P(('ctx', 'mem')), may hold values from -6 to 6
- routes: int32 [32768, 1], P(('ctx', 'mem')), may hold values from 0 to 15; in each aligned block of 512 rows (0 to 511, 512 to 1023, ...) at most 64 rows name the same one
- w_query: bfloat16 [2048, 1024], P(None, 'half'), may hold values from -0.125 to 0.125
- w_key: bfloat16 [16, 2048, 1024], P('mem', None, 'half'), may hold values from -0.125 to 0.125
- w_value: bfloat16 [16, 2048, 1024], P('mem', None, 'half'), may hold values from -0.125 to 0.125
- w_beta: bfloat16 [16, 2048, 8], P('mem', None, 'half'), may hold values from -0.125 to 0.125
- w_decay: bfloat16 [16, 2048, 8], P('mem', None, 'half'), may hold values from -0.125 to 0.125
- decay_rate: float32 [16, 8], P('mem', 'half'), may hold values from 0.002 to 0.2
- norm_gain: float32 [1024], P('half'), may hold values from 0.1 to 1.9
- w_out: bfloat16 [1024, 2048], P('half'), may hold values from -0.1875 to 0.1875
Outputs:
- mixed: bfloat16 [32768, 2048], P(('ctx', 'mem', 'half'))
The draws below stay inside these ranges and needn't reach their ends.
Inputs may be any that keep to these rules, and one draw needn't show every extreme that they name: `routes`: each token names one memory. Within each aligned block of 512 rows no memory is named by more than 64 rows, and in some blocks one memory is named by exactly 64 rows.
All inputs are finite; a program needn't handle non-finite values.
Results may differ from the reference program's by a relative error of at most 0.0049.
Values may be sent and summed in bfloat16 or wider, within the bound.
A program may use at most 192 MiB of HBM per device.

```python
import math
import jax
import jax.numpy as jnp
import numpy as np
from jax import lax

D = 2048
HEADS = 8
DK = 128
DV = 128
TOK_DEV = 512
MEMS = 16
CAP = 64
TOKENS = 32768


def steps_of(key, dims, cuts, smallest, high):
    factor_of = 1.0
    for axis_at, shards_of in cuts:
        steps = jax.random.uniform(jax.random.fold_in(jax.random.fold_in(key, 6), axis_at), (shards_of,), jnp.float32, smallest / len(cuts), high / len(cuts))
        factor_of = factor_of * jnp.repeat(jnp.exp(steps), dims[axis_at] // shards_of).reshape((-1,) + (1,) * (len(dims) - 1 - axis_at))
    return factor_of


def shared_out(key, own, number, rows, amount, top, limit, skew):
    sequence = jax.random.permutation(key, amount)
    heavy_load, ordinary = shares(amount, rows * top, limit, skew, True), shares(amount, rows * top, limit, skew, False)
    places = jnp.arange(amount)

    def named(sizes, offset_by):
        used = int((sizes > 0).sum())
        fixed = max(1, used // 4)
        shifted = fixed + (places - fixed + offset_by * (used - fixed)) % max(1, amount - fixed)
        return jnp.zeros((amount,), jnp.int32).at[sequence[jnp.where(places < fixed, places, shifted)]].set(jnp.asarray(sizes, jnp.int32))

    sizes = jnp.where(number % 4 == 0, named(heavy_load, number // 4), named(ordinary, number - number // 4 - 1))
    mixed = jax.random.permutation(jax.random.fold_in(own, 3), amount)
    source_of, sink = mixed[0:amount // 2 * 2:2], mixed[1:amount // 2 * 2:2]
    slack = jnp.minimum(sizes[source_of] - 1, limit - sizes[sink]) // 2
    slack = jnp.where((source_of == sequence[0]) | (sink == sequence[0]) | (sizes[sink] == 0), 0, jnp.maximum(slack, 0))
    shifted = jax.random.randint(jax.random.fold_in(own, 4), (amount // 2,), 0, 1 << 20) % (slack + 1)
    sizes = sizes.at[source_of].add(-shifted).at[sink].add(shifted)
    labels = jnp.searchsorted(jnp.cumsum(sizes), jnp.arange(rows * top), side="right").astype(jnp.int32)
    grid = labels.reshape(top, rows).T
    grid = grid[jax.random.permutation(jax.random.fold_in(own, 1), rows)]
    offset_by = jax.random.randint(jax.random.fold_in(own, 2), (rows, 1), 0, top)
    return jnp.take_along_axis(grid, (jnp.arange(top)[None, :] + offset_by) % top, axis=1)


def shares(count, total, limit, skew, full):
    weights = [(1 << 20) // math.isqrt(rank ** skew) + 1 for rank in range(1, count + 1)]
    largest = limit if full else min(limit, max(-(-total // count), total * weights[0] // sum(weights)))
    least = 1 if total - largest >= count - 1 else 0
    counts, spare = [largest] + [least] * (count - 1), total - largest - least * (count - 1)
    while spare > 0:
        candidates = [i for i in range(1, count) if counts[i] < largest] or [i for i in range(1, count) if counts[i] < limit]
        mass, budget = sum([weights[i] for i in candidates]), spare
        for i in candidates:
            extra = min(limit - counts[i], max(1, budget * weights[i] // mass), spare)
            counts[i] = counts[i] + extra
            spare = spare - extra
    return np.array(counts)


def gaussian(own_key, shape, spread, limit, cuts=(), kind=jnp.bfloat16):
    entries = spread * jax.random.normal(own_key, shape, jnp.float32)
    if cuts:
        entries = entries * steps_of(own_key, shape, cuts, -0.22, 0.18)
    return jnp.clip(entries, -limit, limit).astype(kind)


def setup_inputs(seed: int = 0) -> dict:
    seeds = jax.random.split(jax.random.key(seed), 11)
    tokens = gaussian(seeds[0], (TOKENS, D), 1.0, 6.0, ((0, 64),))
    routes_keys = jax.random.split(jax.random.fold_in(seeds[1], 1), TOKENS // TOK_DEV)
    routes_turns = jax.random.permutation(jax.random.fold_in(seeds[1], 3), TOKENS // TOK_DEV)
    routes = jax.vmap(lambda own, number: shared_out(jax.random.fold_in(seeds[1], 2), own, number, TOK_DEV, MEMS, 1, CAP, 2))(routes_keys, routes_turns).reshape((TOKENS, 1))
    w_query = gaussian(seeds[2], (D, HEADS * DK), D ** -0.5, 0.125, ((1, 2),))
    w_key = gaussian(seeds[3], (MEMS, D, HEADS * DK), D ** -0.5, 0.125, ((0, 4), (2, 2)))
    w_value = gaussian(seeds[4], (MEMS, D, HEADS * DV), D ** -0.5, 0.125, ((0, 4), (2, 2)))
    w_beta = gaussian(seeds[5], (MEMS, D, HEADS), D ** -0.5, 0.125, ((0, 4), (2, 2)))
    w_decay = gaussian(seeds[6], (MEMS, D, HEADS), D ** -0.5, 0.125, ((0, 4), (2, 2)))
    decay_rate = jnp.clip(jnp.exp(math.log(0.2) - 4.6051702 * jax.random.uniform(seeds[7], (MEMS, HEADS), jnp.float32) ** steps_of(seeds[7], (MEMS, HEADS), ((0, 4), (1, 2)), -0.2, 0.2)), 0.002, 0.2)
    norm_gain = jnp.clip(1.0 + 0.18 * jax.random.normal(seeds[8], (HEADS * DV,), jnp.float32), 0.1, 1.9)
    w_out = gaussian(seeds[9], (HEADS * DV, D), (HEADS * DV) ** -0.5, 0.1875, ((0, 2),))
    return {"tokens": tokens, "routes": routes, "w_query": w_query, "w_key": w_key, "w_value": w_value, "w_beta": w_beta, "w_decay": w_decay, "decay_rate": decay_rate, "norm_gain": norm_gain, "w_out": w_out}


def normalize_heads(vectors):
    return vectors / jnp.sqrt(lax.optimization_barrier(jnp.sum(vectors * vectors, axis=-1, keepdims=True)) + 1e-06)

def reference(tokens, routes, w_query, w_key, w_value, w_beta, w_decay, decay_rate, norm_gain, w_out):
    precise_result = lax.Precision.HIGHEST
    route = routes[:, 0].astype(jnp.int32)
    total = route.shape[0]
    bound = total // TOK_DEV * CAP
    positions = jnp.arange(total, dtype=jnp.int32)
    query = jnp.dot(tokens, w_query, preferred_element_type=jnp.float32).reshape(total, HEADS, DK)
    query = normalize_heads(query)

    def memory_pass(collected, index):
        sort_keys = jnp.where(route == index, positions, positions + total)
        order = jnp.argsort(sort_keys, stable=True)[:bound].astype(jnp.int32)
        live = (route[order] == index).astype(jnp.float32)
        rows = tokens[order].astype(jnp.float32)
        keys = jnp.dot(rows, w_key[index].astype(jnp.float32), precision=precise_result).reshape(bound, HEADS, DK)
        keys = normalize_heads(keys)
        values = jnp.dot(rows, w_value[index].astype(jnp.float32), precision=precise_result).reshape(bound, HEADS, DV)
        strength = jax.nn.sigmoid(jnp.dot(rows, w_beta[index].astype(jnp.float32), precision=precise_result)) * live[:, None]
        forget = -decay_rate[index][None, :] * jax.nn.softplus(jnp.dot(rows, w_decay[index].astype(jnp.float32), precision=precise_result)) * live[:, None]
        picked_query = query[order]

        def advance(memory_state, item):
            current_key, value_now, current_query, beta_now, decay_now = item
            fade = jnp.exp(decay_now)
            memory_readout = jnp.einsum('epw,ep->ew', memory_state, current_key, precision=precise_result)
            memory_state = fade[:, None, None] * memory_state - (beta_now * fade)[:, None, None] * current_key[:, :, None] * memory_readout[:, None, :] + beta_now[:, None, None] * current_key[:, :, None] * value_now[:, None, :]
            return (memory_state, jnp.einsum('epw,ep->ew', memory_state, current_query, precision=precise_result))
        start_state = jnp.zeros((HEADS, DK, DV), jnp.float32)
        _, outputs = lax.scan(advance, start_state, (keys, values, picked_query, strength, forget))
        collected = collected.at[order].add(outputs * live[:, None, None])
        return (collected, None)
    empty = jnp.zeros((total, HEADS, DV), jnp.float32)
    heads_out, _ = lax.scan(memory_pass, empty, jnp.arange(MEMS, dtype=jnp.int32))
    scale = 1.0 / jnp.sqrt(lax.optimization_barrier(jnp.mean(heads_out * heads_out, axis=-1, keepdims=True)) + 1e-05)
    normalized_rows = (heads_out * scale * norm_gain.reshape(HEADS, DV)[None, :, :]).astype(jnp.bfloat16)
    normalized_rows = normalized_rows.reshape(total, HEADS * DV)
    return jnp.dot(normalized_rows, w_out, preferred_element_type=jnp.float32).astype(jnp.bfloat16)
```

```python
import functools

import jax
import jax.numpy as jnp
from jax import lax
from jax.experimental import pallas as pl
from jax.experimental.pallas import tpu as pltpu
from jax.sharding import PartitionSpec as P

MESH = pl.DeviceIdType.MESH
F32 = jnp.float32
BF16 = jnp.bfloat16
CTX, MEM, HALF = 16, 4, 2
TOK = 512
D = 2048
DH = D // 2
CAP = 64
LOCAL = 4
HEADS = 4
ROWS = MEM * CAP
K = 128


def mm(a, b):
    return jnp.dot(a, b, preferred_element_type=F32)


def mm_nt(a, b):
    return lax.dot_general(a, b, (((1,), (1,)), ((), ())), preferred_element_type=F32)


def split(x):
    hi = x.astype(BF16)
    return hi, (x - hi.astype(F32)).astype(BF16)


def iota(shape, axis):
    return lax.broadcasted_iota(jnp.int32, shape, axis)


def dispatch_kernel(
    routes_ref, tok_ref, x_ref, cnt_ref, tok, outgoing, counts,
    tok_sem, own_sem, send_sem, recv_sem, csend_sem, crecv_sem, fsend_sem, frecv_sem,
):
    z = lax.axis_index("mem")
    h = lax.axis_index("half")
    load = pltpu.make_async_copy(
        tok_ref.at[:, pl.ds(pl.multiple_of(h * DH, DH), DH)], tok, tok_sem
    )
    load.start()
    barrier = pltpu.get_barrier_semaphore()
    for d in range(1, MEM):
        pl.semaphore_signal(
            barrier, inc=1, device_id={"mem": lax.rem(z + d, MEM)}, device_id_type=MESH
        )
    pl.semaphore_signal(barrier, inc=1, device_id={"half": 1 - h}, device_id_type=MESH)

    route = routes_ref[...]
    member = iota((MEM * LOCAL, TOK), 0) == route
    member_f = member.astype(F32)
    upper = (iota((TOK, TOK), 0) <= iota((TOK, TOK), 1)).astype(F32).astype(BF16)
    running = mm(member_f.astype(BF16), upper)
    place = jnp.sum(running * member_f, axis=0, keepdims=True).astype(jnp.int32) - 1
    slots = route * CAP + place
    totals = jnp.sum(member_f, axis=1, keepdims=True)
    counts[...] = jnp.zeros_like(counts)
    for to in range(MEM):
        counts[to, 0:LOCAL, :] = jnp.broadcast_to(
            totals[to * LOCAL : (to + 1) * LOCAL], (LOCAL, 128)
        )
    load.wait()
    for to in range(MEM):
        pick = (iota((ROWS, TOK), 0) + to * ROWS == slots).astype(F32).astype(BF16)
        outgoing[to] = mm(pick, tok[...]).astype(BF16).reshape(LOCAL, CAP, DH)

    pl.semaphore_wait(barrier, MEM)
    mine = pl.ds(pl.multiple_of(h * DH, DH), DH)

    def rows_of(src):
        return pl.ds(pl.multiple_of(src * CAP, CAP), CAP)

    own = pltpu.make_async_copy(outgoing.at[z], x_ref.at[:, rows_of(z), mine], own_sem.at[0])
    own.start()
    own_cnt = pltpu.make_async_copy(counts.at[z], cnt_ref.at[z], own_sem.at[1])
    own_cnt.start()
    sends = []
    for d in (2, 1, 3):
        to = lax.rem(z + d, MEM)
        cnt = pltpu.make_async_remote_copy(
            counts.at[to], cnt_ref.at[z], csend_sem.at[d], crecv_sem.at[d],
            device_id={"mem": to}, device_id_type=MESH,
        )
        cnt.start()
        copy = pltpu.make_async_remote_copy(
            outgoing.at[to], x_ref.at[:, rows_of(z), mine], send_sem.at[d], recv_sem.at[d],
            device_id={"mem": to}, device_id_type=MESH,
        )
        copy.start()
        sends += [cnt, copy]
    forward = pltpu.make_async_remote_copy(
        outgoing.at[z], x_ref.at[:, rows_of(z), mine], fsend_sem.at[0], frecv_sem.at[0],
        device_id={"half": 1 - h}, device_id_type=MESH,
    )
    forward.start()
    forwards = [forward]
    for d in (1, 3, 2):
        src = lax.rem(z + MEM - d, MEM)
        landed = x_ref.at[:, rows_of(src), mine]
        pltpu.make_async_remote_copy(
            outgoing.at[z], landed, send_sem.at[d], recv_sem.at[d],
            device_id={"mem": src}, device_id_type=MESH,
        ).wait_recv()
        forward = pltpu.make_async_remote_copy(
            landed, landed, fsend_sem.at[d], frecv_sem.at[d],
            device_id={"half": 1 - h}, device_id_type=MESH,
        )
        forward.start()
        forwards.append(forward)
        pltpu.make_async_remote_copy(
            counts.at[z], cnt_ref.at[src], csend_sem.at[d], crecv_sem.at[d],
            device_id={"mem": src}, device_id_type=MESH,
        ).wait_recv()
    for copy in sends:
        copy.wait_send()
    own.wait()
    own_cnt.wait()
    for copy in forwards:
        copy.wait()


def dispatch(routes, tokens):
    dma = pltpu.SemaphoreType.DMA
    return pl.pallas_call(
        dispatch_kernel,
        name="dispatch",
        out_shape=(
            jax.ShapeDtypeStruct((LOCAL, ROWS, D), BF16),
            jax.ShapeDtypeStruct((MEM, 8, 128), F32),
        ),
        in_specs=[pl.BlockSpec(memory_space=pltpu.VMEM), pl.BlockSpec(memory_space=pl.ANY)],
        out_specs=(pl.BlockSpec(memory_space=pl.ANY), pl.BlockSpec(memory_space=pl.ANY)),
        scratch_shapes=[
            pltpu.VMEM((TOK, DH), BF16),
            pltpu.VMEM((MEM, LOCAL, CAP, DH), BF16),
            pltpu.VMEM((MEM, 8, 128), F32),
            dma, dma((2,)), dma((MEM,)), dma((MEM,)), dma((MEM,)), dma((MEM,)),
            dma((MEM,)), dma((MEM,)),
        ],
        compiler_params=pltpu.CompilerParams(collective_id=0, has_side_effects=True),
    )(routes.reshape(1, TOK), tokens)


def local_kernel(
    rate_ref, cnt_ref, x_ref, wk_ref, wv_ref, wq_ref, wb_ref, wd_ref,
    mw_ref, base_ref, reach_ref, gates,
):
    m = pl.program_id(0)
    x = x_ref[0]
    gates[...] = jnp.zeros_like(gates)
    gates[:, 0:HEADS] = wb_ref[0]
    gates[:, HEADS : 2 * HEADS] = wd_ref[0]
    logits = mm(x, gates[...])
    keys_all = mm(x, wk_ref[0])
    values_all = mm(x, wv_ref[0])
    query_all = mm(x, wq_ref[...])

    lane = iota((1, 128), 1)
    rate = jnp.zeros((1, 128), F32)
    for h in range(HEADS):
        rate = jnp.where(lane == HEADS + h, rate_ref[m, h], rate)
    live = (
        iota((MEM, CAP, 128), 1).astype(F32) < cnt_ref[:, pl.ds(m, 1), :]
    ).astype(F32).reshape(ROWS, 128)
    strength = jax.nn.sigmoid(logits) * live
    soft = jnp.maximum(logits, 0.0) + jnp.log1p(jnp.exp(-jnp.abs(logits)))
    forget = -rate * soft * live
    row, col = iota((ROWS, ROWS), 0), iota((ROWS, ROWS), 1)
    lower = row >= col
    apart = row ^ col
    tri = lower.astype(F32).astype(BF16)
    hi, mid = split(forget)
    low = (forget - hi.astype(F32) - mid.astype(F32)).astype(BF16)
    total = mm(tri, hi) + mm(tri, mid) + mm(tri, low)
    total_t = total.T

    heads = range(HEADS)
    keys, query, values, scores, mixing, inverse, grow, target, running = (
        [None] * HEADS for _ in range(9)
    )
    for h in heads:
        at = slice(h * K, (h + 1) * K)
        k = keys_all[:, at]
        q = query_all[:, at]
        k = k * lax.rsqrt(jnp.sum(k * k, axis=1, keepdims=True) + 1e-06)
        q = q * lax.rsqrt(jnp.sum(q * q, axis=1, keepdims=True) + 1e-06)
        keys[h], query[h], values[h] = k, q, values_all[:, at]
        k_hi, k_lo = split(k)
        q_hi, q_lo = split(q)
        left = jnp.concatenate(
            [jnp.concatenate([k_hi, k_lo], axis=1), jnp.concatenate([q_hi, q_lo], axis=1)], axis=0
        )
        both = mm_nt(left, jnp.concatenate([k_hi, k_hi], axis=1)) + mm_nt(
            jnp.concatenate([k_hi, q_hi], axis=0), k_lo
        )
        g_col = total[:, HEADS + h : HEADS + h + 1]
        g_row = total_t[HEADS + h : HEADS + h + 1, :]
        fade = jnp.where(lower, jnp.exp(jnp.where(lower, g_col - g_row, 0.0)), 0.0)
        beta = strength[:, h : h + 1]
        scores[h] = both[ROWS:] * fade
        mixing[h] = jnp.where(row > col, both[:ROWS] * fade * beta, 0.0)
        grow[h] = jnp.exp(g_col)
        running[h] = g_col
        target[h] = jnp.concatenate([(beta * grow[h]) * k, beta * values[h]], axis=1)
        inverse[h] = jnp.where(row == col, 1.0, jnp.where(apart == 1, -mixing[h], 0.0))
    size = 2
    while size < ROWS:
        half_way = [None] * HEADS
        for h in heads:
            part = jnp.where((apart >= size) & (apart < 2 * size), mixing[h], 0.0).astype(BF16)
            half_way[h] = mm(part, inverse[h].astype(BF16)).astype(BF16)
        for h in heads:
            inverse[h] = inverse[h] - mm(inverse[h].astype(BF16), half_way[h])
        size *= 2
    solved = [None] * HEADS
    for h in heads:
        inv = inverse[h].astype(BF16)
        guess = mm(inv, target[h].astype(BF16))
        a_hi, a_lo = split(mixing[h])
        g_hi, g_lo = split(guess)
        rest = target[h] - guess - (mm(a_hi, g_hi) + mm(a_lo, g_hi) + mm(a_hi, g_lo))
        solved[h] = guess + mm(inv, rest.astype(BF16))
    diagonal = iota((K, K), 0) == iota((K, K), 1)
    for h in heads:
        last = running[h][ROWS - 1 : ROWS, :]
        tail = keys[h] * jnp.exp(last - running[h])
        lhs = jnp.concatenate([scores[h], tail.T], axis=0)
        l_hi, l_lo = split(lhs)
        y_hi, y_lo = split(solved[h])
        out = mm(l_hi, y_hi) + mm(l_lo, y_hi) + mm(l_hi, y_lo)
        base_ref[0, :, h * K : (h + 1) * K] = out[:ROWS, K:]
        reach = query[h] * grow[h] - out[:ROWS, :K]
        r_hi, r_lo = split(reach)
        reach_ref[0, :, 2 * h * K : (2 * h + 1) * K] = r_hi
        reach_ref[0, :, (2 * h + 1) * K : (2 * h + 2) * K] = r_lo
        step = jnp.where(diagonal, jnp.exp(last), 0.0) - out[ROWS:, :K]
        mw_ref[h, :, :K] = step.astype(BF16)
        mw_ref[h, :, K:] = out[ROWS:, K:].astype(BF16)


def local_algebra(rate, counts, x, w_key, w_value, w_query, w_beta, w_decay):
    width = HEADS * K
    per_memory = lambda *block: pl.BlockSpec((1,) + block, lambda m: (m, 0, 0))
    return pl.pallas_call(
        local_kernel,
        name="local_algebra",
        grid=(LOCAL,),
        out_shape=(
            jax.ShapeDtypeStruct((LOCAL * HEADS, K, 2 * K), BF16),
            jax.ShapeDtypeStruct((LOCAL, ROWS, width), F32),
            jax.ShapeDtypeStruct((LOCAL, ROWS, 2 * width), BF16),
        ),
        in_specs=[
            pl.BlockSpec(memory_space=pltpu.SMEM),
            pl.BlockSpec((MEM, 8, 128), lambda m: (0, 0, 0)),
            per_memory(ROWS, D),
            per_memory(D, width),
            per_memory(D, width),
            pl.BlockSpec((D, width), lambda m: (0, 0)),
            per_memory(D, HEADS),
            per_memory(D, HEADS),
        ],
        out_specs=(
            pl.BlockSpec((HEADS, K, 2 * K), lambda m: (m, 0, 0)),
            per_memory(ROWS, width),
            per_memory(ROWS, 2 * width),
        ),
        scratch_shapes=[pltpu.VMEM((D, 128), BF16)],
        compiler_params=pltpu.CompilerParams(vmem_limit_bytes=60 * 1024 * 1024),
    )(rate, counts, x, w_key, w_value, w_query, w_beta, w_decay)


def exchange_kernel(
    routes_ref, mw_ref, base_ref, reach_ref, gain_ref, w_ref, out_ref,
    maps, states, entering, reply, returned, picked, partner, w_other,
    own_sem, map_send, map_recv, state_send, state_recv, ret_send, ret_recv,
    pair_send, pair_recv,
):
    c = lax.axis_index("ctx")
    z = lax.axis_index("mem")
    h = lax.axis_index("half")
    other = {"half": 1 - h}
    barrier = pltpu.get_barrier_semaphore()
    for d in range(1, CTX):
        pl.semaphore_signal(
            barrier, inc=1, device_id={"ctx": lax.rem(c + d, CTX)}, device_id_type=MESH
        )
    for d in range(1, MEM):
        pl.semaphore_signal(
            barrier, inc=1, device_id={"mem": lax.rem(z + d, MEM)}, device_id_type=MESH
        )
    pl.semaphore_signal(barrier, inc=1, device_id=other, device_id_type=MESH)
    pl.semaphore_wait(barrier, CTX - 1 + MEM)

    def map_copy(d):
        to = lax.rem(c + d, CTX)
        return pltpu.make_async_remote_copy(
            mw_ref.at[to], maps.at[c], map_send.at[d], map_recv.at[c],
            device_id={"ctx": to}, device_id_type=MESH,
        )

    @pl.when(c < CTX - 1)
    def _():
        for d in range(1, CTX):
            map_copy(d).start()

    own_map = pltpu.make_async_copy(mw_ref.at[c], maps.at[c], own_sem.at[0])
    own_map.start()
    w_copy = pltpu.make_async_remote_copy(
        w_ref, w_other, pair_send.at[0], pair_recv.at[0], device_id=other, device_id_type=MESH
    )
    w_copy.start()
    own_map.wait()

    def state_copy(to):
        return pltpu.make_async_remote_copy(
            states.at[to], entering.at[c], state_send.at[to], state_recv.at[c],
            device_id={"ctx": to}, device_id_type=MESH,
        )

    state = None
    for j in range(CTX - 1):

        @pl.when(c != j)
        def _():
            pltpu.make_async_remote_copy(
                mw_ref.at[j], maps.at[j], map_send.at[0], map_recv.at[j],
                device_id={"ctx": j}, device_id_type=MESH,
            ).wait_recv()

        add = maps[j, :, K:].astype(F32)
        if j == 0:
            state = add
        else:
            step = maps[j, :, :K]
            s_hi, s_lo = split(state)
            state = add + mm(
                jnp.concatenate([step, step], axis=1), jnp.concatenate([s_hi, s_lo], axis=0)
            )
        states[j + 1] = state.astype(BF16)

        @pl.when(c != j + 1)
        def _():
            state_copy(j + 1).start()

    @pl.when(c == 0)
    def _():
        entering[...] = jnp.zeros_like(entering)

    @pl.when(c > 0)
    def _():
        keep = pltpu.make_async_copy(states.at[c], entering.at[c], own_sem.at[0])
        keep.start()
        keep.wait()
        for d in range(1, CTX):
            src = lax.rem(c + d, CTX)
            pltpu.make_async_remote_copy(
                states.at[1], entering.at[src], state_send.at[0], state_recv.at[src],
                device_id={"ctx": src}, device_id_type=MESH,
            ).wait_recv()

    for m in range(LOCAL):
        for n in range(HEADS):
            at = slice(n * K, (n + 1) * K)
            s = entering[m * HEADS + n]
            heads_out = base_ref[m, :, at] + mm(
                reach_ref[m, :, 2 * n * K : (2 * n + 2) * K], jnp.concatenate([s, s], axis=0)
            )
            scale = lax.rsqrt(jnp.mean(heads_out * heads_out, axis=1, keepdims=True) + 1e-05)
            normed = (heads_out * scale * gain_ref[:, at]).astype(BF16)
            for src in range(MEM):
                reply[src, m * CAP : (m + 1) * CAP, at] = normed[src * CAP : (src + 1) * CAP]
    sends = []
    for d in (2, 1, 3):
        to = lax.rem(z + d, MEM)
        copy = pltpu.make_async_remote_copy(
            reply.at[to], returned.at[z], ret_send.at[d], ret_recv.at[d],
            device_id={"mem": to}, device_id_type=MESH,
        )
        copy.start()
        sends.append(copy)

    route = routes_ref[...]
    member_f = (iota((TOK, 128), 1) == route).astype(F32)
    lower = (iota((TOK, TOK), 0) >= iota((TOK, TOK), 1)).astype(F32).astype(BF16)
    running = mm(lower, member_f.astype(BF16))
    place = jnp.sum(running * member_f, axis=1, keepdims=True).astype(jnp.int32) - 1
    slots = route * CAP + place

    def pick(src, rows):
        chosen = (iota((TOK, ROWS), 1) + src * ROWS == slots).astype(F32).astype(BF16)
        return mm(chosen, rows)

    total = pick(z, reply[z])
    for d in (1, 3, 2):
        src = lax.rem(z + MEM - d, MEM)
        pltpu.make_async_remote_copy(
            reply.at[z], returned.at[src], ret_send.at[d], ret_recv.at[d],
            device_id={"mem": src}, device_id_type=MESH,
        ).wait_recv()
        total = total + pick(src, returned[src])
    picked[...] = total.astype(BF16)
    here = pl.ds(pl.multiple_of(h * (TOK // 2), TOK // 2), TOK // 2)
    there = pl.ds(pl.multiple_of((1 - h) * (TOK // 2), TOK // 2), TOK // 2)
    swap = pltpu.make_async_remote_copy(
        picked.at[there], partner, pair_send.at[1], pair_recv.at[1],
        device_id=other, device_id_type=MESH,
    )
    swap.start()
    mixed = mm(picked[here, :], w_ref[...])
    w_copy.wait()
    swap.wait()
    out_ref[...] = (mixed + mm(partner[...], w_other[...])).astype(BF16)
    for copy in sends:
        copy.wait_send()

    @pl.when(c < CTX - 1)
    def _():
        for d in range(1, CTX):
            map_copy(d).wait_send()

    for j in range(CTX - 1):

        @pl.when(c != j + 1)
        def _():
            state_copy(j + 1).wait_send()


def exchange(routes, mw, base, reach, gain, w_out):
    dma = pltpu.SemaphoreType.DMA
    width = HEADS * K
    return pl.pallas_call(
        exchange_kernel,
        name="exchange",
        out_shape=jax.ShapeDtypeStruct((TOK // 2, D), BF16),
        in_specs=[pl.BlockSpec(memory_space=pltpu.VMEM)] * 6,
        out_specs=pl.BlockSpec(memory_space=pltpu.VMEM),
        scratch_shapes=[
            pltpu.VMEM((CTX, K, 2 * K), BF16),
            pltpu.VMEM((CTX, K, K), BF16),
            pltpu.VMEM((CTX, K, K), BF16),
            pltpu.VMEM((MEM, ROWS, width), BF16),
            pltpu.VMEM((MEM, ROWS, width), BF16),
            pltpu.VMEM((TOK, width), BF16),
            pltpu.VMEM((TOK // 2, width), BF16),
            pltpu.VMEM((width, D), BF16),
            dma((1,)), dma((CTX,)), dma((CTX,)), dma((CTX,)), dma((CTX,)),
            dma((MEM,)), dma((MEM,)), dma((2,)), dma((2,)),
        ],
        compiler_params=pltpu.CompilerParams(
            collective_id=1, has_side_effects=True, vmem_limit_bytes=60 * 1024 * 1024
        ),
    )(routes, mw, base, reach, gain.reshape(1, width), w_out)


def per_device(
    tokens, routes, w_query, w_key, w_value, w_beta, w_decay, decay_rate, norm_gain, w_out
):
    x, counts = dispatch(routes, tokens)
    mw, base, reach = local_algebra(
        decay_rate, counts, x, w_key, w_value, w_query, w_beta, w_decay
    )
    return exchange(routes, mw, base, reach, norm_gain, w_out)


def solution(mesh):
    in_specs = (
        P(("ctx", "mem"), None),
        P(("ctx", "mem"), None),
        P(None, "half"),
        P("mem", None, "half"),
        P("mem", None, "half"),
        P("mem", None, "half"),
        P("mem", None, "half"),
        P("mem", "half"),
        P("half"),
        P("half", None),
    )
    out_specs = P(("ctx", "mem", "half"), None)
    return jax.shard_map(
        per_device, mesh=mesh, in_specs=in_specs, out_specs=out_specs, check_vma=False
    )
```

```python
import jax
import jax.numpy as jnp
from jax import lax
from jax.experimental import pallas as pl
from jax.experimental.pallas import tpu as pltpu
from jax.sharding import PartitionSpec as P

MESH = pl.DeviceIdType.MESH
F32 = jnp.float32
BF16 = jnp.bfloat16
CTX, MEM = 16, 4
TOK = 512
D = 2048
DH = D // 2
CAP = 64
LOCAL = 4
HEADS = 4
ROWS = MEM * CAP
K = 128
WIDTH = HEADS * K


def mm(a, b):
    return jnp.dot(a, b, preferred_element_type=F32)


def mm_nt(a, b):
    return lax.dot_general(a, b, (((1,), (1,)), ((), ())), preferred_element_type=F32)


def split(x):
    hi = x.astype(BF16)
    return hi, (x - hi.astype(F32)).astype(BF16)


def iota(shape, axis):
    return lax.broadcasted_iota(jnp.int32, shape, axis)


def ones_where(mask):
    return mask.astype(F32).astype(BF16)


def aligned(index, size):
    return pl.ds(pl.multiple_of(index * size, size), size)


def unit(x):
    return x * lax.rsqrt(jnp.sum(x * x, axis=1, keepdims=True) + 1e-06)


def level_rows(x, size):
    return jnp.concatenate(
        [x[at + size : at + 2 * size] for at in range(0, ROWS, 2 * size)], axis=0
    )


def spread_rows(x, size):
    gap = jnp.zeros((size, x.shape[1]), x.dtype)
    parts = []
    for at in range(0, ROWS // 2, size):
        parts += [gap, x[at : at + size]]
    return jnp.concatenate(parts, axis=0)


def layer_kernel(
    rate_ref, routes_ref, tok_ref, wq_ref, wk_ref, wv_ref, wb_ref, wd_ref, gain_ref, wo_ref,
    out_ref,
    tok, outgoing, counts, cnt, xbuf, wq, wk, wv, gates, total_s, total_ts, keys_s, solved_hi,
    solved_lo, mw, maps, states, entering, base, reach, reply, returned, picked, partner, wo,
    w_other,
    load_sem, wkv_sem, own_sem, x_send, x_recv, c_send, c_recv, f_send, f_recv,
    map_send, map_recv, state_send, state_recv, ret_send, ret_recv, pair_send, pair_recv,
):
    c = lax.axis_index("ctx")
    z = lax.axis_index("mem")
    half = lax.axis_index("half")
    other = {"half": 1 - half}
    mine = aligned(half, DH)
    heads = range(HEADS)

    tok_load = pltpu.make_async_copy(tok_ref.at[:, mine], tok, load_sem.at[0])
    tok_load.start()
    barrier = pltpu.get_barrier_semaphore()
    for d in range(1, MEM):
        pl.semaphore_signal(
            barrier, inc=1, device_id={"mem": lax.rem(z + d, MEM)}, device_id_type=MESH
        )
    pl.semaphore_signal(barrier, inc=1, device_id=other, device_id_type=MESH)
    for d in range(1, CTX):
        pl.semaphore_signal(
            barrier, inc=1, device_id={"ctx": lax.rem(c + d, CTX)}, device_id_type=MESH
        )

    def weights(m):
        return (
            pltpu.make_async_copy(wk_ref.at[m], wk.at[m], wkv_sem.at[0, m]),
            pltpu.make_async_copy(wv_ref.at[m], wv.at[m], wkv_sem.at[1, m]),
        )

    route = routes_ref[...]
    member = (iota((MEM * LOCAL, TOK), 0) == route).astype(F32)
    upper_tok = ones_where(iota((TOK, TOK), 0) <= iota((TOK, TOK), 1))
    place = jnp.sum(mm(member.astype(BF16), upper_tok) * member, axis=0, keepdims=True)
    slots = route * CAP + place.astype(jnp.int32) - 1
    totals = jnp.sum(member, axis=1, keepdims=True)
    counts[...] = jnp.zeros_like(counts)
    for to in range(MEM):
        counts[to, 0:LOCAL, :] = jnp.broadcast_to(
            totals[to * LOCAL : (to + 1) * LOCAL], (LOCAL, 128)
        )
    tok_load.wait()

    def x_copy(d, m):
        to = lax.rem(z + d, MEM)
        return pltpu.make_async_remote_copy(
            outgoing.at[m, to], xbuf.at[m, aligned(z, CAP), mine], x_send.at[d, m],
            x_recv.at[d, m], device_id={"mem": to}, device_id_type=MESH,
        )

    def x_arrival(d, m):
        src = lax.rem(z + MEM - d, MEM)
        return pltpu.make_async_remote_copy(
            outgoing.at[m, z], xbuf.at[m, aligned(src, CAP), mine], x_send.at[d, m],
            x_recv.at[d, m], device_id={"mem": src}, device_id_type=MESH,
        )

    def own_copy(m):
        return pltpu.make_async_copy(
            outgoing.at[m, z], xbuf.at[m, aligned(z, CAP), mine], own_sem.at[m]
        )

    def forward(d, m):
        src = lax.rem(z + MEM - d, MEM)
        landed = xbuf.at[m, aligned(src, CAP), mine]
        return pltpu.make_async_remote_copy(
            landed if d else outgoing.at[m, z], landed, f_send.at[d, m], f_recv.at[d, m],
            device_id=other, device_id_type=MESH,
        )

    def forward_arrival(d, m):
        src = lax.rem(z + MEM - d, MEM)
        landed = xbuf.at[m, aligned(src, CAP), aligned(1 - half, DH)]
        return pltpu.make_async_remote_copy(
            landed, landed, f_send.at[d, m], f_recv.at[d, m],
            device_id=other, device_id_type=MESH,
        )

    def count_copy(d):
        to = lax.rem(z + d, MEM)
        return pltpu.make_async_remote_copy(
            counts.at[to], cnt.at[z], c_send.at[d], c_recv.at[d],
            device_id={"mem": to}, device_id_type=MESH,
        )

    def gather(m):
        at = iota((ROWS, TOK), 0)
        slot = (at // CAP * LOCAL + m) * CAP + at % CAP
        rows = mm(ones_where(slot == slots), tok[...]).astype(BF16)
        outgoing[m] = rows.reshape(MEM, CAP, DH)

    def launch(m):
        for d in (2, 1, 3):
            x_copy(d, m).start()
        forward(0, m).start()
        own_copy(m).start()

    gather(0)
    pl.semaphore_wait(barrier, CTX - 1 + MEM)
    for d in range(1, MEM):
        count_copy(d).start()
    launch(0)
    for copy in weights(0):
        copy.start()
    cnt[z] = counts[z]

    @pl.loop(1, LOCAL)
    def _(m):
        gather(m)
        launch(m)
        for copy in weights(m):
            copy.start()

    wq_load = pltpu.make_async_copy(wq_ref, wq, load_sem.at[1])
    wq_load.start()
    wo_load = pltpu.make_async_copy(wo_ref, wo, load_sem.at[2])
    wo_load.start()

    def pass_on(m):
        for d in (1, 3, 2):
            x_arrival(d, m).wait_recv()
            forward(d, m).start()

    pass_on(0)
    for d in range(1, MEM):
        src = lax.rem(z + MEM - d, MEM)
        pltpu.make_async_remote_copy(
            counts.at[z], cnt.at[src], c_send.at[d], c_recv.at[d],
            device_id={"mem": src}, device_id_type=MESH,
        ).wait_recv()

    def map_copy(p):
        return pltpu.make_async_remote_copy(
            mw.at[p], maps.at[c], map_send.at[p], map_recv.at[c],
            device_id={"ctx": p}, device_id_type=MESH,
        )

    def keep_map(p):
        return pltpu.make_async_copy(mw.at[p], maps.at[c], own_sem.at[LOCAL])

    def fade_of(g_col, g_row):
        lower = iota((ROWS, ROWS), 0) >= iota((ROWS, ROWS), 1)
        return jnp.where(lower, jnp.exp(jnp.where(lower, g_col - g_row, 0.0)), 0.0)

    gates[...] = jnp.zeros_like(gates)

    @pl.loop(0, LOCAL)
    def _(m):
        for copy in weights(m):
            copy.wait()
        own_copy(m).wait()
        for d in range(MEM):
            forward_arrival(d, m).wait_recv()
        x = xbuf[m]
        gates[0:HEADS, :] = wb_ref[m]
        gates[HEADS : 2 * HEADS, :] = wd_ref[m]
        logits = mm_nt(gates[...], x)
        keys_all = mm(x, wk[m])
        values_all = mm(x, wv[m])

        lane = iota((1, 128), 1)
        cnt_of = [cnt[src, pl.ds(m, 1), :] for src in range(MEM)]
        cnt_row = jnp.concatenate(
            [
                jnp.where(lane < CAP, cnt_of[0], cnt_of[1]),
                jnp.where(lane < CAP, cnt_of[2], cnt_of[3]),
            ],
            axis=1,
        )
        live = ((iota((1, ROWS), 1) & (CAP - 1)).astype(F32) < cnt_row).astype(F32)
        gate = iota((16, 1), 0)
        rate = jnp.zeros((16, 1), F32)
        for h in heads:
            rate = jnp.where(gate == HEADS + h, rate_ref[m, h], rate)
        strength = jax.nn.sigmoid(logits) * live
        soft = jnp.maximum(logits, 0.0) + jnp.log1p(jnp.exp(-jnp.abs(logits)))
        forget = -rate * soft * live
        row, col = iota((ROWS, ROWS), 0), iota((ROWS, ROWS), 1)
        apart = row ^ col
        upper = ones_where(row <= col)
        hi, mid = split(forget)
        low = (forget - hi.astype(F32) - mid.astype(F32)).astype(BF16)
        total_t = mm(hi, upper) + mm(mid, upper) + mm(low, upper)
        both_t = jnp.where(gate < HEADS, strength, total_t)
        both = jnp.concatenate([both_t, jnp.zeros((112, ROWS), F32)], axis=0).T
        total_ts[m] = both_t
        total_s[m] = both

        mixing = [None] * HEADS
        inverse = [None] * HEADS
        target = [None] * HEADS
        tails = [None] * HEADS
        for h in heads:
            at = slice(h * K, (h + 1) * K)
            k = unit(keys_all[:, at])
            k_hi, k_lo = split(k)
            keys_s[m, h, :, :K] = k_hi
            keys_s[m, h, :, K:] = k_lo
            gram = mm_nt(
                jnp.concatenate([k_hi, k_lo], axis=1), jnp.concatenate([k_hi, k_hi], axis=1)
            ) + mm_nt(k_hi, k_lo)
            g_col = both[:, HEADS + h : HEADS + h + 1]
            beta = both[:, h : h + 1]
            mix = gram * fade_of(g_col, both_t[HEADS + h : HEADS + h + 1, :]) * beta
            mixing[h] = jnp.where(row > col, mix, 0.0)
            target[h] = jnp.concatenate(
                [(beta * jnp.exp(g_col)) * k, beta * values_all[:, at]], axis=1
            )
            tails[h] = k * jnp.exp(g_col[ROWS - 1 : ROWS, :] - g_col)
            inverse[h] = jnp.where(apart == 1, -mixing[h], 0.0).astype(BF16)
        eye = ones_where(row == col)
        mix_hi = [mixing[h].astype(BF16) for h in heads]
        inverse = [inverse[h] + eye for h in heads]
        size = 2
        while size < ROWS // 2:
            if size < 16:
                here = (apart >= size) & (apart < 2 * size)
                mid_way = [
                    jnp.where(here, mm(mix_hi[h], inverse[h]), 0.0).astype(BF16) for h in heads
                ]
                update = [mm(inverse[h], mid_way[h]).astype(BF16) for h in heads]
            else:
                near = level_rows(apart, size)
                here = (near >= size) & (near < 2 * size)
                mid_way = [
                    jnp.where(here, mm(level_rows(mix_hi[h], size), inverse[h]), 0.0).astype(BF16)
                    for h in heads
                ]
                update = [
                    spread_rows(
                        mm(level_rows(inverse[h], size), spread_rows(mid_way[h], size)).astype(
                            BF16
                        ),
                        size,
                    )
                    for h in heads
                ]
            inverse = [inverse[h] - update[h] for h in heads]
            size *= 2
        mid_way = [mm(mix_hi[h][K:, :K], inverse[h][:K, :K]).astype(BF16) for h in heads]
        corner = [mm(inverse[h][K:, K:], mid_way[h]).astype(BF16) for h in heads]
        inverse = [
            jnp.concatenate(
                [
                    inverse[h][:K],
                    jnp.concatenate([-corner[h], inverse[h][K:, K:]], axis=1),
                ],
                axis=0,
            )
            - eye
            for h in heads
        ]
        guess = [target[h] + mm(inverse[h], target[h].astype(BF16)) for h in heads]
        rest = [None] * HEADS
        for h in heads:
            g_hi, g_lo = split(guess[h])
            m_lo = (mixing[h] - mix_hi[h].astype(F32)).astype(BF16)
            applied = mm(mix_hi[h], g_hi) + mm(m_lo, g_hi) + mm(mix_hi[h], g_lo)
            rest[h] = target[h] - guess[h] - applied
        diagonal = iota((K, K), 0) == iota((K, K), 1)
        for h in heads:
            y = guess[h] + rest[h] + mm(inverse[h], rest[h].astype(BF16))
            y_hi, y_lo = split(y)
            solved_hi[m, h] = y_hi
            solved_lo[m, h] = y_lo
            t_hi, t_lo = split(tails[h].T)
            out = mm(t_hi, y_hi) + mm(t_lo, y_hi) + mm(t_hi, y_lo)
            last = jnp.exp(both[ROWS - 1 : ROWS, HEADS + h : HEADS + h + 1])
            p = m * HEADS + h
            mw[p, :, :K] = (jnp.where(diagonal, last, 0.0) - out[:, :K]).astype(BF16)
            mw[p, :, K:] = out[:, K:].astype(BF16)
        for h in heads:
            p = m * HEADS + h

            @pl.when((p != c) & (c < CTX - 1))
            def _():
                map_copy(p).start()

            @pl.when(p == c)
            def _():
                keep_map(p).start()

        @pl.when(m + 1 < LOCAL)
        def _():
            pass_on(m + 1)

    w_copy = pltpu.make_async_remote_copy(
        wo_ref, w_other, pair_send.at[0], pair_recv.at[0], device_id=other, device_id_type=MESH
    )
    w_copy.start()
    wq_load.wait()

    def local_output(m):
        query_all = mm(xbuf[m], wq[...])
        both = total_s[m]
        for h in heads:
            q = unit(query_all[:, h * K : (h + 1) * K])
            q_hi, q_lo = split(q)
            k_hi, k_lo = keys_s[m, h, :, :K], keys_s[m, h, :, K:]
            gram = mm_nt(
                jnp.concatenate([q_hi, q_lo], axis=1), jnp.concatenate([k_hi, k_hi], axis=1)
            ) + mm_nt(q_hi, k_lo)
            g_col = both[:, HEADS + h : HEADS + h + 1]
            g_row = total_ts[m, HEADS + h : HEADS + h + 1, :]
            s_hi, s_lo = split(gram * fade_of(g_col, g_row))
            y_hi, y_lo = solved_hi[m, h], solved_lo[m, h]
            out = mm(s_hi, y_hi) + mm(s_lo, y_hi) + mm(s_hi, y_lo)
            base[m, :, h * K : (h + 1) * K] = out[:, K:]
            r_hi, r_lo = split(q * jnp.exp(g_col) - out[:, :K])
            reach[m, :, 2 * h * K : (2 * h + 1) * K] = r_hi
            reach[m, :, (2 * h + 1) * K : (2 * h + 2) * K] = r_lo

    @pl.loop(0, LOCAL // 2)
    def _(m):
        local_output(m)

    def state_copy(to):
        return pltpu.make_async_remote_copy(
            states.at[to], entering.at[c], state_send.at[to], state_recv.at[c],
            device_id={"ctx": to}, device_id_type=MESH,
        )

    keep_map(c).wait()
    state = None
    for j in range(CTX - 1):

        @pl.when(c != j)
        def _():
            pltpu.make_async_remote_copy(
                mw.at[j], maps.at[j], map_send.at[j], map_recv.at[j],
                device_id={"ctx": j}, device_id_type=MESH,
            ).wait_recv()

        add = maps[j, :, K:].astype(F32)
        if j == 0:
            state = add
        else:
            step = maps[j, :, :K]
            s_hi, s_lo = split(state)
            state = add + mm(
                jnp.concatenate([step, step], axis=1), jnp.concatenate([s_hi, s_lo], axis=0)
            )
        states[j + 1] = state.astype(BF16)

        @pl.when(c != j + 1)
        def _():
            state_copy(j + 1).start()

    @pl.loop(LOCAL // 2, LOCAL)
    def _(m):
        local_output(m)

    def ret_copy(d, m):
        to = lax.rem(z + d, MEM)
        return pltpu.make_async_remote_copy(
            reply.at[m, to], returned.at[z, m], ret_send.at[d, m], ret_recv.at[d, m],
            device_id={"mem": to}, device_id_type=MESH,
        )

    keep_state = pltpu.make_async_copy(states.at[c], entering.at[c], own_sem.at[LOCAL])

    @pl.when(c == 0)
    def _():
        entering[...] = jnp.zeros_like(entering)

    @pl.when(c > 0)
    def _():
        keep_state.start()
        keep_state.wait()

    @pl.loop(0, LOCAL)
    def _(m):
        for h in heads:
            p = m * HEADS + h

            @pl.when((c > 0) & (p != c))
            def _():
                pltpu.make_async_remote_copy(
                    states.at[1], entering.at[p], state_send.at[1], state_recv.at[p],
                    device_id={"ctx": p}, device_id_type=MESH,
                ).wait_recv()

        for h in heads:
            at = slice(h * K, (h + 1) * K)
            s = entering[m * HEADS + h]
            heads_out = base[m, :, at] + mm(
                reach[m, :, 2 * h * K : (2 * h + 2) * K], jnp.concatenate([s, s], axis=0)
            )
            scale = lax.rsqrt(jnp.mean(heads_out * heads_out, axis=1, keepdims=True) + 1e-05)
            normed = (heads_out * scale * gain_ref[:, at]).astype(BF16)
            reply[m, :, :, at] = normed.reshape(MEM, CAP, K)
        for d in (2, 1, 3):
            ret_copy(d, m).start()

    column = jnp.broadcast_to(slots.astype(F32), (128, TOK)).T[:, 0:1].astype(jnp.int32)

    def pick(src, rows):
        chosen = ones_where(iota((TOK, ROWS), 1) + src * ROWS == column)
        return mm(chosen, rows)

    own_rows = jnp.concatenate([reply[m, z] for m in range(LOCAL)], axis=0)
    total = pick(z, own_rows)
    for d in (1, 3, 2):
        src = lax.rem(z + MEM - d, MEM)
        for m in range(LOCAL):
            pltpu.make_async_remote_copy(
                reply.at[m, z], returned.at[src, m], ret_send.at[d, m], ret_recv.at[d, m],
                device_id={"mem": src}, device_id_type=MESH,
            ).wait_recv()
        total = total + pick(src, returned[src].reshape(ROWS, WIDTH))
    picked[...] = total.astype(BF16)
    swap = pltpu.make_async_remote_copy(
        picked.at[aligned(1 - half, TOK // 2)], partner, pair_send.at[1], pair_recv.at[1],
        device_id=other, device_id_type=MESH,
    )
    swap.start()
    wo_load.wait()
    mixed = mm(picked[aligned(half, TOK // 2), :], wo[...])
    w_copy.wait()
    swap.wait()
    out_ref[...] = (mixed + mm(partner[...], w_other[...])).astype(BF16)

    for d in range(1, MEM):
        count_copy(d).wait_send()

    @pl.loop(0, LOCAL)
    def _(m):
        for d in range(1, MEM):
            x_copy(d, m).wait_send()
            ret_copy(d, m).wait_send()
        for d in range(MEM):
            forward(d, m).wait_send()
        for h in heads:
            p = m * HEADS + h

            @pl.when((p != c) & (c < CTX - 1))
            def _():
                map_copy(p).wait_send()

    @pl.loop(1, CTX)
    def _(j):
        @pl.when(c != j)
        def _():
            state_copy(j).wait_send()


def per_device(
    tokens, routes, w_query, w_key, w_value, w_beta, w_decay, decay_rate, norm_gain, w_out
):
    dma = pltpu.SemaphoreType.DMA
    vmem = pltpu.VMEM
    in_vmem = pl.BlockSpec(memory_space=pltpu.VMEM)
    in_place = pl.BlockSpec(memory_space=pl.ANY)
    return pl.pallas_call(
        layer_kernel,
        name="layer",
        out_shape=jax.ShapeDtypeStruct((TOK // 2, D), BF16),
        in_specs=[
            pl.BlockSpec(memory_space=pltpu.SMEM), in_vmem, in_place, in_place, in_place,
            in_place, in_vmem, in_vmem, in_vmem, in_place,
        ],
        out_specs=in_vmem,
        scratch_shapes=[
            vmem((TOK, DH), BF16),
            vmem((LOCAL, MEM, CAP, DH), BF16),
            vmem((MEM, 8, 128), F32),
            vmem((MEM, 8, 128), F32),
            vmem((LOCAL, ROWS, D), BF16),
            vmem((D, WIDTH), BF16),
            vmem((LOCAL, D, WIDTH), BF16),
            vmem((LOCAL, D, WIDTH), BF16),
            vmem((16, D), BF16),
            vmem((LOCAL, ROWS, 128), F32),
            vmem((LOCAL, 16, ROWS), F32),
            vmem((LOCAL, HEADS, ROWS, 2 * K), BF16),
            vmem((LOCAL, HEADS, ROWS, 2 * K), BF16),
            vmem((LOCAL, HEADS, ROWS, 2 * K), BF16),
            vmem((CTX, K, 2 * K), BF16),
            vmem((CTX, K, 2 * K), BF16),
            vmem((CTX, K, K), BF16),
            vmem((CTX, K, K), BF16),
            vmem((LOCAL, ROWS, WIDTH), F32),
            vmem((LOCAL, ROWS, 2 * WIDTH), BF16),
            vmem((LOCAL, MEM, CAP, WIDTH), BF16),
            vmem((MEM, LOCAL, CAP, WIDTH), BF16),
            vmem((TOK, WIDTH), BF16),
            vmem((TOK // 2, WIDTH), BF16),
            vmem((WIDTH, D), BF16),
            vmem((WIDTH, D), BF16),
            dma((3,)), dma((2, LOCAL)), dma((LOCAL + 1,)),
            dma((MEM, LOCAL)), dma((MEM, LOCAL)), dma((MEM,)), dma((MEM,)),
            dma((MEM, LOCAL)), dma((MEM, LOCAL)),
            dma((CTX,)), dma((CTX,)), dma((CTX,)), dma((CTX,)),
            dma((MEM, LOCAL)), dma((MEM, LOCAL)), dma((2,)), dma((2,)),
        ],
        compiler_params=pltpu.CompilerParams(
            collective_id=0, has_side_effects=True, vmem_limit_bytes=67_043_328
        ),
    )(
        decay_rate,
        routes.reshape(1, TOK),
        tokens,
        w_query,
        w_key,
        w_value,
        jnp.swapaxes(w_beta, 1, 2),
        jnp.swapaxes(w_decay, 1, 2),
        norm_gain.reshape(1, WIDTH),
        w_out,
    )


def solution(mesh):
    in_specs = (
        P(("ctx", "mem"), None),
        P(("ctx", "mem"), None),
        P(None, "half"),
        P("mem", None, "half"),
        P("mem", None, "half"),
        P("mem", None, "half"),
        P("mem", None, "half"),
        P("mem", "half"),
        P("half"),
        P("half", None),
    )
    out_specs = P(("ctx", "mem", "half"), None)
    return jax.shard_map(
        per_device, mesh=mesh, in_specs=in_specs, out_specs=out_specs, check_vma=False
    )
```

```python
import jax
import jax.numpy as jnp
from jax import lax
from jax.experimental import pallas as pl
from jax.experimental.pallas import tpu as pltpu
from jax.sharding import PartitionSpec as P

MESH = pl.DeviceIdType.MESH
F32 = jnp.float32
BF16 = jnp.bfloat16
CTX, MEM = 16, 4
TOK = 512
D = 2048
DH = D // 2
CAP = 64
LOCAL = 4
HEADS = 4
ROWS = MEM * CAP
K = 128
WIDTH = HEADS * K


def mm(a, b):
    return jnp.dot(a, b, preferred_element_type=F32)


def mm_nt(a, b):
    return lax.dot_general(a, b, (((1,), (1,)), ((), ())), preferred_element_type=F32)


def split(x):
    hi = x.astype(BF16)
    return hi, (x - hi.astype(F32)).astype(BF16)


def iota(shape, axis):
    return lax.broadcasted_iota(jnp.int32, shape, axis)


def ones_where(mask):
    return mask.astype(F32).astype(BF16)


def aligned(index, size):
    return pl.ds(pl.multiple_of(index * size, size), size)


def unit(x):
    return x * lax.rsqrt(jnp.sum(x * x, axis=1, keepdims=True) + 1e-06)


def level_rows(x, size):
    return jnp.concatenate(
        [x[at + size : at + 2 * size] for at in range(0, x.shape[0], 2 * size)], axis=0
    )


def spread_rows(x, size):
    gap = jnp.zeros((size, x.shape[1]), x.dtype)
    parts = []
    for at in range(0, x.shape[0], size):
        parts += [gap, x[at : at + size]]
    return jnp.concatenate(parts, axis=0)


def unit_lower_inverses(blocks):
    side = blocks[0].shape[0]
    row, col = iota((side, side), 0), iota((side, side), 1)
    apart = row ^ col
    eye = ones_where(row == col)
    low = [b.astype(BF16) for b in blocks]
    inverse = [jnp.where(apart == 1, -b, 0.0).astype(BF16) + eye for b in blocks]
    size = 2
    while size < side:
        whole = size < 16
        pick = (lambda x: x) if whole else (lambda x: level_rows(x, size))
        put = (lambda x: x) if whole else (lambda x: spread_rows(x, size))
        near = pick(apart)
        here = (near >= size) & (near < 2 * size)
        mid_way = [
            jnp.where(here, mm(pick(a), x), 0.0).astype(BF16) for a, x in zip(low, inverse)
        ]
        update = [
            put(mm(pick(x), put(y)).astype(BF16)) for x, y in zip(inverse, mid_way)
        ]
        inverse = [x - u for x, u in zip(inverse, update)]
        size *= 2
    return inverse, eye


def three_pass(a, b):
    a_hi, a_lo = a
    b_hi, b_lo = b
    return mm(
        jnp.concatenate([a_hi, a_lo, a_hi], axis=1), jnp.concatenate([b_hi, b_hi, b_lo], axis=0)
    )


def layer_kernel(
    rate_ref, routes_ref, tok_ref, wq_ref, wk_ref, wv_ref, wb_ref, wd_ref, gain_ref, wo_ref,
    out_ref,
    tok, outgoing, counts, cnt, xbuf, wq, wk, wv, gates, total_s, total_ts, keys_s, solved_hi,
    solved_lo, mw, maps, states, entering, base, reach, reply, returned, picked, partner, wo,
    w_other,
    load_sem, wkv_sem, own_sem, x_send, x_recv, c_send, c_recv, f_send, f_recv,
    map_send, map_recv, state_send, state_recv, ret_send, ret_recv, pair_send, pair_recv,
):
    c = lax.axis_index("ctx")
    z = lax.axis_index("mem")
    half = lax.axis_index("half")
    other = {"half": 1 - half}
    mine = aligned(half, DH)
    heads = range(HEADS)
    own_stage = lax.rem(c // 4 + 2 * half, LOCAL)
    own_pair = own_stage * HEADS + lax.rem(c, 4)

    def owner(m, h):
        return lax.rem(m + 2 * half, LOCAL) * 4 + h

    tok_load = pltpu.make_async_copy(tok_ref.at[:, mine], tok, load_sem.at[0])
    tok_load.start()
    barrier = pltpu.get_barrier_semaphore()
    for d in range(1, MEM):
        pl.semaphore_signal(
            barrier, inc=1, device_id={"mem": lax.rem(z + d, MEM)}, device_id_type=MESH
        )
    pl.semaphore_signal(barrier, inc=1, device_id=other, device_id_type=MESH)
    for d in range(1, CTX):
        pl.semaphore_signal(
            barrier, inc=1, device_id={"ctx": lax.rem(c + d, CTX)}, device_id_type=MESH
        )

    def weights(m):
        return (
            pltpu.make_async_copy(wk_ref.at[m], wk.at[m], wkv_sem.at[0, m]),
            pltpu.make_async_copy(wv_ref.at[m], wv.at[m], wkv_sem.at[1, m]),
        )

    route = routes_ref[...]
    member = (iota((MEM * LOCAL, TOK), 0) == route).astype(F32)
    upper_tok = ones_where(iota((TOK, TOK), 0) <= iota((TOK, TOK), 1))
    place = jnp.sum(mm(member.astype(BF16), upper_tok) * member, axis=0, keepdims=True)
    slots = route * CAP + place.astype(jnp.int32) - 1
    totals = jnp.sum(member, axis=1, keepdims=True)
    counts[...] = jnp.zeros_like(counts)
    for to in range(MEM):
        counts[to, 0:LOCAL, :] = jnp.broadcast_to(
            totals[to * LOCAL : (to + 1) * LOCAL], (LOCAL, 128)
        )
    tok_load.wait()

    def x_copy(d, m):
        to = lax.rem(z + d, MEM)
        return pltpu.make_async_remote_copy(
            outgoing.at[m, to], xbuf.at[m, aligned(z, CAP), mine], x_send.at[d, m],
            x_recv.at[d, m], device_id={"mem": to}, device_id_type=MESH,
        )

    def x_arrival(d, m):
        src = lax.rem(z + MEM - d, MEM)
        return pltpu.make_async_remote_copy(
            outgoing.at[m, z], xbuf.at[m, aligned(src, CAP), mine], x_send.at[d, m],
            x_recv.at[d, m], device_id={"mem": src}, device_id_type=MESH,
        )

    def own_copy(m):
        return pltpu.make_async_copy(
            outgoing.at[m, z], xbuf.at[m, aligned(z, CAP), mine], own_sem.at[m]
        )

    def forward(d, m):
        src = lax.rem(z + MEM - d, MEM)
        landed = xbuf.at[m, aligned(src, CAP), mine]
        return pltpu.make_async_remote_copy(
            landed if d else outgoing.at[m, z], landed, f_send.at[d, m], f_recv.at[d, m],
            device_id=other, device_id_type=MESH,
        )

    def forward_arrival(d, m):
        src = lax.rem(z + MEM - d, MEM)
        landed = xbuf.at[m, aligned(src, CAP), aligned(1 - half, DH)]
        return pltpu.make_async_remote_copy(
            landed, landed, f_send.at[d, m], f_recv.at[d, m],
            device_id=other, device_id_type=MESH,
        )

    def count_copy(d):
        to = lax.rem(z + d, MEM)
        return pltpu.make_async_remote_copy(
            counts.at[to], cnt.at[z], c_send.at[d], c_recv.at[d],
            device_id={"mem": to}, device_id_type=MESH,
        )

    def gather(m):
        at = iota((ROWS, TOK), 0)
        slot = (at // CAP * LOCAL + m) * CAP + at % CAP
        rows = mm(ones_where(slot == slots), tok[...]).astype(BF16)
        outgoing[m] = rows.reshape(MEM, CAP, DH)

    def launch(m):
        for d in (2, 1, 3):
            x_copy(d, m).start()
        forward(0, m).start()
        own_copy(m).start()

    gather(0)
    pl.semaphore_wait(barrier, CTX - 1 + MEM)
    for d in range(1, MEM):
        count_copy(d).start()
    launch(0)
    for copy in weights(0):
        copy.start()
    cnt[z] = counts[z]

    @pl.loop(1, LOCAL)
    def _(m):
        gather(m)
        launch(m)
        for copy in weights(m):
            copy.start()

    wq_load = pltpu.make_async_copy(wq_ref, wq, load_sem.at[1])
    wq_load.start()
    wo_load = pltpu.make_async_copy(wo_ref, wo, load_sem.at[2])
    wo_load.start()

    def pass_on(m):
        for d in (1, 3, 2):
            x_arrival(d, m).wait_recv()
            forward(d, m).start()

    pass_on(0)
    for d in range(1, MEM):
        src = lax.rem(z + MEM - d, MEM)
        pltpu.make_async_remote_copy(
            counts.at[z], cnt.at[src], c_send.at[d], c_recv.at[d],
            device_id={"mem": src}, device_id_type=MESH,
        ).wait_recv()

    def map_copy(m, h):
        p = m * HEADS + h
        return pltpu.make_async_remote_copy(
            mw.at[p], maps.at[c], map_send.at[p], map_recv.at[c],
            device_id={"ctx": owner(m, h)}, device_id_type=MESH,
        )

    def fade_of(g_col, g_row):
        lower = iota((ROWS, ROWS), 0) >= iota((ROWS, ROWS), 1)
        return jnp.where(lower, jnp.exp(jnp.where(lower, g_col - g_row, 0.0)), 0.0)

    gates[...] = jnp.zeros_like(gates)

    @pl.loop(0, LOCAL)
    def _(m):
        for copy in weights(m):
            copy.wait()
        own_copy(m).wait()
        for d in range(MEM):
            forward_arrival(d, m).wait_recv()
        x = xbuf[m]
        gates[0:HEADS, :] = wb_ref[m]
        gates[HEADS : 2 * HEADS, :] = wd_ref[m]
        logits = mm_nt(gates[...], x)
        keys_all = mm(x, wk[m])
        values_all = mm(x, wv[m])

        lane = iota((1, 128), 1)
        cnt_of = [cnt[src, pl.ds(m, 1), :] for src in range(MEM)]
        cnt_row = jnp.concatenate(
            [
                jnp.where(lane < CAP, cnt_of[0], cnt_of[1]),
                jnp.where(lane < CAP, cnt_of[2], cnt_of[3]),
            ],
            axis=1,
        )
        live = ((iota((1, ROWS), 1) & (CAP - 1)).astype(F32) < cnt_row).astype(F32)
        gate = iota((16, 1), 0)
        rate = jnp.zeros((16, 1), F32)
        for h in heads:
            rate = jnp.where(gate == HEADS + h, rate_ref[m, h], rate)
        strength = jax.nn.sigmoid(logits) * live
        soft = jnp.maximum(logits, 0.0) + jnp.log1p(jnp.exp(-jnp.abs(logits)))
        forget = -rate * soft * live
        upper = ones_where(iota((ROWS, ROWS), 0) <= iota((ROWS, ROWS), 1))
        hi, mid = split(forget)
        low = (forget - hi.astype(F32) - mid.astype(F32)).astype(BF16)
        total_t = mm(hi, upper) + mm(mid, upper) + mm(low, upper)
        both_t = jnp.where(gate < HEADS, strength, total_t)
        both = jnp.concatenate([both_t, jnp.zeros((112, ROWS), F32)], axis=0).T
        total_ts[m] = both_t
        total_s[m] = both

        keys, corner, target = [None] * HEADS, [None] * HEADS, [None] * HEADS
        blocks = [None] * (2 * HEADS)
        last = both[ROWS - 1 : ROWS, :]
        square = iota((K, K), 0), iota((K, K), 1)
        strict = square[0] > square[1]
        for h in heads:
            at = slice(h * K, (h + 1) * K)
            k = unit(keys_all[:, at])
            keys[h] = k
            k_hi, k_lo = split(k)
            keys_s[m, h, :, :K] = k_hi
            keys_s[m, h, :, K:] = k_lo
            gram = mm_nt(
                jnp.concatenate([k_hi, k_lo], axis=1), jnp.concatenate([k_hi, k_hi], axis=1)
            ) + mm_nt(k_hi, k_lo)
            g_col = both[:, HEADS + h : HEADS + h + 1]
            g_row = both_t[HEADS + h : HEADS + h + 1, :]
            beta = both[:, h : h + 1]
            for b in range(2):
                part = slice(b * K, (b + 1) * K)
                gap = jnp.minimum(g_col[part] - g_row[:, part], 0.0)
                mix = gram[part, part] * jnp.exp(gap) * beta[part]
                blocks[2 * h + b] = jnp.where(strict, mix, 0.0)
            corner[h] = gram[K:, :K] * jnp.exp(g_col[K:] - g_row[:, :K]) * beta[K:]
            target[h] = jnp.concatenate(
                [(beta * jnp.exp(g_col)) * k, beta * values_all[:, at]], axis=1
            )
        inverse, eye = unit_lower_inverses(blocks)
        none = jnp.zeros((K, K), BF16)
        cross = [
            mm(corner[h].astype(BF16), inverse[2 * h]).astype(BF16) for h in heads
        ]
        cross = [mm(inverse[2 * h + 1], cross[h]).astype(BF16) for h in heads]
        inverse = [
            jnp.concatenate(
                [
                    jnp.concatenate([inverse[2 * h] - eye, none], axis=1),
                    jnp.concatenate([-cross[h], inverse[2 * h + 1] - eye], axis=1),
                ],
                axis=0,
            )
            for h in heads
        ]
        guess = [target[h] + mm(inverse[h], target[h].astype(BF16)) for h in heads]
        rest = [None] * HEADS
        for h in heads:
            a_hi, a_lo = split(blocks[2 * h])
            b_hi, b_lo = split(blocks[2 * h + 1])
            c_hi, c_lo = split(corner[h])
            mix_hi = jnp.concatenate(
                [jnp.concatenate([a_hi, none], axis=1), jnp.concatenate([c_hi, b_hi], axis=1)],
                axis=0,
            )
            mix_lo = jnp.concatenate(
                [jnp.concatenate([a_lo, none], axis=1), jnp.concatenate([c_lo, b_lo], axis=1)],
                axis=0,
            )
            rest[h] = target[h] - guess[h] - three_pass((mix_hi, mix_lo), split(guess[h]))
        solved = [
            guess[h] + rest[h] + mm(inverse[h], rest[h].astype(BF16)) for h in heads
        ]
        diagonal = square[0] == square[1]
        for h in heads:
            y = split(solved[h])
            solved_hi[m, h], solved_lo[m, h] = y
            g_last = last[:, HEADS + h : HEADS + h + 1]
            tail = keys[h] * jnp.exp(g_last - both[:, HEADS + h : HEADS + h + 1])
            out = three_pass(split(tail.T), y)
            p = m * HEADS + h
            mw[p, :, :K] = (jnp.where(diagonal, jnp.exp(g_last), 0.0) - out[:, :K]).astype(BF16)
            mw[p, :, K:] = out[:, K:].astype(BF16)
        for h in heads:

            @pl.when((m * HEADS + h != own_pair) & (c < CTX - 1))
            def _():
                map_copy(m, h).start()

        @pl.when(m + 1 < LOCAL)
        def _():
            pass_on(m + 1)

    w_copy = pltpu.make_async_remote_copy(
        wo_ref, w_other, pair_send.at[0], pair_recv.at[0], device_id=other, device_id_type=MESH
    )
    w_copy.start()
    wq_load.wait()

    def local_output(m):
        query_all = mm(xbuf[m], wq[...])
        both = total_s[m]
        for h in heads:
            q = unit(query_all[:, h * K : (h + 1) * K])
            q_hi, q_lo = split(q)
            k_hi, k_lo = keys_s[m, h, :, :K], keys_s[m, h, :, K:]
            gram = mm_nt(
                jnp.concatenate([q_hi, q_lo], axis=1), jnp.concatenate([k_hi, k_hi], axis=1)
            ) + mm_nt(q_hi, k_lo)
            g_col = both[:, HEADS + h : HEADS + h + 1]
            g_row = total_ts[m, HEADS + h : HEADS + h + 1, :]
            scores = split(gram * fade_of(g_col, g_row))
            out = three_pass(scores, (solved_hi[m, h], solved_lo[m, h]))
            base[m, :, h * K : (h + 1) * K] = out[:, K:]
            r_hi, r_lo = split(q * jnp.exp(g_col) - out[:, :K])
            reach[m, :, 2 * h * K : (2 * h + 1) * K] = r_hi
            reach[m, :, (2 * h + 1) * K : (2 * h + 2) * K] = r_lo

    def state_copy(to):
        return pltpu.make_async_remote_copy(
            states.at[to], entering.at[own_pair], state_send.at[to], state_recv.at[own_pair],
            device_id={"ctx": to}, device_id_type=MESH,
        )

    def run_pair():
        maps[c] = mw[own_pair]
        state = None
        for j in range(CTX - 1):

            @pl.when(c != j)
            def _():
                pltpu.make_async_remote_copy(
                    mw.at[j], maps.at[j], map_send.at[j], map_recv.at[j],
                    device_id={"ctx": j}, device_id_type=MESH,
                ).wait_recv()

            add = maps[j, :, K:].astype(F32)
            if j == 0:
                state = add
            else:
                step = maps[j, :, :K]
                s_hi, s_lo = split(state)
                state = add + mm(
                    jnp.concatenate([step, step], axis=1), jnp.concatenate([s_hi, s_lo], axis=0)
                )
            states[j + 1] = state.astype(BF16)

            @pl.when(c != j + 1)
            def _():
                state_copy(j + 1).start()

            @pl.when(c == j + 1)
            def _():
                entering[own_pair] = states[j + 1]

    def ret_copy(d, m):
        to = lax.rem(z + d, MEM)
        return pltpu.make_async_remote_copy(
            reply.at[m, to], returned.at[z, m], ret_send.at[d, m], ret_recv.at[d, m],
            device_id={"mem": to}, device_id_type=MESH,
        )

    def send_outputs(m):
        for h in heads:
            p = m * HEADS + h

            @pl.when((c > 0) & (p != own_pair))
            def _():
                pltpu.make_async_remote_copy(
                    states.at[1], entering.at[p], state_send.at[1], state_recv.at[p],
                    device_id={"ctx": owner(m, h)}, device_id_type=MESH,
                ).wait_recv()

        for h in heads:
            at = slice(h * K, (h + 1) * K)
            s = entering[m * HEADS + h]
            heads_out = base[m, :, at] + mm(
                reach[m, :, 2 * h * K : (2 * h + 2) * K], jnp.concatenate([s, s], axis=0)
            )
            scale = lax.rsqrt(jnp.mean(heads_out * heads_out, axis=1, keepdims=True) + 1e-05)
            normed = (heads_out * scale * gain_ref[:, at]).astype(BF16)
            reply[m, :, :, at] = normed.reshape(MEM, CAP, K)
        for d in (2, 1, 3):
            ret_copy(d, m).start()

    @pl.when(c == 0)
    def _():
        entering[...] = jnp.zeros_like(entering)

    turn = jnp.where(own_stage < 2, 0, jnp.where(own_stage == 2, 1, 3))

    @pl.loop(0, LOCAL)
    def _(m):
        @pl.when(m == turn)
        def _():
            run_pair()

        local_output(m)

        @pl.when(m > 0)
        def _():
            send_outputs(m - 1)

    send_outputs(LOCAL - 1)

    column = jnp.broadcast_to(slots.astype(F32), (128, TOK)).T[:, 0:1].astype(jnp.int32)

    def pick(src, rows):
        chosen = ones_where(iota((TOK, ROWS), 1) + src * ROWS == column)
        return mm(chosen, rows)

    own_rows = jnp.concatenate([reply[m, z] for m in range(LOCAL)], axis=0)
    total = pick(z, own_rows)
    for d in (1, 3, 2):
        src = lax.rem(z + MEM - d, MEM)
        for m in range(LOCAL):
            pltpu.make_async_remote_copy(
                reply.at[m, z], returned.at[src, m], ret_send.at[d, m], ret_recv.at[d, m],
                device_id={"mem": src}, device_id_type=MESH,
            ).wait_recv()
        total = total + pick(src, returned[src].reshape(ROWS, WIDTH))
    picked[...] = total.astype(BF16)
    swap = pltpu.make_async_remote_copy(
        picked.at[aligned(1 - half, TOK // 2)], partner, pair_send.at[1], pair_recv.at[1],
        device_id=other, device_id_type=MESH,
    )
    swap.start()
    wo_load.wait()
    mixed = mm(picked[aligned(half, TOK // 2), :], wo[...])
    w_copy.wait()
    swap.wait()
    out_ref[...] = (mixed + mm(partner[...], w_other[...])).astype(BF16)

    for d in range(1, MEM):
        count_copy(d).wait_send()

    @pl.loop(0, LOCAL)
    def _(m):
        for d in range(1, MEM):
            x_copy(d, m).wait_send()
            ret_copy(d, m).wait_send()
        for d in range(MEM):
            forward(d, m).wait_send()
        for h in heads:

            @pl.when((m * HEADS + h != own_pair) & (c < CTX - 1))
            def _():
                map_copy(m, h).wait_send()

    @pl.loop(1, CTX)
    def _(j):
        @pl.when(c != j)
        def _():
            state_copy(j).wait_send()


def per_device(
    tokens, routes, w_query, w_key, w_value, w_beta, w_decay, decay_rate, norm_gain, w_out
):
    dma = pltpu.SemaphoreType.DMA
    vmem = pltpu.VMEM
    in_vmem = pl.BlockSpec(memory_space=pltpu.VMEM)
    in_place = pl.BlockSpec(memory_space=pl.ANY)
    return pl.pallas_call(
        layer_kernel,
        name="layer",
        out_shape=jax.ShapeDtypeStruct((TOK // 2, D), BF16),
        in_specs=[
            pl.BlockSpec(memory_space=pltpu.SMEM), in_vmem, in_place, in_place, in_place,
            in_place, in_vmem, in_vmem, in_vmem, in_place,
        ],
        out_specs=in_vmem,
        scratch_shapes=[
            vmem((TOK, DH), BF16),
            vmem((LOCAL, MEM, CAP, DH), BF16),
            vmem((MEM, 8, 128), F32),
            vmem((MEM, 8, 128), F32),
            vmem((LOCAL, ROWS, D), BF16),
            vmem((D, WIDTH), BF16),
            vmem((LOCAL, D, WIDTH), BF16),
            vmem((LOCAL, D, WIDTH), BF16),
            vmem((16, D), BF16),
            vmem((LOCAL, ROWS, 128), F32),
            vmem((LOCAL, 16, ROWS), F32),
            vmem((LOCAL, HEADS, ROWS, 2 * K), BF16),
            vmem((LOCAL, HEADS, ROWS, 2 * K), BF16),
            vmem((LOCAL, HEADS, ROWS, 2 * K), BF16),
            vmem((CTX, K, 2 * K), BF16),
            vmem((CTX, K, 2 * K), BF16),
            vmem((CTX, K, K), BF16),
            vmem((CTX, K, K), BF16),
            vmem((LOCAL, ROWS, WIDTH), F32),
            vmem((LOCAL, ROWS, 2 * WIDTH), BF16),
            vmem((LOCAL, MEM, CAP, WIDTH), BF16),
            vmem((MEM, LOCAL, CAP, WIDTH), BF16),
            vmem((TOK, WIDTH), BF16),
            vmem((TOK // 2, WIDTH), BF16),
            vmem((WIDTH, D), BF16),
            vmem((WIDTH, D), BF16),
            dma((3,)), dma((2, LOCAL)), dma((LOCAL,)),
            dma((MEM, LOCAL)), dma((MEM, LOCAL)), dma((MEM,)), dma((MEM,)),
            dma((MEM, LOCAL)), dma((MEM, LOCAL)),
            dma((CTX,)), dma((CTX,)), dma((CTX,)), dma((CTX,)),
            dma((MEM, LOCAL)), dma((MEM, LOCAL)), dma((2,)), dma((2,)),
        ],
        compiler_params=pltpu.CompilerParams(
            collective_id=0, has_side_effects=True, vmem_limit_bytes=67_043_328
        ),
    )(
        decay_rate,
        routes.reshape(1, TOK),
        tokens,
        w_query,
        w_key,
        w_value,
        jnp.swapaxes(w_beta, 1, 2),
        jnp.swapaxes(w_decay, 1, 2),
        norm_gain.reshape(1, WIDTH),
        w_out,
    )


def solution(mesh):
    in_specs = (
        P(("ctx", "mem"), None),
        P(("ctx", "mem"), None),
        P(None, "half"),
        P("mem", None, "half"),
        P("mem", None, "half"),
        P("mem", None, "half"),
        P("mem", None, "half"),
        P("mem", "half"),
        P("half"),
        P("half", None),
    )
    out_specs = P(("ctx", "mem", "half"), None)
    return jax.shard_map(
        per_device, mesh=mesh, in_specs=in_specs, out_specs=out_specs, check_vma=False
    )
```

```python
import jax
import jax.numpy as jnp
from jax import lax
from jax.experimental import pallas as pl
from jax.experimental.pallas import tpu as pltpu
from jax.sharding import PartitionSpec as P

MESH = pl.DeviceIdType.MESH
F32 = jnp.float32
BF16 = jnp.bfloat16
CTX, MEM = 16, 4
TOK = 512
D = 2048
DH = D // 2
CAP = 64
LOCAL = 4
HEADS = 4
ROWS = MEM * CAP
K = 128
WIDTH = HEADS * K


def mm(a, b):
    return jnp.dot(a, b, preferred_element_type=F32)


def mm_nt(a, b):
    return lax.dot_general(a, b, (((1,), (1,)), ((), ())), preferred_element_type=F32)


def split(x):
    hi = x.astype(BF16)
    return hi, (x - hi.astype(F32)).astype(BF16)


def iota(shape, axis):
    return lax.broadcasted_iota(jnp.int32, shape, axis)


def ones_where(mask):
    return mask.astype(F32).astype(BF16)


def aligned(index, size):
    return pl.ds(pl.multiple_of(index * size, size), size)


def unit(x):
    return x * lax.rsqrt(jnp.sum(x * x, axis=1, keepdims=True) + 1e-06)


def level_rows(x, size):
    return jnp.concatenate(
        [x[at + size : at + 2 * size] for at in range(0, x.shape[0], 2 * size)], axis=0
    )


def spread_rows(x, size):
    gap = jnp.zeros((size, x.shape[1]), x.dtype)
    parts = []
    for at in range(0, x.shape[0], size):
        parts += [gap, x[at : at + size]]
    return jnp.concatenate(parts, axis=0)


def unit_lower_inverses(blocks, beside):
    beside = list(beside)
    side = blocks[0].shape[0]
    row, col = iota((side, side), 0), iota((side, side), 1)
    apart = row ^ col
    eye = ones_where(row == col)
    low = [b.astype(BF16) for b in blocks]
    inverse = [jnp.where(apart == 1, -b, 0.0).astype(BF16) + eye for b in blocks]
    size = 2
    while size < side:
        whole = size < 16
        pick = (lambda x: x) if whole else (lambda x: level_rows(x, size))
        put = (lambda x: x) if whole else (lambda x: spread_rows(x, size))
        near = pick(apart)
        here = (near >= size) & (near < 2 * size)
        mid_way = [
            jnp.where(here, mm(pick(a), x), 0.0).astype(BF16) for a, x in zip(low, inverse)
        ]
        if beside:
            beside.pop(0)()
        update = [
            put(mm(pick(x), put(y)).astype(BF16)) for x, y in zip(inverse, mid_way)
        ]
        inverse = [x - u for x, u in zip(inverse, update)]
        size *= 2
    for work in beside:
        work()
    return inverse, eye


def three_pass(a, b):
    a_hi, a_lo = a
    b_hi, b_lo = b
    return mm(
        jnp.concatenate([a_hi, a_lo, a_hi], axis=1), jnp.concatenate([b_hi, b_hi, b_lo], axis=0)
    )


def layer_kernel(
    rate_ref, routes_ref, tok_ref, wq_ref, wk_ref, wv_ref, wb_ref, wd_ref, gain_ref, wo_ref,
    out_ref,
    tok, outgoing, counts, cnt, xbuf, wq, wk, wv, gates, kv, logits_s, total_s, total_ts, keys_s, solved_hi,
    solved_lo, mw, maps, states, entering, base, reach, reply, returned, picked, partner, wo,
    w_other,
    load_sem, wkv_sem, own_sem, x_send, x_recv, c_send, c_recv, f_send, f_recv,
    map_send, map_recv, state_send, state_recv, ret_send, ret_recv, pair_send, pair_recv,
):
    c = lax.axis_index("ctx")
    z = lax.axis_index("mem")
    half = lax.axis_index("half")
    other = {"half": 1 - half}
    mine = aligned(half, DH)
    heads = range(HEADS)
    own_stage = lax.rem(c // 4 + 2 * half, LOCAL)
    own_pair = own_stage * HEADS + lax.rem(c, 4)

    def owner(m, h):
        return lax.rem(m + 2 * half, LOCAL) * 4 + h

    tok_load = pltpu.make_async_copy(tok_ref.at[:, mine], tok, load_sem.at[0])
    tok_load.start()
    barrier = pltpu.get_barrier_semaphore()
    for d in range(1, MEM):
        pl.semaphore_signal(
            barrier, inc=1, device_id={"mem": lax.rem(z + d, MEM)}, device_id_type=MESH
        )
    pl.semaphore_signal(barrier, inc=1, device_id=other, device_id_type=MESH)
    for d in range(1, CTX):
        pl.semaphore_signal(
            barrier, inc=1, device_id={"ctx": lax.rem(c + d, CTX)}, device_id_type=MESH
        )

    def weights(m):
        return (
            pltpu.make_async_copy(wk_ref.at[m], wk.at[m], wkv_sem.at[0, m]),
            pltpu.make_async_copy(wv_ref.at[m], wv.at[m], wkv_sem.at[1, m]),
        )

    route = routes_ref[...]
    member = (iota((MEM * LOCAL, TOK), 0) == route).astype(F32)
    upper_tok = ones_where(iota((TOK, TOK), 0) <= iota((TOK, TOK), 1))
    place = jnp.sum(mm(member.astype(BF16), upper_tok) * member, axis=0, keepdims=True)
    slots = route * CAP + place.astype(jnp.int32) - 1
    totals = jnp.sum(member, axis=1, keepdims=True)
    counts[...] = jnp.zeros_like(counts)
    for to in range(MEM):
        counts[to, 0:LOCAL, :] = jnp.broadcast_to(
            totals[to * LOCAL : (to + 1) * LOCAL], (LOCAL, 128)
        )
    tok_load.wait()

    def x_copy(d, m):
        to = lax.rem(z + d, MEM)
        return pltpu.make_async_remote_copy(
            outgoing.at[m, to], xbuf.at[m, aligned(z, CAP), mine], x_send.at[d, m],
            x_recv.at[d, m], device_id={"mem": to}, device_id_type=MESH,
        )

    def x_arrival(d, m):
        src = lax.rem(z + MEM - d, MEM)
        return pltpu.make_async_remote_copy(
            outgoing.at[m, z], xbuf.at[m, aligned(src, CAP), mine], x_send.at[d, m],
            x_recv.at[d, m], device_id={"mem": src}, device_id_type=MESH,
        )

    def own_copy(m):
        return pltpu.make_async_copy(
            outgoing.at[m, z], xbuf.at[m, aligned(z, CAP), mine], own_sem.at[m]
        )

    def forward(d, m):
        src = lax.rem(z + MEM - d, MEM)
        landed = xbuf.at[m, aligned(src, CAP), mine]
        return pltpu.make_async_remote_copy(
            landed if d else outgoing.at[m, z], landed, f_send.at[d, m], f_recv.at[d, m],
            device_id=other, device_id_type=MESH,
        )

    def forward_arrival(d, m):
        src = lax.rem(z + MEM - d, MEM)
        landed = xbuf.at[m, aligned(src, CAP), aligned(1 - half, DH)]
        return pltpu.make_async_remote_copy(
            landed, landed, f_send.at[d, m], f_recv.at[d, m],
            device_id=other, device_id_type=MESH,
        )

    def count_copy(d):
        to = lax.rem(z + d, MEM)
        return pltpu.make_async_remote_copy(
            counts.at[to], cnt.at[z], c_send.at[d], c_recv.at[d],
            device_id={"mem": to}, device_id_type=MESH,
        )

    def gather(m):
        at = iota((ROWS, TOK), 0)
        slot = (at // CAP * LOCAL + m) * CAP + at % CAP
        rows = mm(ones_where(slot == slots), tok[...]).astype(BF16)
        outgoing[m] = rows.reshape(MEM, CAP, DH)

    def launch(m):
        for d in (2, 1, 3):
            x_copy(d, m).start()
        forward(0, m).start()
        own_copy(m).start()

    gather(0)
    pl.semaphore_wait(barrier, CTX - 1 + MEM)
    for d in range(1, MEM):
        count_copy(d).start()
    launch(0)
    for copy in weights(0):
        copy.start()
    cnt[z] = counts[z]

    @pl.loop(1, LOCAL)
    def _(m):
        gather(m)
        launch(m)
        for copy in weights(m):
            copy.start()

    wq_load = pltpu.make_async_copy(wq_ref, wq, load_sem.at[1])
    wq_load.start()
    wo_load = pltpu.make_async_copy(wo_ref, wo, load_sem.at[2])
    wo_load.start()

    def pass_on(m):
        for d in (1, 3, 2):
            x_arrival(d, m).wait_recv()
            forward(d, m).start()

    pass_on(0)
    for d in range(1, MEM):
        src = lax.rem(z + MEM - d, MEM)
        pltpu.make_async_remote_copy(
            counts.at[z], cnt.at[src], c_send.at[d], c_recv.at[d],
            device_id={"mem": src}, device_id_type=MESH,
        ).wait_recv()

    def map_copy(m, h):
        p = m * HEADS + h
        return pltpu.make_async_remote_copy(
            mw.at[p], maps.at[c], map_send.at[p], map_recv.at[c],
            device_id={"ctx": owner(m, h)}, device_id_type=MESH,
        )

    def fade_of(g_col, g_row):
        lower = iota((ROWS, ROWS), 0) >= iota((ROWS, ROWS), 1)
        return jnp.where(lower, jnp.exp(jnp.where(lower, g_col - g_row, 0.0)), 0.0)

    gates[...] = jnp.zeros_like(gates)

    def wait_tokens(m):
        for copy in weights(m):
            copy.wait()
        own_copy(m).wait()
        for d in range(MEM):
            forward_arrival(d, m).wait_recv()

    def projections(m):
        def gate_part():
            gates[0:HEADS, :] = wb_ref[m]
            gates[HEADS : 2 * HEADS, :] = wd_ref[m]
            logits_s[...] = mm_nt(gates[...], xbuf[m])

        def part(w, at, to):
            def run():
                kv[:, to : to + 2 * K] = mm(xbuf[m], w[m, :, at : at + 2 * K])

            return run

        return [gate_part] + [
            part(w, at, first + at) for w, first in ((wk, 0), (wv, WIDTH)) for at in (0, 2 * K)
        ]

    def make_maps(m, following):
        if following is not None:
            pass_on(following)
        logits = logits_s[...]
        keys_all = kv[:, :WIDTH]
        values_all = kv[:, WIDTH:]

        lane = iota((1, 128), 1)
        cnt_of = [cnt[src, pl.ds(m, 1), :] for src in range(MEM)]
        cnt_row = jnp.concatenate(
            [
                jnp.where(lane < CAP, cnt_of[0], cnt_of[1]),
                jnp.where(lane < CAP, cnt_of[2], cnt_of[3]),
            ],
            axis=1,
        )
        live = ((iota((1, ROWS), 1) & (CAP - 1)).astype(F32) < cnt_row).astype(F32)
        gate = iota((16, 1), 0)
        rate = jnp.zeros((16, 1), F32)
        for h in heads:
            rate = jnp.where(gate == HEADS + h, rate_ref[m, h], rate)
        strength = jax.nn.sigmoid(logits) * live
        soft = jnp.maximum(logits, 0.0) + jnp.log1p(jnp.exp(-jnp.abs(logits)))
        forget = -rate * soft * live
        upper = ones_where(iota((ROWS, ROWS), 0) <= iota((ROWS, ROWS), 1))
        hi, mid = split(forget)
        low = (forget - hi.astype(F32) - mid.astype(F32)).astype(BF16)
        total_t = mm(hi, upper) + mm(mid, upper) + mm(low, upper)
        both_t = jnp.where(gate < HEADS, strength, total_t)
        both = jnp.concatenate([both_t, jnp.zeros((112, ROWS), F32)], axis=0).T
        total_ts[m] = both_t
        total_s[m] = both

        keys, corner, target = [None] * HEADS, [None] * HEADS, [None] * HEADS
        blocks = [None] * (2 * HEADS)
        last = both[ROWS - 1 : ROWS, :]
        square = iota((K, K), 0), iota((K, K), 1)
        strict = square[0] > square[1]
        for h in heads:
            at = slice(h * K, (h + 1) * K)
            k = unit(keys_all[:, at])
            keys[h] = k
            k_hi, k_lo = split(k)
            keys_s[m, h, :, :K] = k_hi
            keys_s[m, h, :, K:] = k_lo
            gram = mm_nt(
                jnp.concatenate([k_hi, k_lo], axis=1), jnp.concatenate([k_hi, k_hi], axis=1)
            ) + mm_nt(k_hi, k_lo)
            g_col = both[:, HEADS + h : HEADS + h + 1]
            g_row = both_t[HEADS + h : HEADS + h + 1, :]
            beta = both[:, h : h + 1]
            for b in range(2):
                part = slice(b * K, (b + 1) * K)
                gap = jnp.minimum(g_col[part] - g_row[:, part], 0.0)
                mix = gram[part, part] * jnp.exp(gap) * beta[part]
                blocks[2 * h + b] = jnp.where(strict, mix, 0.0)
            corner[h] = gram[K:, :K] * jnp.exp(g_col[K:] - g_row[:, :K]) * beta[K:]
            target[h] = jnp.concatenate(
                [(beta * jnp.exp(g_col)) * k, beta * values_all[:, at]], axis=1
            )
        beside = []
        if following is not None:
            wait_tokens(following)
            beside = projections(following)
        inverse, eye = unit_lower_inverses(blocks, beside)
        none = jnp.zeros((K, K), BF16)
        cross = [
            mm(corner[h].astype(BF16), inverse[2 * h]).astype(BF16) for h in heads
        ]
        cross = [mm(inverse[2 * h + 1], cross[h]).astype(BF16) for h in heads]
        inverse = [
            jnp.concatenate(
                [
                    jnp.concatenate([inverse[2 * h] - eye, none], axis=1),
                    jnp.concatenate([-cross[h], inverse[2 * h + 1] - eye], axis=1),
                ],
                axis=0,
            )
            for h in heads
        ]
        guess = [target[h] + mm(inverse[h], target[h].astype(BF16)) for h in heads]
        rest = [None] * HEADS
        for h in heads:
            a_hi, a_lo = split(blocks[2 * h])
            b_hi, b_lo = split(blocks[2 * h + 1])
            c_hi, c_lo = split(corner[h])
            mix_hi = jnp.concatenate(
                [jnp.concatenate([a_hi, none], axis=1), jnp.concatenate([c_hi, b_hi], axis=1)],
                axis=0,
            )
            mix_lo = jnp.concatenate(
                [jnp.concatenate([a_lo, none], axis=1), jnp.concatenate([c_lo, b_lo], axis=1)],
                axis=0,
            )
            rest[h] = target[h] - guess[h] - three_pass((mix_hi, mix_lo), split(guess[h]))
        solved = [
            guess[h] + rest[h] + mm(inverse[h], rest[h].astype(BF16)) for h in heads
        ]
        diagonal = square[0] == square[1]
        for h in heads:
            y = split(solved[h])
            solved_hi[m, h], solved_lo[m, h] = y
            g_last = last[:, HEADS + h : HEADS + h + 1]
            tail = keys[h] * jnp.exp(g_last - both[:, HEADS + h : HEADS + h + 1])
            out = three_pass(split(tail.T), y)
            p = m * HEADS + h
            mw[p, :, :K] = (jnp.where(diagonal, jnp.exp(g_last), 0.0) - out[:, :K]).astype(BF16)
            mw[p, :, K:] = out[:, K:].astype(BF16)
        for h in heads:

            @pl.when((m * HEADS + h != own_pair) & (c < CTX - 1))
            def _():
                map_copy(m, h).start()

    wait_tokens(0)
    for work in projections(0):
        work()

    @pl.loop(0, LOCAL - 1)
    def _(m):
        make_maps(m, m + 1)

    make_maps(LOCAL - 1, None)

    w_copy = pltpu.make_async_remote_copy(
        wo_ref, w_other, pair_send.at[0], pair_recv.at[0], device_id=other, device_id_type=MESH
    )
    w_copy.start()
    wq_load.wait()

    def local_output(m):
        query_all = mm(xbuf[m], wq[...])
        both = total_s[m]
        for h in heads:
            q = unit(query_all[:, h * K : (h + 1) * K])
            q_hi, q_lo = split(q)
            k_hi, k_lo = keys_s[m, h, :, :K], keys_s[m, h, :, K:]
            gram = mm_nt(
                jnp.concatenate([q_hi, q_lo], axis=1), jnp.concatenate([k_hi, k_hi], axis=1)
            ) + mm_nt(q_hi, k_lo)
            g_col = both[:, HEADS + h : HEADS + h + 1]
            g_row = total_ts[m, HEADS + h : HEADS + h + 1, :]
            scores = split(gram * fade_of(g_col, g_row))
            out = three_pass(scores, (solved_hi[m, h], solved_lo[m, h]))
            base[m, :, h * K : (h + 1) * K] = out[:, K:]
            r_hi, r_lo = split(q * jnp.exp(g_col) - out[:, :K])
            reach[m, :, 2 * h * K : (2 * h + 1) * K] = r_hi
            reach[m, :, (2 * h + 1) * K : (2 * h + 2) * K] = r_lo

    def state_copy(to):
        return pltpu.make_async_remote_copy(
            states.at[to], entering.at[own_pair], state_send.at[to], state_recv.at[own_pair],
            device_id={"ctx": to}, device_id_type=MESH,
        )

    def run_pair():
        maps[c] = mw[own_pair]
        state = None
        for j in range(CTX - 1):

            @pl.when(c != j)
            def _():
                pltpu.make_async_remote_copy(
                    mw.at[j], maps.at[j], map_send.at[j], map_recv.at[j],
                    device_id={"ctx": j}, device_id_type=MESH,
                ).wait_recv()

            add = maps[j, :, K:].astype(F32)
            if j == 0:
                state = add
            else:
                step = maps[j, :, :K]
                s_hi, s_lo = split(state)
                state = add + mm(
                    jnp.concatenate([step, step], axis=1), jnp.concatenate([s_hi, s_lo], axis=0)
                )
            states[j + 1] = state.astype(BF16)

            @pl.when(c != j + 1)
            def _():
                state_copy(j + 1).start()

            @pl.when(c == j + 1)
            def _():
                entering[own_pair] = states[j + 1]

    def ret_copy(d, m):
        to = lax.rem(z + d, MEM)
        return pltpu.make_async_remote_copy(
            reply.at[m, to], returned.at[z, m], ret_send.at[d, m], ret_recv.at[d, m],
            device_id={"mem": to}, device_id_type=MESH,
        )

    def send_outputs(m):
        for h in heads:
            p = m * HEADS + h

            @pl.when((c > 0) & (p != own_pair))
            def _():
                pltpu.make_async_remote_copy(
                    states.at[1], entering.at[p], state_send.at[1], state_recv.at[p],
                    device_id={"ctx": owner(m, h)}, device_id_type=MESH,
                ).wait_recv()

        for h in heads:
            at = slice(h * K, (h + 1) * K)
            s = entering[m * HEADS + h]
            heads_out = base[m, :, at] + mm(
                reach[m, :, 2 * h * K : (2 * h + 2) * K], jnp.concatenate([s, s], axis=0)
            )
            scale = lax.rsqrt(jnp.mean(heads_out * heads_out, axis=1, keepdims=True) + 1e-05)
            normed = (heads_out * scale * gain_ref[:, at]).astype(BF16)
            reply[m, :, :, at] = normed.reshape(MEM, CAP, K)
        for d in (2, 1, 3):
            ret_copy(d, m).start()

    @pl.when(c == 0)
    def _():
        entering[...] = jnp.zeros_like(entering)

    turn = jnp.where(own_stage < 2, 0, 1)

    @pl.loop(0, LOCAL - 1)
    def _(m):
        @pl.when((own_stage < LOCAL - 1) & (m == turn))
        def _():
            run_pair()

        local_output(m)

    @pl.when(own_stage == LOCAL - 1)
    def _():
        run_pair()

    @pl.loop(0, LOCAL - 1)
    def _(m):
        send_outputs(m)

    local_output(LOCAL - 1)
    send_outputs(LOCAL - 1)

    column = jnp.broadcast_to(slots.astype(F32), (128, TOK)).T[:, 0:1].astype(jnp.int32)

    def pick(src, rows):
        chosen = ones_where(iota((TOK, ROWS), 1) + src * ROWS == column)
        return mm(chosen, rows)

    own_rows = jnp.concatenate([reply[m, z] for m in range(LOCAL)], axis=0)
    total = pick(z, own_rows)
    for d in (1, 3, 2):
        src = lax.rem(z + MEM - d, MEM)
        for m in range(LOCAL):
            pltpu.make_async_remote_copy(
                reply.at[m, z], returned.at[src, m], ret_send.at[d, m], ret_recv.at[d, m],
                device_id={"mem": src}, device_id_type=MESH,
            ).wait_recv()
        total = total + pick(src, returned[src].reshape(ROWS, WIDTH))
    picked[...] = total.astype(BF16)
    swap = pltpu.make_async_remote_copy(
        picked.at[aligned(1 - half, TOK // 2)], partner, pair_send.at[1], pair_recv.at[1],
        device_id=other, device_id_type=MESH,
    )
    swap.start()
    wo_load.wait()
    mixed = mm(picked[aligned(half, TOK // 2), :], wo[...])
    w_copy.wait()
    swap.wait()
    out_ref[...] = (mixed + mm(partner[...], w_other[...])).astype(BF16)

    for d in range(1, MEM):
        count_copy(d).wait_send()

    @pl.loop(0, LOCAL)
    def _(m):
        for d in range(1, MEM):
            x_copy(d, m).wait_send()
            ret_copy(d, m).wait_send()
        for d in range(MEM):
            forward(d, m).wait_send()
        for h in heads:

            @pl.when((m * HEADS + h != own_pair) & (c < CTX - 1))
            def _():
                map_copy(m, h).wait_send()

    @pl.loop(1, CTX)
    def _(j):
        @pl.when(c != j)
        def _():
            state_copy(j).wait_send()


def per_device(
    tokens, routes, w_query, w_key, w_value, w_beta, w_decay, decay_rate, norm_gain, w_out
):
    dma = pltpu.SemaphoreType.DMA
    vmem = pltpu.VMEM
    in_vmem = pl.BlockSpec(memory_space=pltpu.VMEM)
    in_place = pl.BlockSpec(memory_space=pl.ANY)
    return pl.pallas_call(
        layer_kernel,
        name="layer",
        out_shape=jax.ShapeDtypeStruct((TOK // 2, D), BF16),
        in_specs=[
            pl.BlockSpec(memory_space=pltpu.SMEM), in_vmem, in_place, in_place, in_place,
            in_place, in_vmem, in_vmem, in_vmem, in_place,
        ],
        out_specs=in_vmem,
        scratch_shapes=[
            vmem((TOK, DH), BF16),
            vmem((LOCAL, MEM, CAP, DH), BF16),
            vmem((MEM, 8, 128), F32),
            vmem((MEM, 8, 128), F32),
            vmem((LOCAL, ROWS, D), BF16),
            vmem((D, WIDTH), BF16),
            vmem((LOCAL, D, WIDTH), BF16),
            vmem((LOCAL, D, WIDTH), BF16),
            vmem((16, D), BF16),
            vmem((ROWS, 2 * WIDTH), F32),
            vmem((16, ROWS), F32),
            vmem((LOCAL, ROWS, 128), F32),
            vmem((LOCAL, 16, ROWS), F32),
            vmem((LOCAL, HEADS, ROWS, 2 * K), BF16),
            vmem((LOCAL, HEADS, ROWS, 2 * K), BF16),
            vmem((LOCAL, HEADS, ROWS, 2 * K), BF16),
            vmem((CTX, K, 2 * K), BF16),
            vmem((CTX, K, 2 * K), BF16),
            vmem((CTX, K, K), BF16),
            vmem((CTX, K, K), BF16),
            vmem((LOCAL, ROWS, WIDTH), F32),
            vmem((LOCAL, ROWS, 2 * WIDTH), BF16),
            vmem((LOCAL, MEM, CAP, WIDTH), BF16),
            vmem((MEM, LOCAL, CAP, WIDTH), BF16),
            vmem((TOK, WIDTH), BF16),
            vmem((TOK // 2, WIDTH), BF16),
            vmem((WIDTH, D), BF16),
            vmem((WIDTH, D), BF16),
            dma((3,)), dma((2, LOCAL)), dma((LOCAL,)),
            dma((MEM, LOCAL)), dma((MEM, LOCAL)), dma((MEM,)), dma((MEM,)),
            dma((MEM, LOCAL)), dma((MEM, LOCAL)),
            dma((CTX,)), dma((CTX,)), dma((CTX,)), dma((CTX,)),
            dma((MEM, LOCAL)), dma((MEM, LOCAL)), dma((2,)), dma((2,)),
        ],
        compiler_params=pltpu.CompilerParams(
            collective_id=0, has_side_effects=True, vmem_limit_bytes=67_043_328
        ),
    )(
        decay_rate,
        routes.reshape(1, TOK),
        tokens,
        w_query,
        w_key,
        w_value,
        jnp.swapaxes(w_beta, 1, 2),
        jnp.swapaxes(w_decay, 1, 2),
        norm_gain.reshape(1, WIDTH),
        w_out,
    )


def solution(mesh):
    in_specs = (
        P(("ctx", "mem"), None),
        P(("ctx", "mem"), None),
        P(None, "half"),
        P("mem", None, "half"),
        P("mem", None, "half"),
        P("mem", None, "half"),
        P("mem", None, "half"),
        P("mem", "half"),
        P("half"),
        P("half", None),
    )
    out_specs = P(("ctx", "mem", "half"), None)
    return jax.shard_map(
        per_device, mesh=mesh, in_specs=in_specs, out_specs=out_specs, check_vma=False
    )
```

```python
import jax
import jax.numpy as jnp
from jax import lax
from jax.experimental import pallas as pl
from jax.experimental.pallas import tpu as pltpu
from jax.sharding import PartitionSpec as P

MESH = pl.DeviceIdType.MESH
F32 = jnp.float32
BF16 = jnp.bfloat16
CTX, MEM = 16, 4
TOK = 512
D = 2048
DH = D // 2
CAP = 64
LOCAL = 4
HEADS = 4
ROWS = MEM * CAP
K = 128
WIDTH = HEADS * K


def mm(a, b):
    return jnp.dot(a, b, preferred_element_type=F32)


def mm_nt(a, b):
    return lax.dot_general(a, b, (((1,), (1,)), ((), ())), preferred_element_type=F32)


def split(x):
    hi = x.astype(BF16)
    return hi, (x - hi.astype(F32)).astype(BF16)


def iota(shape, axis):
    return lax.broadcasted_iota(jnp.int32, shape, axis)


def ones_where(mask):
    return mask.astype(F32).astype(BF16)


def aligned(index, size):
    return pl.ds(pl.multiple_of(index * size, size), size)


def unit(x):
    return x * lax.rsqrt(jnp.sum(x * x, axis=1, keepdims=True) + 1e-06)


def level_rows(x, size):
    return jnp.concatenate(
        [x[at + size : at + 2 * size] for at in range(0, x.shape[0], 2 * size)], axis=0
    )


def spread_rows(x, size):
    gap = jnp.zeros((size, x.shape[1]), x.dtype)
    parts = []
    for at in range(0, x.shape[0], size):
        parts += [gap, x[at : at + size]]
    return jnp.concatenate(parts, axis=0)


def unit_lower_inverses(low, inverse, beside):
    beside = list(beside)
    side = low[0].shape[0]
    apart = iota((side, side), 0) ^ iota((side, side), 1)
    size = 2
    while size < side:
        whole = size < 16
        pick = (lambda x: x) if whole else (lambda x: level_rows(x, size))
        put = (lambda x: x) if whole else (lambda x: spread_rows(x, size))
        near = pick(apart)
        here = (near >= size) & (near < 2 * size)
        mid_way = [
            jnp.where(here, mm(pick(a), x), 0.0).astype(BF16) for a, x in zip(low, inverse)
        ]
        if beside:
            beside.pop(0)()
        update = [
            put(mm(pick(x), put(y)).astype(BF16)) for x, y in zip(inverse, mid_way)
        ]
        inverse = [x - u for x, u in zip(inverse, update)]
        size *= 2
    for work in beside:
        work()
    return inverse


def three_pass(a, b):
    a_hi, a_lo = a
    b_hi, b_lo = b
    return mm(
        jnp.concatenate([a_hi, a_lo, a_hi], axis=1), jnp.concatenate([b_hi, b_hi, b_lo], axis=0)
    )


def layer_kernel(
    rate_ref, routes_hbm, tok_ref, wq_ref, wk_ref, wv_ref, wb_hbm, wd_hbm, gain_hbm, wo_ref,
    out_ref,
    routes_ref, wb_ref, wd_ref, gain_ref, tok, outgoing, counts, cnt, xbuf, wq, wk, wv, gates, kv, logits_s, fades, total_ts, keys_s, solved_hi,
    solved_lo, mw, maps, states, entering, base, reach, reply, returned, picked, partner, wo,
    w_other,
    load_sem, wkv_sem, own_sem, x_send, x_recv, c_send, c_recv, f_send, f_recv,
    map_send, map_recv, state_send, state_recv, ret_send, ret_recv, pair_send, pair_recv,
):
    c = lax.axis_index("ctx")
    z = lax.axis_index("mem")
    half = lax.axis_index("half")
    other = {"half": 1 - half}
    mine = aligned(half, DH)
    heads = range(HEADS)
    own_stage = lax.rem(c // 4 + 2 * half, LOCAL)
    own_pair = own_stage * HEADS + lax.rem(c, 4)

    def owner(m, h):
        return lax.rem(m + 2 * half, LOCAL) * 4 + h

    tok_load = pltpu.make_async_copy(tok_ref.at[:, mine], tok, load_sem.at[0])
    routes_load = pltpu.make_async_copy(routes_hbm, routes_ref, load_sem.at[3])
    routes_load.start()
    tok_load.start()
    small_loads = [
        pltpu.make_async_copy(wb_hbm, wb_ref, load_sem.at[4]),
        pltpu.make_async_copy(wd_hbm, wd_ref, load_sem.at[5]),
        pltpu.make_async_copy(gain_hbm, gain_ref, load_sem.at[6]),
    ]
    for load in small_loads:
        load.start()
    barrier = pltpu.get_barrier_semaphore()
    for d in range(1, MEM):
        pl.semaphore_signal(
            barrier, inc=1, device_id={"mem": lax.rem(z + d, MEM)}, device_id_type=MESH
        )
    pl.semaphore_signal(barrier, inc=1, device_id=other, device_id_type=MESH)
    for d in range(1, CTX):
        pl.semaphore_signal(
            barrier, inc=1, device_id={"ctx": lax.rem(c + d, CTX)}, device_id_type=MESH
        )

    def weights(m):
        return (
            pltpu.make_async_copy(wk_ref.at[m], wk.at[m], wkv_sem.at[0, m]),
            pltpu.make_async_copy(wv_ref.at[m], wv.at[m], wkv_sem.at[1, m]),
        )

    routes_load.wait()
    route = routes_ref[...]
    member = (iota((MEM * LOCAL, TOK), 0) == route).astype(F32)
    upper_tok = ones_where(iota((TOK, TOK), 0) <= iota((TOK, TOK), 1))
    place = jnp.sum(mm(member.astype(BF16), upper_tok) * member, axis=0, keepdims=True)
    slots = route * CAP + place.astype(jnp.int32) - 1
    totals = jnp.sum(member, axis=1, keepdims=True)
    counts[...] = jnp.zeros_like(counts)
    for to in range(MEM):
        counts[to, 0:LOCAL, :] = jnp.broadcast_to(
            totals[to * LOCAL : (to + 1) * LOCAL], (LOCAL, 128)
        )
    tok_load.wait()

    def x_copy(d, m):
        to = lax.rem(z + d, MEM)
        return pltpu.make_async_remote_copy(
            outgoing.at[m, to], xbuf.at[m, aligned(z, CAP), mine], x_send.at[d, m],
            x_recv.at[d, m], device_id={"mem": to}, device_id_type=MESH,
        )

    def x_arrival(d, m):
        src = lax.rem(z + MEM - d, MEM)
        return pltpu.make_async_remote_copy(
            outgoing.at[m, z], xbuf.at[m, aligned(src, CAP), mine], x_send.at[d, m],
            x_recv.at[d, m], device_id={"mem": src}, device_id_type=MESH,
        )

    def own_copy(m):
        return pltpu.make_async_copy(
            outgoing.at[m, z], xbuf.at[m, aligned(z, CAP), mine], own_sem.at[m]
        )

    def forward(d, m):
        src = lax.rem(z + MEM - d, MEM)
        landed = xbuf.at[m, aligned(src, CAP), mine]
        return pltpu.make_async_remote_copy(
            landed if d else outgoing.at[m, z], landed, f_send.at[d, m], f_recv.at[d, m],
            device_id=other, device_id_type=MESH,
        )

    def forward_arrival(d, m):
        src = lax.rem(z + MEM - d, MEM)
        landed = xbuf.at[m, aligned(src, CAP), aligned(1 - half, DH)]
        return pltpu.make_async_remote_copy(
            landed, landed, f_send.at[d, m], f_recv.at[d, m],
            device_id=other, device_id_type=MESH,
        )

    def count_copy(d):
        to = lax.rem(z + d, MEM)
        return pltpu.make_async_remote_copy(
            counts.at[to], cnt.at[z], c_send.at[d], c_recv.at[d],
            device_id={"mem": to}, device_id_type=MESH,
        )

    def gather(m):
        at = iota((ROWS, TOK), 0)
        slot = (at // CAP * LOCAL + m) * CAP + at % CAP
        rows = mm(ones_where(slot == slots), tok[...]).astype(BF16)
        outgoing[m] = rows.reshape(MEM, CAP, DH)

    def launch(m):
        for d in (2, 1, 3):
            x_copy(d, m).start()
        forward(0, m).start()
        own_copy(m).start()

    gather(0)
    pl.semaphore_wait(barrier, CTX - 1 + MEM)
    for d in range(1, MEM):
        count_copy(d).start()
    launch(0)
    for copy in weights(0):
        copy.start()
    cnt[z] = counts[z]

    @pl.loop(1, LOCAL)
    def _(m):
        gather(m)
        launch(m)
        for copy in weights(m):
            copy.start()

    wq_load = pltpu.make_async_copy(wq_ref, wq, load_sem.at[1])
    wq_load.start()
    wo_load = pltpu.make_async_copy(wo_ref, wo, load_sem.at[2])
    wo_load.start()

    def pass_on(m):
        for d in (1, 3, 2):
            x_arrival(d, m).wait_recv()
            forward(d, m).start()

    pass_on(0)
    for d in range(1, MEM):
        src = lax.rem(z + MEM - d, MEM)
        pltpu.make_async_remote_copy(
            counts.at[z], cnt.at[src], c_send.at[d], c_recv.at[d],
            device_id={"mem": src}, device_id_type=MESH,
        ).wait_recv()

    def map_copy(m, h):
        p = m * HEADS + h
        return pltpu.make_async_remote_copy(
            mw.at[p], maps.at[c], map_send.at[p], map_recv.at[c],
            device_id={"ctx": owner(m, h)}, device_id_type=MESH,
        )

    gates[...] = jnp.zeros_like(gates)
    for load in small_loads:
        load.wait()
    square = iota((K, K), 0), iota((K, K), 1)
    none = jnp.zeros((K, K), BF16)

    def block_lower(first, below, second):
        return jnp.concatenate(
            [
                jnp.concatenate([first, none], axis=1),
                jnp.concatenate([below, second], axis=1),
            ],
            axis=0,
        )

    def wait_tokens(m):
        for copy in weights(m):
            copy.wait()
        own_copy(m).wait()
        for d in range(MEM):
            forward_arrival(d, m).wait_recv()

    def projections(m):
        def gate_part():
            gates[0:HEADS, :] = wb_ref[m]
            gates[HEADS : 2 * HEADS, :] = wd_ref[m]
            logits_s[...] = mm_nt(gates[...], xbuf[m])

        def part(w, at, to):
            def run():
                kv[:, to : to + 2 * K] = mm(xbuf[m], w[m, :, at : at + 2 * K])

            return run

        return [gate_part] + [
            part(w, at, first + at) for w, first in ((wk, 0), (wv, WIDTH)) for at in (0, 2 * K)
        ]

    def make_maps(m, following):
        if following is not None:
            pass_on(following)
        logits = logits_s[...]
        keys_all = kv[:, :WIDTH]
        values_all = kv[:, WIDTH:]

        lane = iota((1, 128), 1)
        cnt_of = [cnt[src, pl.ds(m, 1), :] for src in range(MEM)]
        cnt_row = jnp.concatenate(
            [
                jnp.where(lane < CAP, cnt_of[0], cnt_of[1]),
                jnp.where(lane < CAP, cnt_of[2], cnt_of[3]),
            ],
            axis=1,
        )
        live = ((iota((1, ROWS), 1) & (CAP - 1)).astype(F32) < cnt_row).astype(F32)
        gate = iota((16, 1), 0)
        rate = jnp.zeros((16, 1), F32)
        for h in heads:
            rate = jnp.where(gate == HEADS + h, rate_ref[m, h], rate)
        strength = jax.nn.sigmoid(logits) * live
        soft = jnp.maximum(logits, 0.0) + jnp.log1p(jnp.exp(-jnp.abs(logits)))
        forget = -rate * soft * live
        upper = ones_where(iota((ROWS, ROWS), 0) <= iota((ROWS, ROWS), 1))
        hi, mid = split(forget)
        low = (forget - hi.astype(F32) - mid.astype(F32)).astype(BF16)
        total_t = mm(hi, upper) + mm(mid, upper) + mm(low, upper)
        both_t = jnp.where(gate < HEADS, strength, total_t)
        total_ts[m] = both_t
        b_hi, b_mid = split(both_t)
        b_low = (both_t - b_hi.astype(F32) - b_mid.astype(F32)).astype(BF16)
        at_gate = iota((48, 2 * WIDTH), 0) & 15
        wide = lax.dot_general(
            jnp.concatenate([b_hi, b_mid, b_low], axis=0),
            ones_where(at_gate == iota((48, 2 * WIDTH), 1) // K),
            (((0,), (0,)), ((), ())),
            preferred_element_type=F32,
        )
        fades[m] = wide[:, WIDTH:]

        keys, corner, target = [None] * HEADS, [None] * HEADS, [None] * HEADS
        blocks, inverse = [None] * (2 * HEADS), [None] * (2 * HEADS)
        strict = square[0] > square[1]
        pair = (square[0] ^ square[1]) == 1
        eye = ones_where(square[0] == square[1])
        for h in heads:
            at = slice(h * K, (h + 1) * K)
            k = unit(keys_all[:, at])
            keys[h] = k
            k_hi, k_lo = split(k)
            keys_s[m, h, :, :K] = k_hi
            keys_s[m, h, :, K:] = k_lo
            gram = mm_nt(
                jnp.concatenate([k_hi, k_lo], axis=1), jnp.concatenate([k_hi, k_hi], axis=1)
            ) + mm_nt(k_hi, k_lo)
            beta = wide[:, at]
            g_col = wide[:, WIDTH + h * K : WIDTH + (h + 1) * K]
            g_row = both_t[HEADS + h : HEADS + h + 1, :]
            for b in range(2):
                part = slice(b * K, (b + 1) * K)
                gap = jnp.minimum(g_col[part] - g_row[:, part], 0.0)
                mix = jnp.where(strict, gram[part, part] * jnp.exp(gap) * beta[part], 0.0)
                blocks[2 * h + b] = split(mix)
                inverse[2 * h + b] = jnp.where(pair, -mix, 0.0).astype(BF16) + eye
            corner[h] = split(gram[K:, :K] * jnp.exp(g_col[K:] - g_row[:, :K]) * beta[K:])
            target[h] = jnp.concatenate(
                [(beta * jnp.exp(g_col)) * k, beta * values_all[:, at]], axis=1
            )
        beside = []
        if following is not None:
            wait_tokens(following)
            beside = projections(following)
        inverse = unit_lower_inverses([b[0] for b in blocks], inverse, beside)
        cross = [mm(corner[h][0], inverse[2 * h]).astype(BF16) for h in heads]
        cross = [mm(inverse[2 * h + 1], cross[h]).astype(BF16) for h in heads]
        inverse = [
            block_lower(inverse[2 * h] - eye, -cross[h], inverse[2 * h + 1] - eye) for h in heads
        ]
        shift = [mm(inverse[h], target[h].astype(BF16)) for h in heads]
        guess = [target[h] + shift[h] for h in heads]
        rest = [None] * HEADS
        for h in heads:
            mix = tuple(
                block_lower(blocks[2 * h][i], corner[h][i], blocks[2 * h + 1][i]) for i in range(2)
            )
            rest[h] = -(shift[h] + three_pass(mix, split(guess[h])))
        solved = [
            guess[h] + (rest[h] + mm(inverse[h], rest[h].astype(BF16))) for h in heads
        ]
        diagonal = square[0] == square[1]
        for h in heads:
            y = split(solved[h])
            solved_hi[m, h], solved_lo[m, h] = y
            g_col = fades[m, :, h * K : (h + 1) * K]
            g_last = g_col[ROWS - 1 : ROWS, :]
            out = three_pass(split((keys[h] * jnp.exp(g_last - g_col)).T), y)
            p = m * HEADS + h
            mw[p, :, :K] = (jnp.where(diagonal, jnp.exp(g_last), 0.0) - out[:, :K]).astype(BF16)
            mw[p, :, K:] = out[:, K:].astype(BF16)
        for h in heads:

            @pl.when((m * HEADS + h != own_pair) & (c < CTX - 1))
            def _():
                map_copy(m, h).start()

    wait_tokens(0)
    for work in projections(0):
        work()

    @pl.loop(0, LOCAL - 1)
    def _(m):
        make_maps(m, m + 1)

    make_maps(LOCAL - 1, None)

    w_copy = pltpu.make_async_remote_copy(
        wo_ref, w_other, pair_send.at[0], pair_recv.at[0], device_id=other, device_id_type=MESH
    )
    w_copy.start()
    wq_load.wait()

    def local_output(m):
        query_all = mm(xbuf[m], wq[...])
        lower = square[0] >= square[1]
        for h in heads:
            at = slice(h * K, (h + 1) * K)
            q = unit(query_all[:, at])
            q_hi, q_lo = split(q)
            k_hi, k_lo = keys_s[m, h, :, :K], keys_s[m, h, :, K:]
            gram = mm_nt(
                jnp.concatenate([q_hi, q_lo], axis=1), jnp.concatenate([k_hi, k_hi], axis=1)
            ) + mm_nt(q_hi, k_lo)
            g_col = fades[m, :, at]
            g_row = total_ts[m, HEADS + h : HEADS + h + 1, :]
            parts = []
            for b in range(2):
                part = slice(b * K, (b + 1) * K)
                gap = jnp.minimum(g_col[part] - g_row[:, part], 0.0)
                parts.append(split(jnp.where(lower, gram[part, part] * jnp.exp(gap), 0.0)))
            below = split(gram[K:, :K] * jnp.exp(g_col[K:] - g_row[:, :K]))
            scores = tuple(block_lower(parts[0][i], below[i], parts[1][i]) for i in range(2))
            out = three_pass(scores, (solved_hi[m, h], solved_lo[m, h]))
            base[m, :, h * K : (h + 1) * K] = out[:, K:]
            r_hi, r_lo = split(q * jnp.exp(g_col) - out[:, :K])
            reach[m, :, 2 * h * K : (2 * h + 1) * K] = r_hi
            reach[m, :, (2 * h + 1) * K : (2 * h + 2) * K] = r_lo

    def state_copy(to):
        return pltpu.make_async_remote_copy(
            states.at[to], entering.at[own_pair], state_send.at[to], state_recv.at[own_pair],
            device_id={"ctx": to}, device_id_type=MESH,
        )

    def run_pair():
        maps[c] = mw[own_pair]
        state = None
        for j in range(CTX - 1):

            @pl.when(c != j)
            def _():
                pltpu.make_async_remote_copy(
                    mw.at[j], maps.at[j], map_send.at[j], map_recv.at[j],
                    device_id={"ctx": j}, device_id_type=MESH,
                ).wait_recv()

            add = maps[j, :, K:].astype(F32)
            if j == 0:
                state = add
            else:
                step = maps[j, :, :K]
                s_hi, s_lo = split(state)
                state = add + mm(
                    jnp.concatenate([step, step], axis=1), jnp.concatenate([s_hi, s_lo], axis=0)
                )
            states[j + 1] = state.astype(BF16)

            @pl.when(c != j + 1)
            def _():
                state_copy(j + 1).start()

            @pl.when(c == j + 1)
            def _():
                entering[own_pair] = states[j + 1]

    def ret_copy(d, m):
        to = lax.rem(z + d, MEM)
        return pltpu.make_async_remote_copy(
            reply.at[m, to], returned.at[z, m], ret_send.at[d, m], ret_recv.at[d, m],
            device_id={"mem": to}, device_id_type=MESH,
        )

    def send_outputs(m):
        for h in heads:
            p = m * HEADS + h

            @pl.when((c > 0) & (p != own_pair))
            def _():
                pltpu.make_async_remote_copy(
                    states.at[1], entering.at[p], state_send.at[1], state_recv.at[p],
                    device_id={"ctx": owner(m, h)}, device_id_type=MESH,
                ).wait_recv()

        for h in heads:
            at = slice(h * K, (h + 1) * K)
            s = entering[m * HEADS + h]
            heads_out = base[m, :, at] + mm(
                reach[m, :, 2 * h * K : (2 * h + 2) * K], jnp.concatenate([s, s], axis=0)
            )
            scale = lax.rsqrt(jnp.mean(heads_out * heads_out, axis=1, keepdims=True) + 1e-05)
            normed = (heads_out * scale * gain_ref[:, at]).astype(BF16)
            reply[m, :, :, at] = normed.reshape(MEM, CAP, K)
        for d in (2, 1, 3):
            ret_copy(d, m).start()

    @pl.when(c == 0)
    def _():
        entering[...] = jnp.zeros_like(entering)

    turn = jnp.where(own_stage < 2, 0, 1)

    @pl.loop(0, LOCAL - 1)
    def _(m):
        @pl.when((own_stage < LOCAL - 1) & (m == turn))
        def _():
            run_pair()

        local_output(m)

    @pl.loop(0, LOCAL - 1)
    def _(m):
        @pl.when((own_stage == LOCAL - 1) & (m == LOCAL - 2))
        def _():
            run_pair()

        send_outputs(m)

    local_output(LOCAL - 1)
    send_outputs(LOCAL - 1)

    column = jnp.broadcast_to(slots.astype(F32), (128, TOK)).T[:, 0:1].astype(jnp.int32)

    def pick(src, rows):
        chosen = ones_where(iota((TOK, ROWS), 1) + src * ROWS == column)
        return mm(chosen, rows)

    own_rows = jnp.concatenate([reply[m, z] for m in range(LOCAL)], axis=0)
    total = pick(z, own_rows)
    for d in (1, 3, 2):
        src = lax.rem(z + MEM - d, MEM)
        for m in range(LOCAL):
            pltpu.make_async_remote_copy(
                reply.at[m, z], returned.at[src, m], ret_send.at[d, m], ret_recv.at[d, m],
                device_id={"mem": src}, device_id_type=MESH,
            ).wait_recv()
        total = total + pick(src, returned[src].reshape(ROWS, WIDTH))
    picked[...] = total.astype(BF16)
    swap = pltpu.make_async_remote_copy(
        picked.at[aligned(1 - half, TOK // 2)], partner, pair_send.at[1], pair_recv.at[1],
        device_id=other, device_id_type=MESH,
    )
    swap.start()
    wo_load.wait()
    mixed = mm(picked[aligned(half, TOK // 2), :], wo[...])
    w_copy.wait()
    swap.wait()
    out_ref[...] = (mixed + mm(partner[...], w_other[...])).astype(BF16)

    for d in range(1, MEM):
        count_copy(d).wait_send()

    @pl.loop(0, LOCAL)
    def _(m):
        for d in range(1, MEM):
            x_copy(d, m).wait_send()
            ret_copy(d, m).wait_send()
        for d in range(MEM):
            forward(d, m).wait_send()
        for h in heads:

            @pl.when((m * HEADS + h != own_pair) & (c < CTX - 1))
            def _():
                map_copy(m, h).wait_send()

    @pl.loop(1, CTX)
    def _(j):
        @pl.when(c != j)
        def _():
            state_copy(j).wait_send()


def per_device(
    tokens, routes, w_query, w_key, w_value, w_beta, w_decay, decay_rate, norm_gain, w_out
):
    dma = pltpu.SemaphoreType.DMA
    vmem = pltpu.VMEM
    in_vmem = pl.BlockSpec(memory_space=pltpu.VMEM)
    in_place = pl.BlockSpec(memory_space=pl.ANY)
    return pl.pallas_call(
        layer_kernel,
        name="layer",
        out_shape=jax.ShapeDtypeStruct((TOK // 2, D), BF16),
        in_specs=[
            pl.BlockSpec(memory_space=pltpu.SMEM), in_place, in_place, in_place, in_place,
            in_place, in_place, in_place, in_place, in_place,
        ],
        out_specs=in_vmem,
        scratch_shapes=[
            vmem((1, TOK), jnp.int32),
            vmem((LOCAL, HEADS, D), BF16),
            vmem((LOCAL, HEADS, D), BF16),
            vmem((1, WIDTH), F32),
            vmem((TOK, DH), BF16),
            vmem((LOCAL, MEM, CAP, DH), BF16),
            vmem((MEM, 8, 128), F32),
            vmem((MEM, 8, 128), F32),
            vmem((LOCAL, ROWS, D), BF16),
            vmem((D, WIDTH), BF16),
            vmem((LOCAL, D, WIDTH), BF16),
            vmem((LOCAL, D, WIDTH), BF16),
            vmem((16, D), BF16),
            vmem((ROWS, 2 * WIDTH), F32),
            vmem((16, ROWS), F32),
            vmem((LOCAL, ROWS, WIDTH), F32),
            vmem((LOCAL, 16, ROWS), F32),
            vmem((LOCAL, HEADS, ROWS, 2 * K), BF16),
            vmem((LOCAL, HEADS, ROWS, 2 * K), BF16),
            vmem((LOCAL, HEADS, ROWS, 2 * K), BF16),
            vmem((CTX, K, 2 * K), BF16),
            vmem((CTX, K, 2 * K), BF16),
            vmem((CTX, K, K), BF16),
            vmem((CTX, K, K), BF16),
            vmem((LOCAL, ROWS, WIDTH), F32),
            vmem((LOCAL, ROWS, 2 * WIDTH), BF16),
            vmem((LOCAL, MEM, CAP, WIDTH), BF16),
            vmem((MEM, LOCAL, CAP, WIDTH), BF16),
            vmem((TOK, WIDTH), BF16),
            vmem((TOK // 2, WIDTH), BF16),
            vmem((WIDTH, D), BF16),
            vmem((WIDTH, D), BF16),
            dma((7,)), dma((2, LOCAL)), dma((LOCAL,)),
            dma((MEM, LOCAL)), dma((MEM, LOCAL)), dma((MEM,)), dma((MEM,)),
            dma((MEM, LOCAL)), dma((MEM, LOCAL)),
            dma((CTX,)), dma((CTX,)), dma((CTX,)), dma((CTX,)),
            dma((MEM, LOCAL)), dma((MEM, LOCAL)), dma((2,)), dma((2,)),
        ],
        compiler_params=pltpu.CompilerParams(
            collective_id=0, has_side_effects=True, vmem_limit_bytes=67_043_328
        ),
    )(
        decay_rate,
        routes.reshape(1, TOK),
        tokens,
        w_query,
        w_key,
        w_value,
        jnp.swapaxes(w_beta, 1, 2),
        jnp.swapaxes(w_decay, 1, 2),
        norm_gain.reshape(1, WIDTH),
        w_out,
    )


def solution(mesh):
    in_specs = (
        P(("ctx", "mem"), None),
        P(("ctx", "mem"), None),
        P(None, "half"),
        P("mem", None, "half"),
        P("mem", None, "half"),
        P("mem", None, "half"),
        P("mem", None, "half"),
        P("mem", "half"),
        P("half"),
        P("half", None),
    )
    out_specs = P(("ctx", "mem", "half"), None)
    return jax.shard_map(
        per_device, mesh=mesh, in_specs=in_specs, out_specs=out_specs, check_vma=False
    )
```

```python
import jax
import jax.numpy as jnp
from jax import lax
from jax.experimental import pallas as pl
from jax.experimental.pallas import tpu as pltpu
from jax.sharding import PartitionSpec as P

MESH = pl.DeviceIdType.MESH
F32 = jnp.float32
BF16 = jnp.bfloat16
CTX, MEM = 16, 4
TOK = 512
D = 2048
DH = D // 2
CAP = 64
LOCAL = 4
HEADS = 4
ROWS = MEM * CAP
K = 128
WIDTH = HEADS * K


def mm(a, b):
    return jnp.dot(a, b, preferred_element_type=F32)


def mm_nt(a, b):
    return lax.dot_general(a, b, (((1,), (1,)), ((), ())), preferred_element_type=F32)


def split(x):
    hi = x.astype(BF16)
    return hi, (x - hi.astype(F32)).astype(BF16)


def iota(shape, axis):
    return lax.broadcasted_iota(jnp.int32, shape, axis)


def ones_where(mask):
    return mask.astype(F32).astype(BF16)


def aligned(index, size):
    return pl.ds(pl.multiple_of(index * size, size), size)


def unit(x):
    return x * lax.rsqrt(jnp.sum(x * x, axis=1, keepdims=True) + 1e-06)


def level_rows(x, size):
    return jnp.concatenate(
        [x[at + size : at + 2 * size] for at in range(0, x.shape[0], 2 * size)], axis=0
    )


def spread_rows(x, size):
    gap = jnp.zeros((size, x.shape[1]), x.dtype)
    parts = []
    for at in range(0, x.shape[0], size):
        parts += [gap, x[at : at + size]]
    return jnp.concatenate(parts, axis=0)


def unit_lower_inverses(low, inverse, beside):
    beside = list(beside)
    side = low[0].shape[0]
    apart = iota((side, side), 0) ^ iota((side, side), 1)
    size = 2
    while size < side:
        whole = size < 16
        pick = (lambda x: x) if whole else (lambda x: level_rows(x, size))
        put = (lambda x: x) if whole else (lambda x: spread_rows(x, size))
        near = pick(apart)
        here = (near >= size) & (near < 2 * size)
        mid_way = [
            jnp.where(here, mm(pick(a), x), 0.0).astype(BF16) for a, x in zip(low, inverse)
        ]
        if beside:
            beside.pop(0)()
        update = [
            put(mm(pick(x), put(y)).astype(BF16)) for x, y in zip(inverse, mid_way)
        ]
        inverse = [x - u for x, u in zip(inverse, update)]
        size *= 2
    for work in beside:
        work()
    return inverse


def three_pass(a, b):
    a_hi, a_lo = a
    b_hi, b_lo = b
    return mm(
        jnp.concatenate([a_hi, a_lo, a_hi], axis=1), jnp.concatenate([b_hi, b_hi, b_lo], axis=0)
    )


def layer_kernel(
    rate_ref, routes_hbm, tok_ref, wq_ref, wk_ref, wv_ref, wb_hbm, wd_hbm, gain_hbm, wo_ref,
    out_ref,
    routes_ref, wb_ref, wd_ref, gain_ref, tok, outgoing, counts, cnt, xbuf, wq, wk, wv, gates, kv, logits_s, fades, total_ts, keys_s, solved_hi,
    solved_lo, mw, maps, states, entering, base, reach, reply, returned, picked, partner, wo,
    w_other,
    load_sem, wkv_sem, own_sem, x_send, x_recv, c_send, c_recv, f_send, f_recv,
    map_send, map_recv, state_send, state_recv, ret_send, ret_recv, pair_send, pair_recv,
):
    c = lax.axis_index("ctx")
    z = lax.axis_index("mem")
    half = lax.axis_index("half")
    other = {"half": 1 - half}
    mine = aligned(half, DH)
    heads = range(HEADS)
    own_stage = lax.rem(c // 4 + 2 * half, LOCAL)
    own_pair = own_stage * HEADS + lax.rem(c, 4)

    def owner(m, h):
        return lax.rem(m + 2 * half, LOCAL) * 4 + h

    tok_load = pltpu.make_async_copy(tok_ref.at[:, mine], tok, load_sem.at[0])
    routes_load = pltpu.make_async_copy(routes_hbm, routes_ref, load_sem.at[3])
    routes_load.start()
    tok_load.start()
    small_loads = [
        pltpu.make_async_copy(wb_hbm, wb_ref, load_sem.at[4]),
        pltpu.make_async_copy(wd_hbm, wd_ref, load_sem.at[5]),
        pltpu.make_async_copy(gain_hbm, gain_ref, load_sem.at[6]),
    ]
    for load in small_loads:
        load.start()
    barrier = pltpu.get_barrier_semaphore()
    for d in range(1, MEM):
        pl.semaphore_signal(
            barrier, inc=1, device_id={"mem": lax.rem(z + d, MEM)}, device_id_type=MESH
        )
    pl.semaphore_signal(barrier, inc=1, device_id=other, device_id_type=MESH)
    for d in range(1, CTX):
        pl.semaphore_signal(
            barrier, inc=1, device_id={"ctx": lax.rem(c + d, CTX)}, device_id_type=MESH
        )

    def weights(m):
        return (
            pltpu.make_async_copy(wk_ref.at[m], wk.at[m], wkv_sem.at[0, m]),
            pltpu.make_async_copy(wv_ref.at[m], wv.at[m], wkv_sem.at[1, m]),
        )

    routes_load.wait()
    route = routes_ref[...]
    member = (iota((MEM * LOCAL, TOK), 0) == route).astype(F32)
    upper_tok = ones_where(iota((TOK, TOK), 0) <= iota((TOK, TOK), 1))
    place = jnp.sum(mm(member.astype(BF16), upper_tok) * member, axis=0, keepdims=True)
    slots = route * CAP + place.astype(jnp.int32) - 1
    totals = jnp.sum(member, axis=1, keepdims=True)
    counts[...] = jnp.zeros_like(counts)
    for to in range(MEM):
        counts[to, 0:LOCAL, :] = jnp.broadcast_to(
            totals[to * LOCAL : (to + 1) * LOCAL], (LOCAL, 128)
        )
    tok_load.wait()

    def x_copy(d, m):
        to = lax.rem(z + d, MEM)
        return pltpu.make_async_remote_copy(
            outgoing.at[m, to], xbuf.at[m, aligned(z, CAP), mine], x_send.at[d, m],
            x_recv.at[d, m], device_id={"mem": to}, device_id_type=MESH,
        )

    def x_arrival(d, m):
        src = lax.rem(z + MEM - d, MEM)
        return pltpu.make_async_remote_copy(
            outgoing.at[m, z], xbuf.at[m, aligned(src, CAP), mine], x_send.at[d, m],
            x_recv.at[d, m], device_id={"mem": src}, device_id_type=MESH,
        )

    def own_copy(m):
        return pltpu.make_async_copy(
            outgoing.at[m, z], xbuf.at[m, aligned(z, CAP), mine], own_sem.at[m]
        )

    def forward(d, m):
        src = lax.rem(z + MEM - d, MEM)
        landed = xbuf.at[m, aligned(src, CAP), mine]
        return pltpu.make_async_remote_copy(
            landed if d else outgoing.at[m, z], landed, f_send.at[d, m], f_recv.at[d, m],
            device_id=other, device_id_type=MESH,
        )

    def forward_arrival(d, m):
        src = lax.rem(z + MEM - d, MEM)
        landed = xbuf.at[m, aligned(src, CAP), aligned(1 - half, DH)]
        return pltpu.make_async_remote_copy(
            landed, landed, f_send.at[d, m], f_recv.at[d, m],
            device_id=other, device_id_type=MESH,
        )

    def count_copy(d):
        to = lax.rem(z + d, MEM)
        return pltpu.make_async_remote_copy(
            counts.at[to], cnt.at[z], c_send.at[d], c_recv.at[d],
            device_id={"mem": to}, device_id_type=MESH,
        )

    def gather(m):
        at = iota((ROWS, TOK), 0)
        slot = (at // CAP * LOCAL + m) * CAP + at % CAP
        rows = mm(ones_where(slot == slots), tok[...]).astype(BF16)
        outgoing[m] = rows.reshape(MEM, CAP, DH)

    def launch(m):
        for d in (2, 1, 3):
            x_copy(d, m).start()
        forward(0, m).start()
        own_copy(m).start()

    gather(0)
    pl.semaphore_wait(barrier, CTX - 1 + MEM)
    for d in range(1, MEM):
        count_copy(d).start()
    launch(0)
    for copy in weights(0):
        copy.start()
    cnt[z] = counts[z]

    @pl.loop(1, LOCAL)
    def _(m):
        gather(m)
        for copy in weights(m):
            copy.start()

    wq_load = pltpu.make_async_copy(wq_ref, wq, load_sem.at[1])
    wq_load.start()
    wo_load = pltpu.make_async_copy(wo_ref, wo, load_sem.at[2])
    wo_load.start()

    def pass_on(m):
        for d in (1, 3, 2):
            x_arrival(d, m).wait_recv()
            forward(d, m).start()

    for d in range(1, MEM):
        x_copy(d, 0).wait_send()

    @pl.loop(1, LOCAL)
    def _(m):
        launch(m)

    pass_on(0)
    for d in range(1, MEM):
        src = lax.rem(z + MEM - d, MEM)
        pltpu.make_async_remote_copy(
            counts.at[z], cnt.at[src], c_send.at[d], c_recv.at[d],
            device_id={"mem": src}, device_id_type=MESH,
        ).wait_recv()

    def map_copy(m, h):
        p = m * HEADS + h
        return pltpu.make_async_remote_copy(
            mw.at[p], maps.at[c], map_send.at[p], map_recv.at[c],
            device_id={"ctx": owner(m, h)}, device_id_type=MESH,
        )

    gates[...] = jnp.zeros_like(gates)
    for load in small_loads:
        load.wait()
    square = iota((K, K), 0), iota((K, K), 1)

    def lower_times(matrix, right):
        first, below, second = matrix
        return jnp.concatenate(
            [mm(first, right[:K]), mm(jnp.concatenate([below, second], axis=1), right)], axis=0
        )

    def lower_times_exact(matrix, right):
        first, below, second = matrix
        r_hi, r_lo = right
        return jnp.concatenate(
            [
                three_pass(first, (r_hi[:K], r_lo[:K])),
                three_pass(
                    tuple(jnp.concatenate([below[i], second[i]], axis=1) for i in range(2)), right
                ),
            ],
            axis=0,
        )

    def wait_tokens(m):
        for copy in weights(m):
            copy.wait()
        own_copy(m).wait()
        for d in range(MEM):
            forward_arrival(d, m).wait_recv()

    def projections(m):
        def gate_part():
            gates[0:HEADS, :] = wb_ref[m]
            gates[HEADS : 2 * HEADS, :] = wd_ref[m]
            logits_s[...] = mm_nt(gates[...], xbuf[m])

        def part(w, at, to):
            def run():
                kv[:, to : to + 2 * K] = mm(xbuf[m], w[m, :, at : at + 2 * K])

            return run

        return [gate_part] + [
            part(w, at, first + at) for w, first in ((wk, 0), (wv, WIDTH)) for at in (0, 2 * K)
        ]

    def make_maps(m, following):
        if following is not None:
            pass_on(following)
        logits = logits_s[...]
        keys_all = kv[:, :WIDTH]
        values_all = kv[:, WIDTH:]

        lane = iota((1, 128), 1)
        cnt_of = [cnt[src, pl.ds(m, 1), :] for src in range(MEM)]
        cnt_row = jnp.concatenate(
            [
                jnp.where(lane < CAP, cnt_of[0], cnt_of[1]),
                jnp.where(lane < CAP, cnt_of[2], cnt_of[3]),
            ],
            axis=1,
        )
        live = ((iota((1, ROWS), 1) & (CAP - 1)).astype(F32) < cnt_row).astype(F32)
        gate = iota((16, 1), 0)
        rate = jnp.zeros((16, 1), F32)
        for h in heads:
            rate = jnp.where(gate == HEADS + h, rate_ref[m, h], rate)
        strength = jax.nn.sigmoid(logits) * live
        soft = jnp.maximum(logits, 0.0) + jnp.log1p(jnp.exp(-jnp.abs(logits)))
        forget = -rate * soft * live
        upper = ones_where(iota((ROWS, ROWS), 0) <= iota((ROWS, ROWS), 1))
        hi, mid = split(forget)
        low = (forget - hi.astype(F32) - mid.astype(F32)).astype(BF16)
        total_t = mm(hi, upper) + mm(mid, upper) + mm(low, upper)
        both_t = jnp.where(gate < HEADS, strength, total_t)
        total_ts[m] = both_t
        b_hi, b_mid = split(both_t)
        b_low = (both_t - b_hi.astype(F32) - b_mid.astype(F32)).astype(BF16)
        at_gate = iota((48, 2 * WIDTH), 0) & 15
        wide = lax.dot_general(
            jnp.concatenate([b_hi, b_mid, b_low], axis=0),
            ones_where(at_gate == iota((48, 2 * WIDTH), 1) // K),
            (((0,), (0,)), ((), ())),
            preferred_element_type=F32,
        )
        fades[m] = wide[:, WIDTH:]

        keys, corner, target = [None] * HEADS, [None] * HEADS, [None] * HEADS
        blocks, inverse = [None] * (2 * HEADS), [None] * (2 * HEADS)
        strict = square[0] > square[1]
        pair = (square[0] ^ square[1]) == 1
        eye = ones_where(square[0] == square[1])
        for h in heads:
            at = slice(h * K, (h + 1) * K)
            k = unit(keys_all[:, at])
            keys[h] = k
            k_hi, k_lo = split(k)
            keys_s[m, h, :, :K] = k_hi
            keys_s[m, h, :, K:] = k_lo
            gram = mm_nt(
                jnp.concatenate([k_hi, k_lo], axis=1), jnp.concatenate([k_hi, k_hi], axis=1)
            ) + mm_nt(k_hi, k_lo)
            beta = wide[:, at]
            g_col = wide[:, WIDTH + h * K : WIDTH + (h + 1) * K]
            g_row = both_t[HEADS + h : HEADS + h + 1, :]
            for b in range(2):
                part = slice(b * K, (b + 1) * K)
                gap = jnp.minimum(g_col[part] - g_row[:, part], 0.0)
                mix = jnp.where(strict, gram[part, part] * jnp.exp(gap) * beta[part], 0.0)
                blocks[2 * h + b] = split(mix)
                inverse[2 * h + b] = jnp.where(pair, -mix, 0.0).astype(BF16) + eye
            corner[h] = split(gram[K:, :K] * jnp.exp(g_col[K:] - g_row[:, :K]) * beta[K:])
            target[h] = jnp.concatenate(
                [(beta * jnp.exp(g_col)) * k, beta * values_all[:, at]], axis=1
            )
        beside = []
        if following is not None:
            wait_tokens(following)
            beside = projections(following)
        inverse = unit_lower_inverses([b[0] for b in blocks], inverse, beside)
        cross = [mm(corner[h][0], inverse[2 * h]).astype(BF16) for h in heads]
        cross = [mm(inverse[2 * h + 1], cross[h]).astype(BF16) for h in heads]
        inverse = [
            (inverse[2 * h] - eye, -cross[h], inverse[2 * h + 1] - eye) for h in heads
        ]
        shift = [lower_times(inverse[h], target[h].astype(BF16)) for h in heads]
        guess = [target[h] + shift[h] for h in heads]
        rest = [None] * HEADS
        for h in heads:
            mix = (blocks[2 * h], corner[h], blocks[2 * h + 1])
            rest[h] = -(shift[h] + lower_times_exact(mix, split(guess[h])))
        solved = [
            guess[h] + (rest[h] + lower_times(inverse[h], rest[h].astype(BF16))) for h in heads
        ]
        diagonal = square[0] == square[1]
        for h in heads:
            y = split(solved[h])
            solved_hi[m, h], solved_lo[m, h] = y
            g_col = fades[m, :, h * K : (h + 1) * K]
            g_last = g_col[ROWS - 1 : ROWS, :]
            out = three_pass(split((keys[h] * jnp.exp(g_last - g_col)).T), y)
            p = m * HEADS + h
            mw[p, :, :K] = (jnp.where(diagonal, jnp.exp(g_last), 0.0) - out[:, :K]).astype(BF16)
            mw[p, :, K:] = out[:, K:].astype(BF16)
        for h in heads:

            @pl.when((m * HEADS + h != own_pair) & (c < CTX - 1))
            def _():
                map_copy(m, h).start()

    def state_copy(to):
        return pltpu.make_async_remote_copy(
            states.at[to], entering.at[own_pair], state_send.at[to], state_recv.at[own_pair],
            device_id={"ctx": to}, device_id_type=MESH,
        )

    def run_pair():
        maps[c] = mw[own_pair]
        for j in range(CTX - 1):

            @pl.when(c != j)
            def _():
                pltpu.make_async_remote_copy(
                    mw.at[j], maps.at[j], map_send.at[j], map_recv.at[j],
                    device_id={"ctx": j}, device_id_type=MESH,
                ).wait_recv()

        state = maps[0, :, K:].astype(F32)
        states[1] = state.astype(BF16)
        for j in range(1, CTX - 1):
            step = maps[j, :, :K]
            s_hi, s_lo = split(state)
            state = maps[j, :, K:].astype(F32) + mm(
                jnp.concatenate([step, step], axis=1), jnp.concatenate([s_hi, s_lo], axis=0)
            )
            states[j + 1] = state.astype(BF16)

        @pl.loop(1, CTX)
        def _(j):
            @pl.when(c != j)
            def _():
                state_copy(j).start()

        @pl.when(c > 0)
        def _():
            entering[own_pair] = states[c]

    @pl.when(c == 0)
    def _():
        entering[...] = jnp.zeros_like(entering)

    wait_tokens(0)
    for work in projections(0):
        work()

    @pl.loop(0, LOCAL - 1)
    def _(m):
        make_maps(m, m + 1)

    @pl.when(own_stage < 2)
    def _():
        run_pair()

    make_maps(LOCAL - 1, None)

    w_copy = pltpu.make_async_remote_copy(
        wo_ref, w_other, pair_send.at[0], pair_recv.at[0], device_id=other, device_id_type=MESH
    )
    w_copy.start()
    wq_load.wait()

    def local_output(m):
        query_all = mm(xbuf[m], wq[...])
        lower = square[0] >= square[1]
        for h in heads:
            at = slice(h * K, (h + 1) * K)
            q = unit(query_all[:, at])
            q_hi, q_lo = split(q)
            k_hi, k_lo = keys_s[m, h, :, :K], keys_s[m, h, :, K:]
            gram = mm_nt(
                jnp.concatenate([q_hi, q_lo], axis=1), jnp.concatenate([k_hi, k_hi], axis=1)
            ) + mm_nt(q_hi, k_lo)
            g_col = fades[m, :, at]
            g_row = total_ts[m, HEADS + h : HEADS + h + 1, :]
            parts = []
            for b in range(2):
                part = slice(b * K, (b + 1) * K)
                gap = jnp.minimum(g_col[part] - g_row[:, part], 0.0)
                parts.append(split(jnp.where(lower, gram[part, part] * jnp.exp(gap), 0.0)))
            below = split(gram[K:, :K] * jnp.exp(g_col[K:] - g_row[:, :K]))
            out = lower_times_exact(
                (parts[0], below, parts[1]), (solved_hi[m, h], solved_lo[m, h])
            )
            base[m, :, h * K : (h + 1) * K] = out[:, K:]
            r_hi, r_lo = split(q * jnp.exp(g_col) - out[:, :K])
            reach[m, :, 2 * h * K : (2 * h + 1) * K] = r_hi
            reach[m, :, (2 * h + 1) * K : (2 * h + 2) * K] = r_lo

    def ret_copy(d, m):
        to = lax.rem(z + d, MEM)
        return pltpu.make_async_remote_copy(
            reply.at[m, to], returned.at[z, m], ret_send.at[d, m], ret_recv.at[d, m],
            device_id={"mem": to}, device_id_type=MESH,
        )

    def send_outputs(m):
        for h in heads:
            p = m * HEADS + h

            @pl.when((c > 0) & (p != own_pair))
            def _():
                pltpu.make_async_remote_copy(
                    states.at[1], entering.at[p], state_send.at[1], state_recv.at[p],
                    device_id={"ctx": owner(m, h)}, device_id_type=MESH,
                ).wait_recv()

        for h in heads:
            at = slice(h * K, (h + 1) * K)
            s = entering[m * HEADS + h]
            heads_out = base[m, :, at] + mm(
                reach[m, :, 2 * h * K : (2 * h + 2) * K], jnp.concatenate([s, s], axis=0)
            )
            scale = lax.rsqrt(jnp.mean(heads_out * heads_out, axis=1, keepdims=True) + 1e-05)
            normed = (heads_out * scale * gain_ref[:, at]).astype(BF16)
            reply[m, :, :, at] = normed.reshape(MEM, CAP, K)
        for d in (2, 1, 3):
            ret_copy(d, m).start()

    @pl.loop(0, LOCAL)
    def _(m):
        @pl.when((own_stage > 1) & (m == 2 * own_stage - 3))
        def _():
            run_pair()

        local_output(m)
        send_outputs(m)

    column = jnp.broadcast_to(slots.astype(F32), (128, TOK)).T[:, 0:1].astype(jnp.int32)

    def pick(src, rows):
        chosen = ones_where(iota((TOK, ROWS), 1) + src * ROWS == column)
        return mm(chosen, rows)

    own_rows = jnp.concatenate([reply[m, z] for m in range(LOCAL)], axis=0)
    total = pick(z, own_rows)
    for d in (1, 3, 2):
        src = lax.rem(z + MEM - d, MEM)
        for m in range(LOCAL):
            pltpu.make_async_remote_copy(
                reply.at[m, z], returned.at[src, m], ret_send.at[d, m], ret_recv.at[d, m],
                device_id={"mem": src}, device_id_type=MESH,
            ).wait_recv()
        total = total + pick(src, returned[src].reshape(ROWS, WIDTH))
    picked[...] = total.astype(BF16)
    swap = pltpu.make_async_remote_copy(
        picked.at[aligned(1 - half, TOK // 2)], partner, pair_send.at[1], pair_recv.at[1],
        device_id=other, device_id_type=MESH,
    )
    swap.start()
    wo_load.wait()
    mixed = mm(picked[aligned(half, TOK // 2), :], wo[...])
    w_copy.wait()
    swap.wait()
    out_ref[...] = (mixed + mm(partner[...], w_other[...])).astype(BF16)

    for d in range(1, MEM):
        count_copy(d).wait_send()

    @pl.loop(0, LOCAL)
    def _(m):
        for d in range(1, MEM):
            ret_copy(d, m).wait_send()

            @pl.when(m > 0)
            def _():
                x_copy(d, m).wait_send()

        for d in range(MEM):
            forward(d, m).wait_send()
        for h in heads:

            @pl.when((m * HEADS + h != own_pair) & (c < CTX - 1))
            def _():
                map_copy(m, h).wait_send()

    @pl.loop(1, CTX)
    def _(j):
        @pl.when(c != j)
        def _():
            state_copy(j).wait_send()


def per_device(
    tokens, routes, w_query, w_key, w_value, w_beta, w_decay, decay_rate, norm_gain, w_out
):
    dma = pltpu.SemaphoreType.DMA
    vmem = pltpu.VMEM
    in_vmem = pl.BlockSpec(memory_space=pltpu.VMEM)
    in_place = pl.BlockSpec(memory_space=pl.ANY)
    return pl.pallas_call(
        layer_kernel,
        name="layer",
        out_shape=jax.ShapeDtypeStruct((TOK // 2, D), BF16),
        in_specs=[
            pl.BlockSpec(memory_space=pltpu.SMEM), in_place, in_place, in_place, in_place,
            in_place, in_place, in_place, in_place, in_place,
        ],
        out_specs=in_vmem,
        scratch_shapes=[
            vmem((1, TOK), jnp.int32),
            vmem((LOCAL, HEADS, D), BF16),
            vmem((LOCAL, HEADS, D), BF16),
            vmem((1, WIDTH), F32),
            vmem((TOK, DH), BF16),
            vmem((LOCAL, MEM, CAP, DH), BF16),
            vmem((MEM, 8, 128), F32),
            vmem((MEM, 8, 128), F32),
            vmem((LOCAL, ROWS, D), BF16),
            vmem((D, WIDTH), BF16),
            vmem((LOCAL, D, WIDTH), BF16),
            vmem((LOCAL, D, WIDTH), BF16),
            vmem((16, D), BF16),
            vmem((ROWS, 2 * WIDTH), F32),
            vmem((16, ROWS), F32),
            vmem((LOCAL, ROWS, WIDTH), F32),
            vmem((LOCAL, 16, ROWS), F32),
            vmem((LOCAL, HEADS, ROWS, 2 * K), BF16),
            vmem((LOCAL, HEADS, ROWS, 2 * K), BF16),
            vmem((LOCAL, HEADS, ROWS, 2 * K), BF16),
            vmem((CTX, K, 2 * K), BF16),
            vmem((CTX, K, 2 * K), BF16),
            vmem((CTX, K, K), BF16),
            vmem((CTX, K, K), BF16),
            vmem((LOCAL, ROWS, WIDTH), F32),
            vmem((LOCAL, ROWS, 2 * WIDTH), BF16),
            vmem((LOCAL, MEM, CAP, WIDTH), BF16),
            vmem((MEM, LOCAL, CAP, WIDTH), BF16),
            vmem((TOK, WIDTH), BF16),
            vmem((TOK // 2, WIDTH), BF16),
            vmem((WIDTH, D), BF16),
            vmem((WIDTH, D), BF16),
            dma((7,)), dma((2, LOCAL)), dma((LOCAL,)),
            dma((MEM, LOCAL)), dma((MEM, LOCAL)), dma((MEM,)), dma((MEM,)),
            dma((MEM, LOCAL)), dma((MEM, LOCAL)),
            dma((CTX,)), dma((CTX,)), dma((CTX,)), dma((CTX,)),
            dma((MEM, LOCAL)), dma((MEM, LOCAL)), dma((2,)), dma((2,)),
        ],
        compiler_params=pltpu.CompilerParams(
            collective_id=0, has_side_effects=True, vmem_limit_bytes=67_043_328
        ),
    )(
        decay_rate,
        routes.reshape(1, TOK),
        tokens,
        w_query,
        w_key,
        w_value,
        jnp.swapaxes(w_beta, 1, 2),
        jnp.swapaxes(w_decay, 1, 2),
        norm_gain.reshape(1, WIDTH),
        w_out,
    )


def solution(mesh):
    in_specs = (
        P(("ctx", "mem"), None),
        P(("ctx", "mem"), None),
        P(None, "half"),
        P("mem", None, "half"),
        P("mem", None, "half"),
        P("mem", None, "half"),
        P("mem", None, "half"),
        P("mem", "half"),
        P("half"),
        P("half", None),
    )
    out_specs = P(("ctx", "mem", "half"), None)
    return jax.shard_map(
        per_device, mesh=mesh, in_specs=in_specs, out_specs=out_specs, check_vma=False
    )
```

```python
import jax
import jax.numpy as jnp
from jax import lax
from jax.experimental import pallas as pl
from jax.experimental.pallas import tpu as pltpu
from jax.sharding import PartitionSpec as P

MESH = pl.DeviceIdType.MESH
F32 = jnp.float32
BF16 = jnp.bfloat16
CTX, MEM = 16, 4
TOK = 512
D = 2048
DH = D // 2
CAP = 64
LOCAL = 4
HEADS = 4
ROWS = MEM * CAP
K = 128
WIDTH = HEADS * K


def mm(a, b):
    return jnp.dot(a, b, preferred_element_type=F32)


def mm_nt(a, b):
    return lax.dot_general(a, b, (((1,), (1,)), ((), ())), preferred_element_type=F32)


def split(x):
    hi = x.astype(BF16)
    return hi, (x - hi.astype(F32)).astype(BF16)


def iota(shape, axis):
    return lax.broadcasted_iota(jnp.int32, shape, axis)


def ones_where(mask):
    return mask.astype(F32).astype(BF16)


def aligned(index, size):
    return pl.ds(pl.multiple_of(index * size, size), size)


def unit(x):
    return x * lax.rsqrt(jnp.sum(x * x, axis=1, keepdims=True) + 1e-06)


def level_rows(x, size):
    return jnp.concatenate(
        [x[at + size : at + 2 * size] for at in range(0, x.shape[0], 2 * size)], axis=0
    )


def spread_rows(x, size):
    gap = jnp.zeros((size, x.shape[1]), x.dtype)
    parts = []
    for at in range(0, x.shape[0], size):
        parts += [gap, x[at : at + size]]
    return jnp.concatenate(parts, axis=0)


def unit_lower_inverses(low, inverse, beside):
    beside = list(beside)
    side = low[0].shape[0]
    apart = iota((side, side), 0) ^ iota((side, side), 1)
    size = 2
    while size < side:
        whole = size < 16
        pick = (lambda x: x) if whole else (lambda x: level_rows(x, size))
        put = (lambda x: x) if whole else (lambda x: spread_rows(x, size))
        near = pick(apart)
        here = (near >= size) & (near < 2 * size)
        mid_way = [
            jnp.where(here, mm(pick(a), x), 0.0).astype(BF16) for a, x in zip(low, inverse)
        ]
        if beside:
            beside.pop(0)()
        update = [
            put(mm(pick(x), put(y)).astype(BF16)) for x, y in zip(inverse, mid_way)
        ]
        inverse = [x - u for x, u in zip(inverse, update)]
        size *= 2
    for work in beside:
        work()
    return inverse


def three_pass(a, b):
    a_hi, a_lo = a
    b_hi, b_lo = b
    return mm(
        jnp.concatenate([a_hi, a_lo, a_hi], axis=1), jnp.concatenate([b_hi, b_hi, b_lo], axis=0)
    )


def layer_kernel(
    rate_ref, routes_hbm, tok_ref, wq_ref, wk_ref, wv_ref, wb_hbm, wd_hbm, gain_hbm, wo_ref,
    out_ref,
    routes_ref, wb_ref, wd_ref, gain_ref, tok, outgoing, counts, cnt, xbuf, wq, wk, wv, gates, kv, logits_s, fades, total_ts, keys_s, solved_hi,
    solved_lo, mw, maps, states, entering, base, reach, reply, returned, picked, partner, wo,
    w_other,
    load_sem, wkv_sem, own_sem, x_send, x_recv, c_send, c_recv, f_send, f_recv,
    map_send, map_recv, state_send, state_recv, ret_send, ret_recv, pair_send, pair_recv,
):
    c = lax.axis_index("ctx")
    z = lax.axis_index("mem")
    half = lax.axis_index("half")
    other = {"half": 1 - half}
    mine = aligned(half, DH)
    heads = range(HEADS)
    own_stage = lax.rem(c // 4 + 2 * half, LOCAL)
    own_pair = own_stage * HEADS + lax.rem(c, 4)

    def owner(m, h):
        return lax.rem(m + 2 * half, LOCAL) * 4 + h

    tok_load = pltpu.make_async_copy(tok_ref.at[:, mine], tok, load_sem.at[0])
    routes_load = pltpu.make_async_copy(routes_hbm, routes_ref, load_sem.at[3])
    routes_load.start()
    tok_load.start()
    small_loads = [
        pltpu.make_async_copy(wb_hbm, wb_ref, load_sem.at[4]),
        pltpu.make_async_copy(wd_hbm, wd_ref, load_sem.at[5]),
        pltpu.make_async_copy(gain_hbm, gain_ref, load_sem.at[6]),
    ]
    for load in small_loads:
        load.start()
    barrier = pltpu.get_barrier_semaphore()
    for d in range(1, MEM):
        pl.semaphore_signal(
            barrier, inc=1, device_id={"mem": lax.rem(z + d, MEM)}, device_id_type=MESH
        )
    pl.semaphore_signal(barrier, inc=1, device_id=other, device_id_type=MESH)
    for d in range(1, CTX):
        pl.semaphore_signal(
            barrier, inc=1, device_id={"ctx": lax.rem(c + d, CTX)}, device_id_type=MESH
        )

    def weights(m):
        return (
            pltpu.make_async_copy(wk_ref.at[m], wk.at[m], wkv_sem.at[0, m]),
            pltpu.make_async_copy(wv_ref.at[m], wv.at[m], wkv_sem.at[1, m]),
        )

    routes_load.wait()
    route = routes_ref[...]
    member = (iota((MEM * LOCAL, TOK), 0) == route).astype(F32)
    upper_tok = ones_where(iota((TOK, TOK), 0) <= iota((TOK, TOK), 1))
    place = jnp.sum(mm(member.astype(BF16), upper_tok) * member, axis=0, keepdims=True)
    slots = route * CAP + place.astype(jnp.int32) - 1
    totals = jnp.sum(member, axis=1, keepdims=True)
    counts[...] = jnp.zeros_like(counts)
    for to in range(MEM):
        counts[to, 0:LOCAL, :] = jnp.broadcast_to(
            totals[to * LOCAL : (to + 1) * LOCAL], (LOCAL, 128)
        )
    tok_load.wait()

    def x_copy(d, m):
        to = lax.rem(z + d, MEM)
        return pltpu.make_async_remote_copy(
            outgoing.at[m, to], xbuf.at[m, aligned(z, CAP), mine], x_send.at[d, m],
            x_recv.at[d, m], device_id={"mem": to}, device_id_type=MESH,
        )

    def x_arrival(d, m):
        src = lax.rem(z + MEM - d, MEM)
        return pltpu.make_async_remote_copy(
            outgoing.at[m, z], xbuf.at[m, aligned(src, CAP), mine], x_send.at[d, m],
            x_recv.at[d, m], device_id={"mem": src}, device_id_type=MESH,
        )

    def own_copy(m):
        return pltpu.make_async_copy(
            outgoing.at[m, z], xbuf.at[m, aligned(z, CAP), mine], own_sem.at[m]
        )

    def forward(d, m):
        src = lax.rem(z + MEM - d, MEM)
        landed = xbuf.at[m, aligned(src, CAP), mine]
        return pltpu.make_async_remote_copy(
            landed if d else outgoing.at[m, z], landed, f_send.at[d, m], f_recv.at[d, m],
            device_id=other, device_id_type=MESH,
        )

    def forward_arrival(d, m):
        src = lax.rem(z + MEM - d, MEM)
        landed = xbuf.at[m, aligned(src, CAP), aligned(1 - half, DH)]
        return pltpu.make_async_remote_copy(
            landed, landed, f_send.at[d, m], f_recv.at[d, m],
            device_id=other, device_id_type=MESH,
        )

    def count_copy(d):
        to = lax.rem(z + d, MEM)
        return pltpu.make_async_remote_copy(
            counts.at[to], cnt.at[z], c_send.at[d], c_recv.at[d],
            device_id={"mem": to}, device_id_type=MESH,
        )

    def gather(m):
        at = iota((ROWS, TOK), 0)
        slot = (at // CAP * LOCAL + m) * CAP + at % CAP
        rows = mm(ones_where(slot == slots), tok[...]).astype(BF16)
        outgoing[m] = rows.reshape(MEM, CAP, DH)

    def launch(m):
        for d in (2, 1, 3):
            x_copy(d, m).start()
        forward(0, m).start()
        own_copy(m).start()

    gather(0)
    pl.semaphore_wait(barrier, CTX - 1 + MEM)
    for d in range(1, MEM):
        count_copy(d).start()
    launch(0)
    for copy in weights(0):
        copy.start()
    cnt[z] = counts[z]

    @pl.loop(1, LOCAL)
    def _(m):
        gather(m)
        launch(m)
        for copy in weights(m):
            copy.start()

    wq_load = pltpu.make_async_copy(wq_ref, wq, load_sem.at[1])
    wq_load.start()
    wo_load = pltpu.make_async_copy(wo_ref, wo, load_sem.at[2])
    wo_load.start()

    def pass_on(m):
        for d in (1, 3, 2):
            x_arrival(d, m).wait_recv()
            forward(d, m).start()

    pass_on(0)
    for d in range(1, MEM):
        src = lax.rem(z + MEM - d, MEM)
        pltpu.make_async_remote_copy(
            counts.at[z], cnt.at[src], c_send.at[d], c_recv.at[d],
            device_id={"mem": src}, device_id_type=MESH,
        ).wait_recv()

    def map_copy(m, h):
        p = m * HEADS + h
        return pltpu.make_async_remote_copy(
            mw.at[p], maps.at[c], map_send.at[p], map_recv.at[c],
            device_id={"ctx": owner(m, h)}, device_id_type=MESH,
        )

    gates[...] = jnp.zeros_like(gates)
    for load in small_loads:
        load.wait()
    square = iota((K, K), 0), iota((K, K), 1)

    def lower_times(matrix, right):
        first, below, second = matrix
        return jnp.concatenate(
            [mm(first, right[:K]), mm(jnp.concatenate([below, second], axis=1), right)], axis=0
        )

    def lower_times_exact(matrix, right):
        first, below, second = matrix
        r_hi, r_lo = right
        return jnp.concatenate(
            [
                three_pass(first, (r_hi[:K], r_lo[:K])),
                three_pass(
                    tuple(jnp.concatenate([below[i], second[i]], axis=1) for i in range(2)), right
                ),
            ],
            axis=0,
        )

    def wait_tokens(m):
        for copy in weights(m):
            copy.wait()
        own_copy(m).wait()
        for d in range(MEM):
            forward_arrival(d, m).wait_recv()

    def projections(m):
        def gate_part():
            gates[0:HEADS, :] = wb_ref[m]
            gates[HEADS : 2 * HEADS, :] = wd_ref[m]
            logits_s[...] = mm_nt(gates[...], xbuf[m])

        def part(w, at, to):
            def run():
                kv[:, to : to + 2 * K] = mm(xbuf[m], w[m, :, at : at + 2 * K])

            return run

        return [gate_part] + [
            part(w, at, first + at) for w, first in ((wk, 0), (wv, WIDTH)) for at in (0, 2 * K)
        ]

    def make_maps(m, following):
        if following is not None:
            pass_on(following)
        logits = logits_s[...]
        keys_all = kv[:, :WIDTH]
        values_all = kv[:, WIDTH:]

        lane = iota((1, 128), 1)
        cnt_of = [cnt[src, pl.ds(m, 1), :] for src in range(MEM)]
        cnt_row = jnp.concatenate(
            [
                jnp.where(lane < CAP, cnt_of[0], cnt_of[1]),
                jnp.where(lane < CAP, cnt_of[2], cnt_of[3]),
            ],
            axis=1,
        )
        live = ((iota((1, ROWS), 1) & (CAP - 1)).astype(F32) < cnt_row).astype(F32)
        gate = iota((16, 1), 0)
        rate = jnp.zeros((16, 1), F32)
        for h in heads:
            rate = jnp.where(gate == HEADS + h, rate_ref[m, h], rate)
        strength = jax.nn.sigmoid(logits) * live
        soft = jnp.maximum(logits, 0.0) + jnp.log1p(jnp.exp(-jnp.abs(logits)))
        forget = -rate * soft * live
        upper = ones_where(iota((ROWS, ROWS), 0) <= iota((ROWS, ROWS), 1))
        hi, mid = split(forget)
        low = (forget - hi.astype(F32) - mid.astype(F32)).astype(BF16)
        total_t = mm(hi, upper) + mm(mid, upper) + mm(low, upper)
        both_t = jnp.where(gate < HEADS, strength, total_t)
        total_ts[m] = both_t
        b_hi, b_mid = split(both_t)
        b_low = (both_t - b_hi.astype(F32) - b_mid.astype(F32)).astype(BF16)
        at_gate = iota((48, 2 * WIDTH), 0) & 15
        wide = lax.dot_general(
            jnp.concatenate([b_hi, b_mid, b_low], axis=0),
            ones_where(at_gate == iota((48, 2 * WIDTH), 1) // K),
            (((0,), (0,)), ((), ())),
            preferred_element_type=F32,
        )
        fades[m] = wide[:, WIDTH:]

        keys, corner, target = [None] * HEADS, [None] * HEADS, [None] * HEADS
        blocks, inverse = [None] * (2 * HEADS), [None] * (2 * HEADS)
        strict = square[0] > square[1]
        pair = (square[0] ^ square[1]) == 1
        eye = ones_where(square[0] == square[1])
        for h in heads:
            at = slice(h * K, (h + 1) * K)
            k = unit(keys_all[:, at])
            keys[h] = k
            k_hi, k_lo = split(k)
            keys_s[m, h, :, :K] = k_hi
            keys_s[m, h, :, K:] = k_lo
            gram = mm_nt(
                jnp.concatenate([k_hi, k_lo], axis=1), jnp.concatenate([k_hi, k_hi], axis=1)
            ) + mm_nt(k_hi, k_lo)
            beta = wide[:, at]
            g_col = wide[:, WIDTH + h * K : WIDTH + (h + 1) * K]
            g_row = both_t[HEADS + h : HEADS + h + 1, :]
            for b in range(2):
                part = slice(b * K, (b + 1) * K)
                gap = jnp.minimum(g_col[part] - g_row[:, part], 0.0)
                mix = jnp.where(strict, gram[part, part] * jnp.exp(gap) * beta[part], 0.0)
                blocks[2 * h + b] = split(mix)
                inverse[2 * h + b] = jnp.where(pair, -mix, 0.0).astype(BF16) + eye
            corner[h] = split(gram[K:, :K] * jnp.exp(g_col[K:] - g_row[:, :K]) * beta[K:])
            target[h] = jnp.concatenate(
                [(beta * jnp.exp(g_col)) * k, beta * values_all[:, at]], axis=1
            )
        beside = []
        if following is not None:
            wait_tokens(following)
            beside = projections(following)
        inverse = unit_lower_inverses([b[0] for b in blocks], inverse, beside)
        cross = [mm(corner[h][0], inverse[2 * h]).astype(BF16) for h in heads]
        cross = [mm(inverse[2 * h + 1], cross[h]).astype(BF16) for h in heads]
        inverse = [
            (inverse[2 * h] - eye, -cross[h], inverse[2 * h + 1] - eye) for h in heads
        ]
        shift = [lower_times(inverse[h], target[h].astype(BF16)) for h in heads]
        guess = [target[h] + shift[h] for h in heads]
        rest = [None] * HEADS
        for h in heads:
            mix = (blocks[2 * h], corner[h], blocks[2 * h + 1])
            rest[h] = -(shift[h] + lower_times_exact(mix, split(guess[h])))
        solved = [
            guess[h] + (rest[h] + lower_times(inverse[h], rest[h].astype(BF16))) for h in heads
        ]
        diagonal = square[0] == square[1]
        for h in heads:
            y = split(solved[h])
            solved_hi[m, h], solved_lo[m, h] = y
            g_col = fades[m, :, h * K : (h + 1) * K]
            g_last = g_col[ROWS - 1 : ROWS, :]
            out = three_pass(split((keys[h] * jnp.exp(g_last - g_col)).T), y)
            p = m * HEADS + h
            mw[p, :, :K] = (jnp.where(diagonal, jnp.exp(g_last), 0.0) - out[:, :K]).astype(BF16)
            mw[p, :, K:] = out[:, K:].astype(BF16)
        for h in heads:

            @pl.when((m * HEADS + h != own_pair) & (c < CTX - 1))
            def _():
                map_copy(m, h).start()

    def state_copy(to):
        return pltpu.make_async_remote_copy(
            states.at[to], entering.at[own_pair], state_send.at[to], state_recv.at[own_pair],
            device_id={"ctx": to}, device_id_type=MESH,
        )

    def run_pair():
        maps[c] = mw[own_pair]
        for j in range(CTX - 1):

            @pl.when(c != j)
            def _():
                pltpu.make_async_remote_copy(
                    mw.at[j], maps.at[j], map_send.at[j], map_recv.at[j],
                    device_id={"ctx": j}, device_id_type=MESH,
                ).wait_recv()

        pairs = []
        for j in range(0, CTX - 2, 2):
            joined = mm(maps[j + 1, :, :K], maps[j])
            m_hi, m_lo = split(joined[:, :K])
            pairs.append(
                (
                    jnp.concatenate([m_hi, m_lo, m_hi], axis=1),
                    joined[:, K:] + maps[j + 1, :, K:].astype(F32),
                )
            )
        states[1] = maps[0, :, K:]
        state = pairs[0][1]
        even = [state]
        for step, add in pairs[1:]:
            s_hi, s_lo = split(state)
            state = add + mm(step, jnp.concatenate([s_hi, s_hi, s_lo], axis=0))
            even.append(state)
        for n, state in enumerate(even):
            j = 2 * n + 2
            s_hi, s_lo = split(state)
            states[j] = s_hi
            step = maps[j, :, :K]
            states[j + 1] = (
                maps[j, :, K:].astype(F32)
                + mm(
                    jnp.concatenate([step, step], axis=1), jnp.concatenate([s_hi, s_lo], axis=0)
                )
            ).astype(BF16)

        @pl.loop(1, CTX)
        def _(j):
            @pl.when(c != j)
            def _():
                state_copy(j).start()

        @pl.when(c > 0)
        def _():
            entering[own_pair] = states[c]

    @pl.when(c == 0)
    def _():
        entering[...] = jnp.zeros_like(entering)

    wait_tokens(0)
    for work in projections(0):
        work()

    @pl.loop(0, LOCAL - 1)
    def _(m):
        make_maps(m, m + 1)

    @pl.when(own_stage == 0)
    def _():
        run_pair()

    make_maps(LOCAL - 1, None)

    w_copy = pltpu.make_async_remote_copy(
        wo_ref, w_other, pair_send.at[0], pair_recv.at[0], device_id=other, device_id_type=MESH
    )
    w_copy.start()
    wq_load.wait()

    def local_output(m):
        query_all = mm(xbuf[m], wq[...])
        lower = square[0] >= square[1]
        for h in heads:
            at = slice(h * K, (h + 1) * K)
            q = unit(query_all[:, at])
            q_hi, q_lo = split(q)
            k_hi, k_lo = keys_s[m, h, :, :K], keys_s[m, h, :, K:]
            gram = mm_nt(
                jnp.concatenate([q_hi, q_lo], axis=1), jnp.concatenate([k_hi, k_hi], axis=1)
            ) + mm_nt(q_hi, k_lo)
            g_col = fades[m, :, at]
            g_row = total_ts[m, HEADS + h : HEADS + h + 1, :]
            parts = []
            for b in range(2):
                part = slice(b * K, (b + 1) * K)
                gap = jnp.minimum(g_col[part] - g_row[:, part], 0.0)
                parts.append(split(jnp.where(lower, gram[part, part] * jnp.exp(gap), 0.0)))
            below = split(gram[K:, :K] * jnp.exp(g_col[K:] - g_row[:, :K]))
            out = lower_times_exact(
                (parts[0], below, parts[1]), (solved_hi[m, h], solved_lo[m, h])
            )
            base[m, :, h * K : (h + 1) * K] = out[:, K:]
            r_hi, r_lo = split(q * jnp.exp(g_col) - out[:, :K])
            reach[m, :, 2 * h * K : (2 * h + 1) * K] = r_hi
            reach[m, :, (2 * h + 1) * K : (2 * h + 2) * K] = r_lo

    def ret_copy(d, m):
        to = lax.rem(z + d, MEM)
        return pltpu.make_async_remote_copy(
            reply.at[m, to], returned.at[z, m], ret_send.at[d, m], ret_recv.at[d, m],
            device_id={"mem": to}, device_id_type=MESH,
        )

    def send_outputs(m):
        for h in heads:
            p = m * HEADS + h

            @pl.when((c > 0) & (p != own_pair))
            def _():
                pltpu.make_async_remote_copy(
                    states.at[1], entering.at[p], state_send.at[1], state_recv.at[p],
                    device_id={"ctx": owner(m, h)}, device_id_type=MESH,
                ).wait_recv()

        for h in heads:
            at = slice(h * K, (h + 1) * K)
            s = entering[m * HEADS + h]
            heads_out = base[m, :, at] + mm(
                reach[m, :, 2 * h * K : (2 * h + 2) * K], jnp.concatenate([s, s], axis=0)
            )
            scale = lax.rsqrt(jnp.mean(heads_out * heads_out, axis=1, keepdims=True) + 1e-05)
            normed = (heads_out * scale * gain_ref[:, at]).astype(BF16)
            reply[m, :, :, at] = normed.reshape(MEM, CAP, K)
        for d in (2, 1, 3):
            ret_copy(d, m).start()

    @pl.loop(0, LOCAL - 1)
    def _(m):
        @pl.when((m < 2) & (own_stage == m + 1))
        def _():
            run_pair()

        local_output(m)

    send_outputs(0)
    local_output(LOCAL - 1)

    @pl.loop(1, LOCAL)
    def _(m):
        @pl.when((m == 2) & (own_stage == LOCAL - 1))
        def _():
            run_pair()

        send_outputs(m)

    column = jnp.broadcast_to(slots.astype(F32), (128, TOK)).T[:, 0:1].astype(jnp.int32)

    def pick(src, rows):
        chosen = ones_where(iota((TOK, ROWS), 1) + src * ROWS == column)
        return mm(chosen, rows)

    own_rows = jnp.concatenate([reply[m, z] for m in range(LOCAL)], axis=0)
    total = pick(z, own_rows)
    for d in (1, 3, 2):
        src = lax.rem(z + MEM - d, MEM)
        for m in range(LOCAL):
            pltpu.make_async_remote_copy(
                reply.at[m, z], returned.at[src, m], ret_send.at[d, m], ret_recv.at[d, m],
                device_id={"mem": src}, device_id_type=MESH,
            ).wait_recv()
        total = total + pick(src, returned[src].reshape(ROWS, WIDTH))
    picked[...] = total.astype(BF16)
    swap = pltpu.make_async_remote_copy(
        picked.at[aligned(1 - half, TOK // 2)], partner, pair_send.at[1], pair_recv.at[1],
        device_id=other, device_id_type=MESH,
    )
    swap.start()
    wo_load.wait()
    mixed = mm(picked[aligned(half, TOK // 2), :], wo[...])
    w_copy.wait()
    swap.wait()
    out_ref[...] = (mixed + mm(partner[...], w_other[...])).astype(BF16)

    for d in range(1, MEM):
        count_copy(d).wait_send()

    @pl.loop(0, LOCAL)
    def _(m):
        for d in range(1, MEM):
            x_copy(d, m).wait_send()
            ret_copy(d, m).wait_send()
        for d in range(MEM):
            forward(d, m).wait_send()
        for h in heads:

            @pl.when((m * HEADS + h != own_pair) & (c < CTX - 1))
            def _():
                map_copy(m, h).wait_send()

    @pl.loop(1, CTX)
    def _(j):
        @pl.when(c != j)
        def _():
            state_copy(j).wait_send()


def per_device(
    tokens, routes, w_query, w_key, w_value, w_beta, w_decay, decay_rate, norm_gain, w_out
):
    dma = pltpu.SemaphoreType.DMA
    vmem = pltpu.VMEM
    in_vmem = pl.BlockSpec(memory_space=pltpu.VMEM)
    in_place = pl.BlockSpec(memory_space=pl.ANY)
    return pl.pallas_call(
        layer_kernel,
        name="layer",
        out_shape=jax.ShapeDtypeStruct((TOK // 2, D), BF16),
        in_specs=[
            pl.BlockSpec(memory_space=pltpu.SMEM), in_place, in_place, in_place, in_place,
            in_place, in_place, in_place, in_place, in_place,
        ],
        out_specs=in_vmem,
        scratch_shapes=[
            vmem((1, TOK), jnp.int32),
            vmem((LOCAL, HEADS, D), BF16),
            vmem((LOCAL, HEADS, D), BF16),
            vmem((1, WIDTH), F32),
            vmem((TOK, DH), BF16),
            vmem((LOCAL, MEM, CAP, DH), BF16),
            vmem((MEM, 8, 128), F32),
            vmem((MEM, 8, 128), F32),
            vmem((LOCAL, ROWS, D), BF16),
            vmem((D, WIDTH), BF16),
            vmem((LOCAL, D, WIDTH), BF16),
            vmem((LOCAL, D, WIDTH), BF16),
            vmem((16, D), BF16),
            vmem((ROWS, 2 * WIDTH), F32),
            vmem((16, ROWS), F32),
            vmem((LOCAL, ROWS, WIDTH), F32),
            vmem((LOCAL, 16, ROWS), F32),
            vmem((LOCAL, HEADS, ROWS, 2 * K), BF16),
            vmem((LOCAL, HEADS, ROWS, 2 * K), BF16),
            vmem((LOCAL, HEADS, ROWS, 2 * K), BF16),
            vmem((CTX, K, 2 * K), BF16),
            vmem((CTX, K, 2 * K), BF16),
            vmem((CTX, K, K), BF16),
            vmem((CTX, K, K), BF16),
            vmem((LOCAL, ROWS, WIDTH), F32),
            vmem((LOCAL, ROWS, 2 * WIDTH), BF16),
            vmem((LOCAL, MEM, CAP, WIDTH), BF16),
            vmem((MEM, LOCAL, CAP, WIDTH), BF16),
            vmem((TOK, WIDTH), BF16),
            vmem((TOK // 2, WIDTH), BF16),
            vmem((WIDTH, D), BF16),
            vmem((WIDTH, D), BF16),
            dma((7,)), dma((2, LOCAL)), dma((LOCAL,)),
            dma((MEM, LOCAL)), dma((MEM, LOCAL)), dma((MEM,)), dma((MEM,)),
            dma((MEM, LOCAL)), dma((MEM, LOCAL)),
            dma((CTX,)), dma((CTX,)), dma((CTX,)), dma((CTX,)),
            dma((MEM, LOCAL)), dma((MEM, LOCAL)), dma((2,)), dma((2,)),
        ],
        compiler_params=pltpu.CompilerParams(
            collective_id=0, has_side_effects=True, vmem_limit_bytes=67_043_328
        ),
    )(
        decay_rate,
        routes.reshape(1, TOK),
        tokens,
        w_query,
        w_key,
        w_value,
        jnp.swapaxes(w_beta, 1, 2),
        jnp.swapaxes(w_decay, 1, 2),
        norm_gain.reshape(1, WIDTH),
        w_out,
    )


def solution(mesh):
    in_specs = (
        P(("ctx", "mem"), None),
        P(("ctx", "mem"), None),
        P(None, "half"),
        P("mem", None, "half"),
        P("mem", None, "half"),
        P("mem", None, "half"),
        P("mem", None, "half"),
        P("mem", "half"),
        P("half"),
        P("half", None),
    )
    out_specs = P(("ctx", "mem", "half"), None)
    return jax.shard_map(
        per_device, mesh=mesh, in_specs=in_specs, out_specs=out_specs, check_vma=False
    )
```

```python
import jax
import jax.numpy as jnp
from jax import lax
from jax.experimental import pallas as pl
from jax.experimental.pallas import tpu as pltpu
from jax.sharding import PartitionSpec as P

MESH = pl.DeviceIdType.MESH
F32 = jnp.float32
BF16 = jnp.bfloat16
CTX, MEM = 16, 4
TOK = 512
D = 2048
DH = D // 2
CAP = 64
LOCAL = 4
HEADS = 4
ROWS = MEM * CAP
K = 128
WIDTH = HEADS * K


def mm(a, b):
    return jnp.dot(a, b, preferred_element_type=F32)


def mm_nt(a, b):
    return lax.dot_general(a, b, (((1,), (1,)), ((), ())), preferred_element_type=F32)


def split(x):
    hi = x.astype(BF16)
    return hi, (x - hi.astype(F32)).astype(BF16)


def iota(shape, axis):
    return lax.broadcasted_iota(jnp.int32, shape, axis)


def ones_where(mask):
    return mask.astype(F32).astype(BF16)


def aligned(index, size):
    return pl.ds(pl.multiple_of(index * size, size), size)


def unit(x):
    return x * lax.rsqrt(jnp.sum(x * x, axis=1, keepdims=True) + 1e-06)


def level_rows(x, size):
    return jnp.concatenate(
        [x[at + size : at + 2 * size] for at in range(0, x.shape[0], 2 * size)], axis=0
    )


def spread_rows(x, size):
    gap = jnp.zeros((size, x.shape[1]), x.dtype)
    parts = []
    for at in range(0, x.shape[0], size):
        parts += [gap, x[at : at + size]]
    return jnp.concatenate(parts, axis=0)


def unit_lower_inverses(low, inverse, beside):
    beside = list(beside)
    side = low[0].shape[0]
    apart = iota((side, side), 0) ^ iota((side, side), 1)
    size = 2
    while size < side:
        whole = size < 16
        pick = (lambda x: x) if whole else (lambda x: level_rows(x, size))
        put = (lambda x: x) if whole else (lambda x: spread_rows(x, size))
        near = pick(apart)
        here = (near >= size) & (near < 2 * size)
        mid_way = [
            jnp.where(here, mm(pick(a), x), 0.0).astype(BF16) for a, x in zip(low, inverse)
        ]
        if beside:
            beside.pop(0)()
        update = [
            put(mm(pick(x), put(y)).astype(BF16)) for x, y in zip(inverse, mid_way)
        ]
        inverse = [x - u for x, u in zip(inverse, update)]
        size *= 2
    for work in beside:
        work()
    return inverse


def three_pass(a, b):
    a_hi, a_lo = a
    b_hi, b_lo = b
    return mm(
        jnp.concatenate([a_hi, a_lo, a_hi], axis=1), jnp.concatenate([b_hi, b_hi, b_lo], axis=0)
    )


def layer_kernel(
    rate_ref, routes_hbm, tok_ref, wq_ref, wk_ref, wv_ref, wb_hbm, wd_hbm, gain_hbm, wo_ref,
    out_ref,
    routes_ref, wb_ref, wd_ref, gain_ref, tok, outgoing, counts, cnt, xbuf, wq, wk, wv, gates, kv, logits_s, fades, total_ts, keys_s, solved_hi,
    solved_lo, mw, maps, states, entering, base, reach, reply, returned, picked, partner, wo,
    w_other,
    load_sem, wkv_sem, own_sem, x_send, x_recv, c_send, c_recv, f_send, f_recv,
    map_send, map_recv, state_send, state_recv, ret_send, ret_recv, pair_send, pair_recv,
):
    c = lax.axis_index("ctx")
    z = lax.axis_index("mem")
    half = lax.axis_index("half")
    other = {"half": 1 - half}
    mine = aligned(half, DH)
    heads = range(HEADS)
    own_stage = lax.rem(c // 4 + 2 * half, LOCAL)
    own_pair = own_stage * HEADS + lax.rem(c, 4)

    def owner(m, h):
        return lax.rem(m + 2 * half, LOCAL) * 4 + h

    tok_load = pltpu.make_async_copy(tok_ref.at[:, mine], tok, load_sem.at[0])
    routes_load = pltpu.make_async_copy(routes_hbm, routes_ref, load_sem.at[3])
    routes_load.start()
    tok_load.start()
    small_loads = [
        pltpu.make_async_copy(wb_hbm, wb_ref, load_sem.at[4]),
        pltpu.make_async_copy(wd_hbm, wd_ref, load_sem.at[5]),
        pltpu.make_async_copy(gain_hbm, gain_ref, load_sem.at[6]),
    ]
    for load in small_loads:
        load.start()
    barrier = pltpu.get_barrier_semaphore()
    for d in range(1, MEM):
        pl.semaphore_signal(
            barrier, inc=1, device_id={"mem": lax.rem(z + d, MEM)}, device_id_type=MESH
        )
    pl.semaphore_signal(barrier, inc=1, device_id=other, device_id_type=MESH)
    for d in range(1, CTX):
        pl.semaphore_signal(
            barrier, inc=1, device_id={"ctx": lax.rem(c + d, CTX)}, device_id_type=MESH
        )

    def weights(m):
        return (
            pltpu.make_async_copy(wk_ref.at[m], wk.at[m], wkv_sem.at[0, m]),
            pltpu.make_async_copy(wv_ref.at[m], wv.at[m], wkv_sem.at[1, m]),
        )

    routes_load.wait()
    route = routes_ref[...]
    member = (iota((MEM * LOCAL, TOK), 0) == route).astype(F32)
    upper_tok = ones_where(iota((TOK, TOK), 0) <= iota((TOK, TOK), 1))
    place = jnp.sum(mm(member.astype(BF16), upper_tok) * member, axis=0, keepdims=True)
    slots = route * CAP + place.astype(jnp.int32) - 1
    totals = jnp.sum(member, axis=1, keepdims=True)
    counts[...] = jnp.zeros_like(counts)
    for to in range(MEM):
        counts[to, 0:LOCAL, :] = jnp.broadcast_to(
            totals[to * LOCAL : (to + 1) * LOCAL], (LOCAL, 128)
        )
    tok_load.wait()

    def x_copy(d, m):
        to = lax.rem(z + d, MEM)
        return pltpu.make_async_remote_copy(
            outgoing.at[m, to], xbuf.at[m, aligned(z, CAP), mine], x_send.at[d, m],
            x_recv.at[d, m], device_id={"mem": to}, device_id_type=MESH,
        )

    def x_arrival(d, m):
        src = lax.rem(z + MEM - d, MEM)
        return pltpu.make_async_remote_copy(
            outgoing.at[m, z], xbuf.at[m, aligned(src, CAP), mine], x_send.at[d, m],
            x_recv.at[d, m], device_id={"mem": src}, device_id_type=MESH,
        )

    def own_copy(m):
        return pltpu.make_async_copy(
            outgoing.at[m, z], xbuf.at[m, aligned(z, CAP), mine], own_sem.at[m]
        )

    def forward(d, m):
        src = lax.rem(z + MEM - d, MEM)
        landed = xbuf.at[m, aligned(src, CAP), mine]
        return pltpu.make_async_remote_copy(
            landed if d else outgoing.at[m, z], landed, f_send.at[d, m], f_recv.at[d, m],
            device_id=other, device_id_type=MESH,
        )

    def forward_arrival(d, m):
        src = lax.rem(z + MEM - d, MEM)
        landed = xbuf.at[m, aligned(src, CAP), aligned(1 - half, DH)]
        return pltpu.make_async_remote_copy(
            landed, landed, f_send.at[d, m], f_recv.at[d, m],
            device_id=other, device_id_type=MESH,
        )

    def count_copy(d):
        to = lax.rem(z + d, MEM)
        return pltpu.make_async_remote_copy(
            counts.at[to], cnt.at[z], c_send.at[d], c_recv.at[d],
            device_id={"mem": to}, device_id_type=MESH,
        )

    def gather(m):
        at = iota((ROWS, TOK), 0)
        slot = (at // CAP * LOCAL + m) * CAP + at % CAP
        rows = mm(ones_where(slot == slots), tok[...]).astype(BF16)
        outgoing[m] = rows.reshape(MEM, CAP, DH)

    def launch(m):
        for d in (2, 1, 3):
            x_copy(d, m).start()
        forward(0, m).start()
        own_copy(m).start()

    gather(0)
    pl.semaphore_wait(barrier, CTX - 1 + MEM)
    for d in range(1, MEM):
        count_copy(d).start()
    launch(0)
    for copy in weights(0):
        copy.start()
    cnt[z] = counts[z]

    @pl.loop(1, LOCAL)
    def _(m):
        gather(m)
        launch(m)
        for copy in weights(m):
            copy.start()

    wq_load = pltpu.make_async_copy(wq_ref, wq, load_sem.at[1])
    wq_load.start()
    wo_load = pltpu.make_async_copy(wo_ref, wo, load_sem.at[2])
    wo_load.start()

    def pass_on(m):
        for d in (1, 3, 2):
            x_arrival(d, m).wait_recv()
            forward(d, m).start()

    pass_on(0)
    for d in range(1, MEM):
        src = lax.rem(z + MEM - d, MEM)
        pltpu.make_async_remote_copy(
            counts.at[z], cnt.at[src], c_send.at[d], c_recv.at[d],
            device_id={"mem": src}, device_id_type=MESH,
        ).wait_recv()

    def map_copy(m, h):
        p = m * HEADS + h
        return pltpu.make_async_remote_copy(
            mw.at[p], maps.at[c], map_send.at[p], map_recv.at[c],
            device_id={"ctx": owner(m, h)}, device_id_type=MESH,
        )

    gates[...] = jnp.zeros_like(gates)
    for load in small_loads:
        load.wait()
    square = iota((K, K), 0), iota((K, K), 1)

    def lower_times(matrix, right):
        first, below, second = matrix
        return jnp.concatenate(
            [mm(first, right[:K]), mm(jnp.concatenate([below, second], axis=1), right)], axis=0
        )

    def lower_times_exact(matrix, right):
        first, below, second = matrix
        r_hi, r_lo = right
        return jnp.concatenate(
            [
                three_pass(first, (r_hi[:K], r_lo[:K])),
                three_pass(
                    tuple(jnp.concatenate([below[i], second[i]], axis=1) for i in range(2)), right
                ),
            ],
            axis=0,
        )

    def wait_tokens(m):
        for copy in weights(m):
            copy.wait()
        own_copy(m).wait()
        for d in range(MEM):
            forward_arrival(d, m).wait_recv()

    def projections(m):
        def gate_part():
            gates[0:HEADS, :] = wb_ref[m]
            gates[HEADS : 2 * HEADS, :] = wd_ref[m]
            logits_s[...] = mm_nt(gates[...], xbuf[m])

        def part(w, at, to):
            def run():
                kv[:, to : to + 2 * K] = mm(xbuf[m], w[m, :, at : at + 2 * K])

            return run

        return [gate_part] + [
            part(w, at, first + at) for w, first in ((wk, 0), (wv, WIDTH)) for at in (0, 2 * K)
        ]

    def make_maps(m, following):
        if following is not None:
            pass_on(following)
        logits = logits_s[...]
        keys_all = kv[:, :WIDTH]
        values_all = kv[:, WIDTH:]

        lane = iota((1, 128), 1)
        cnt_of = [cnt[src, pl.ds(m, 1), :] for src in range(MEM)]
        cnt_row = jnp.concatenate(
            [
                jnp.where(lane < CAP, cnt_of[0], cnt_of[1]),
                jnp.where(lane < CAP, cnt_of[2], cnt_of[3]),
            ],
            axis=1,
        )
        live = ((iota((1, ROWS), 1) & (CAP - 1)).astype(F32) < cnt_row).astype(F32)
        gate = iota((16, 1), 0)
        rate = jnp.zeros((16, 1), F32)
        for h in heads:
            rate = jnp.where(gate == HEADS + h, rate_ref[m, h], rate)
        strength = jax.nn.sigmoid(logits) * live
        soft = jnp.maximum(logits, 0.0) + jnp.log1p(jnp.exp(-jnp.abs(logits)))
        forget = -rate * soft * live
        upper = ones_where(iota((ROWS, ROWS), 0) <= iota((ROWS, ROWS), 1))
        hi, mid = split(forget)
        low = (forget - hi.astype(F32) - mid.astype(F32)).astype(BF16)
        total_t = mm(hi, upper) + mm(mid, upper) + mm(low, upper)
        both_t = jnp.where(gate < HEADS, strength, total_t)
        total_ts[m] = both_t
        b_hi, b_mid = split(both_t)
        b_low = (both_t - b_hi.astype(F32) - b_mid.astype(F32)).astype(BF16)
        at_gate = iota((48, 2 * WIDTH), 0) & 15
        wide = lax.dot_general(
            jnp.concatenate([b_hi, b_mid, b_low], axis=0),
            ones_where(at_gate == iota((48, 2 * WIDTH), 1) // K),
            (((0,), (0,)), ((), ())),
            preferred_element_type=F32,
        )
        fades[m] = wide[:, WIDTH:]

        keys, corner, target = [None] * HEADS, [None] * HEADS, [None] * HEADS
        blocks, inverse = [None] * (2 * HEADS), [None] * (2 * HEADS)
        strict = square[0] > square[1]
        pair = (square[0] ^ square[1]) == 1
        eye = ones_where(square[0] == square[1])
        for h in heads:
            at = slice(h * K, (h + 1) * K)
            k = unit(keys_all[:, at])
            keys[h] = k
            k_hi, k_lo = split(k)
            keys_s[m, h, :, :K] = k_hi
            keys_s[m, h, :, K:] = k_lo
            gram = mm_nt(
                jnp.concatenate([k_hi, k_lo], axis=1), jnp.concatenate([k_hi, k_hi], axis=1)
            ) + mm_nt(k_hi, k_lo)
            beta = wide[:, at]
            g_col = wide[:, WIDTH + h * K : WIDTH + (h + 1) * K]
            g_row = both_t[HEADS + h : HEADS + h + 1, :]
            for b in range(2):
                part = slice(b * K, (b + 1) * K)
                gap = jnp.minimum(g_col[part] - g_row[:, part], 0.0)
                mix = jnp.where(strict, gram[part, part] * jnp.exp(gap) * beta[part], 0.0)
                blocks[2 * h + b] = split(mix)
                inverse[2 * h + b] = jnp.where(pair, -mix, 0.0).astype(BF16) + eye
            corner[h] = split(gram[K:, :K] * jnp.exp(g_col[K:] - g_row[:, :K]) * beta[K:])
            target[h] = jnp.concatenate(
                [(beta * jnp.exp(g_col)) * k, beta * values_all[:, at]], axis=1
            )
        beside = []
        if following is not None:
            wait_tokens(following)
            beside = projections(following)
        inverse = unit_lower_inverses([b[0] for b in blocks], inverse, beside)
        cross = [mm(corner[h][0], inverse[2 * h]).astype(BF16) for h in heads]
        cross = [mm(inverse[2 * h + 1], cross[h]).astype(BF16) for h in heads]
        inverse = [
            (inverse[2 * h] - eye, -cross[h], inverse[2 * h + 1] - eye) for h in heads
        ]
        shift = [lower_times(inverse[h], target[h].astype(BF16)) for h in heads]
        guess = [target[h] + shift[h] for h in heads]
        rest = [None] * HEADS
        for h in heads:
            mix = (blocks[2 * h], corner[h], blocks[2 * h + 1])
            rest[h] = -(shift[h] + lower_times_exact(mix, split(guess[h])))
        solved = [
            guess[h] + (rest[h] + lower_times(inverse[h], rest[h].astype(BF16))) for h in heads
        ]
        diagonal = square[0] == square[1]
        for h in heads:
            y = split(solved[h])
            solved_hi[m, h], solved_lo[m, h] = y
            g_col = fades[m, :, h * K : (h + 1) * K]
            g_last = g_col[ROWS - 1 : ROWS, :]
            out = three_pass(split((keys[h] * jnp.exp(g_last - g_col)).T), y)
            p = m * HEADS + h
            mw[p, :, :K] = (jnp.where(diagonal, jnp.exp(g_last), 0.0) - out[:, :K]).astype(BF16)
            mw[p, :, K:] = out[:, K:].astype(BF16)
        for turn in heads:
            h = lax.rem(c + turn, HEADS)

            @pl.when((m * HEADS + h != own_pair) & (c < CTX - 1))
            def _():
                map_copy(m, h).start()

    def state_copy(to):
        return pltpu.make_async_remote_copy(
            states.at[to], entering.at[own_pair], state_send.at[to], state_recv.at[own_pair],
            device_id={"ctx": to}, device_id_type=MESH,
        )

    def run_pair():
        maps[c] = mw[own_pair]
        for j in range(CTX - 1):

            @pl.when(c != j)
            def _():
                pltpu.make_async_remote_copy(
                    mw.at[j], maps.at[j], map_send.at[j], map_recv.at[j],
                    device_id={"ctx": j}, device_id_type=MESH,
                ).wait_recv()

        pairs = []
        for j in range(0, CTX - 2, 2):
            joined = mm(maps[j + 1, :, :K], maps[j])
            m_hi, m_lo = split(joined[:, :K])
            pairs.append(
                (
                    jnp.concatenate([m_hi, m_lo, m_hi], axis=1),
                    joined[:, K:] + maps[j + 1, :, K:].astype(F32),
                )
            )
        states[1] = maps[0, :, K:]
        state = pairs[0][1]
        even = [state]
        for step, add in pairs[1:]:
            s_hi, s_lo = split(state)
            state = add + mm(step, jnp.concatenate([s_hi, s_hi, s_lo], axis=0))
            even.append(state)
        for n, state in enumerate(even):
            j = 2 * n + 2
            s_hi, s_lo = split(state)
            states[j] = s_hi
            step = maps[j, :, :K]
            states[j + 1] = (
                maps[j, :, K:].astype(F32)
                + mm(
                    jnp.concatenate([step, step], axis=1), jnp.concatenate([s_hi, s_lo], axis=0)
                )
            ).astype(BF16)

        @pl.loop(1, CTX)
        def _(turn):
            to = lax.rem(c + turn, CTX)

            @pl.when(to > 0)
            def _():
                state_copy(to).start()

        @pl.when(c > 0)
        def _():
            entering[own_pair] = states[c]

    @pl.when(c == 0)
    def _():
        entering[...] = jnp.zeros_like(entering)

    wait_tokens(0)
    for work in projections(0):
        work()

    @pl.loop(0, LOCAL - 1)
    def _(m):
        make_maps(m, m + 1)

    @pl.when(own_stage == 0)
    def _():
        run_pair()

    make_maps(LOCAL - 1, None)

    w_copy = pltpu.make_async_remote_copy(
        wo_ref, w_other, pair_send.at[0], pair_recv.at[0], device_id=other, device_id_type=MESH
    )
    w_copy.start()
    wq_load.wait()

    def local_output(m):
        query_all = mm(xbuf[m], wq[...])
        lower = square[0] >= square[1]
        for h in heads:
            at = slice(h * K, (h + 1) * K)
            q = unit(query_all[:, at])
            q_hi, q_lo = split(q)
            k_hi, k_lo = keys_s[m, h, :, :K], keys_s[m, h, :, K:]
            gram = mm_nt(
                jnp.concatenate([q_hi, q_lo], axis=1), jnp.concatenate([k_hi, k_hi], axis=1)
            ) + mm_nt(q_hi, k_lo)
            g_col = fades[m, :, at]
            g_row = total_ts[m, HEADS + h : HEADS + h + 1, :]
            parts = []
            for b in range(2):
                part = slice(b * K, (b + 1) * K)
                gap = jnp.minimum(g_col[part] - g_row[:, part], 0.0)
                parts.append(split(jnp.where(lower, gram[part, part] * jnp.exp(gap), 0.0)))
            below = split(gram[K:, :K] * jnp.exp(g_col[K:] - g_row[:, :K]))
            out = lower_times_exact(
                (parts[0], below, parts[1]), (solved_hi[m, h], solved_lo[m, h])
            )
            base[m, :, h * K : (h + 1) * K] = out[:, K:]
            r_hi, r_lo = split(q * jnp.exp(g_col) - out[:, :K])
            reach[m, :, 2 * h * K : (2 * h + 1) * K] = r_hi
            reach[m, :, (2 * h + 1) * K : (2 * h + 2) * K] = r_lo

    def ret_copy(d, m):
        to = lax.rem(z + d, MEM)
        return pltpu.make_async_remote_copy(
            reply.at[m, to], returned.at[z, m], ret_send.at[d, m], ret_recv.at[d, m],
            device_id={"mem": to}, device_id_type=MESH,
        )

    def send_outputs(m):
        for h in heads:
            p = m * HEADS + h

            @pl.when((c > 0) & (p != own_pair))
            def _():
                pltpu.make_async_remote_copy(
                    states.at[1], entering.at[p], state_send.at[1], state_recv.at[p],
                    device_id={"ctx": owner(m, h)}, device_id_type=MESH,
                ).wait_recv()

        for h in heads:
            at = slice(h * K, (h + 1) * K)
            s = entering[m * HEADS + h]
            heads_out = base[m, :, at] + mm(
                reach[m, :, 2 * h * K : (2 * h + 2) * K], jnp.concatenate([s, s], axis=0)
            )
            scale = lax.rsqrt(jnp.mean(heads_out * heads_out, axis=1, keepdims=True) + 1e-05)
            normed = (heads_out * scale * gain_ref[:, at]).astype(BF16)
            reply[m, :, :, at] = normed.reshape(MEM, CAP, K)
        for d in (2, 1, 3):
            ret_copy(d, m).start()

    @pl.loop(0, LOCAL - 1)
    def _(m):
        @pl.when((m < 2) & (own_stage == m + 1))
        def _():
            run_pair()

        local_output(m)

    send_outputs(0)
    local_output(LOCAL - 1)

    @pl.loop(1, LOCAL)
    def _(m):
        @pl.when((m == 2) & (own_stage == LOCAL - 1))
        def _():
            run_pair()

        send_outputs(m)

    column = jnp.broadcast_to(slots.astype(F32), (128, TOK)).T[:, 0:1].astype(jnp.int32)

    def pick(src, rows):
        chosen = ones_where(iota((TOK, ROWS), 1) + src * ROWS == column)
        return mm(chosen, rows)

    own_rows = jnp.concatenate([reply[m, z] for m in range(LOCAL)], axis=0)
    total = pick(z, own_rows)
    for d in (1, 3, 2):
        src = lax.rem(z + MEM - d, MEM)
        for m in range(LOCAL):
            pltpu.make_async_remote_copy(
                reply.at[m, z], returned.at[src, m], ret_send.at[d, m], ret_recv.at[d, m],
                device_id={"mem": src}, device_id_type=MESH,
            ).wait_recv()
        total = total + pick(src, returned[src].reshape(ROWS, WIDTH))
    picked[...] = total.astype(BF16)
    swap = pltpu.make_async_remote_copy(
        picked.at[aligned(1 - half, TOK // 2)], partner, pair_send.at[1], pair_recv.at[1],
        device_id=other, device_id_type=MESH,
    )
    swap.start()
    wo_load.wait()
    mixed = mm(picked[aligned(half, TOK // 2), :], wo[...])
    w_copy.wait()
    swap.wait()
    out_ref[...] = (mixed + mm(partner[...], w_other[...])).astype(BF16)

    for d in range(1, MEM):
        count_copy(d).wait_send()

    @pl.loop(0, LOCAL)
    def _(m):
        for d in range(1, MEM):
            x_copy(d, m).wait_send()
            ret_copy(d, m).wait_send()
        for d in range(MEM):
            forward(d, m).wait_send()
        for h in heads:

            @pl.when((m * HEADS + h != own_pair) & (c < CTX - 1))
            def _():
                map_copy(m, h).wait_send()

    @pl.loop(1, CTX)
    def _(j):
        @pl.when(c != j)
        def _():
            state_copy(j).wait_send()


def hand_over(mixed_ref, out_ref):
    out_ref[...] = mixed_ref[...]


def per_device(
    tokens, routes, w_query, w_key, w_value, w_beta, w_decay, decay_rate, norm_gain, w_out
):
    dma = pltpu.SemaphoreType.DMA
    vmem = pltpu.VMEM
    in_vmem = pl.BlockSpec(memory_space=pltpu.VMEM)
    in_place = pl.BlockSpec(memory_space=pl.ANY)
    mixed = pl.pallas_call(
        layer_kernel,
        name="layer",
        out_shape=jax.ShapeDtypeStruct((TOK // 2, D), BF16),
        in_specs=[
            pl.BlockSpec(memory_space=pltpu.SMEM), in_place, in_place, in_place, in_place,
            in_place, in_place, in_place, in_place, in_place,
        ],
        out_specs=in_vmem,
        scratch_shapes=[
            vmem((1, TOK), jnp.int32),
            vmem((LOCAL, HEADS, D), BF16),
            vmem((LOCAL, HEADS, D), BF16),
            vmem((1, WIDTH), F32),
            vmem((TOK, DH), BF16),
            vmem((LOCAL, MEM, CAP, DH), BF16),
            vmem((MEM, 8, 128), F32),
            vmem((MEM, 8, 128), F32),
            vmem((LOCAL, ROWS, D), BF16),
            vmem((D, WIDTH), BF16),
            vmem((LOCAL, D, WIDTH), BF16),
            vmem((LOCAL, D, WIDTH), BF16),
            vmem((16, D), BF16),
            vmem((ROWS, 2 * WIDTH), F32),
            vmem((16, ROWS), F32),
            vmem((LOCAL, ROWS, WIDTH), F32),
            vmem((LOCAL, 16, ROWS), F32),
            vmem((LOCAL, HEADS, ROWS, 2 * K), BF16),
            vmem((LOCAL, HEADS, ROWS, 2 * K), BF16),
            vmem((LOCAL, HEADS, ROWS, 2 * K), BF16),
            vmem((CTX, K, 2 * K), BF16),
            vmem((CTX, K, 2 * K), BF16),
            vmem((CTX, K, K), BF16),
            vmem((CTX, K, K), BF16),
            vmem((LOCAL, ROWS, WIDTH), F32),
            vmem((LOCAL, ROWS, 2 * WIDTH), BF16),
            vmem((LOCAL, MEM, CAP, WIDTH), BF16),
            vmem((MEM, LOCAL, CAP, WIDTH), BF16),
            vmem((TOK, WIDTH), BF16),
            vmem((TOK // 2, WIDTH), BF16),
            vmem((WIDTH, D), BF16),
            vmem((WIDTH, D), BF16),
            dma((7,)), dma((2, LOCAL)), dma((LOCAL,)),
            dma((MEM, LOCAL)), dma((MEM, LOCAL)), dma((MEM,)), dma((MEM,)),
            dma((MEM, LOCAL)), dma((MEM, LOCAL)),
            dma((CTX,)), dma((CTX,)), dma((CTX,)), dma((CTX,)),
            dma((MEM, LOCAL)), dma((MEM, LOCAL)), dma((2,)), dma((2,)),
        ],
        compiler_params=pltpu.CompilerParams(
            collective_id=0, has_side_effects=True, vmem_limit_bytes=67_043_328
        ),
    )(
        decay_rate,
        routes.reshape(1, TOK),
        tokens,
        w_query,
        w_key,
        w_value,
        jnp.swapaxes(w_beta, 1, 2),
        jnp.swapaxes(w_decay, 1, 2),
        norm_gain.reshape(1, WIDTH),
        w_out,
    )
    rows = pl.BlockSpec((TOK // 8, D), lambda i: (i, 0))
    return pl.pallas_call(
        hand_over,
        name="hand_over",
        grid=(4,),
        out_shape=jax.ShapeDtypeStruct((TOK // 2, D), BF16),
        in_specs=[rows],
        out_specs=rows,
    )(mixed)


def solution(mesh):
    in_specs = (
        P(("ctx", "mem"), None),
        P(("ctx", "mem"), None),
        P(None, "half"),
        P("mem", None, "half"),
        P("mem", None, "half"),
        P("mem", None, "half"),
        P("mem", None, "half"),
        P("mem", "half"),
        P("half"),
        P("half", None),
    )
    out_specs = P(("ctx", "mem", "half"), None)
    return jax.shard_map(
        per_device, mesh=mesh, in_specs=in_specs, out_specs=out_specs, check_vma=False
    )
```

```python
import jax
import jax.numpy as jnp
from jax import lax
from jax.experimental import pallas as pl
from jax.experimental.pallas import tpu as pltpu
from jax.sharding import PartitionSpec as P

MESH = pl.DeviceIdType.MESH
F32 = jnp.float32
BF16 = jnp.bfloat16
CTX, MEM = 16, 4
TOK = 512
D = 2048
DH = D // 2
CAP = 64
LOCAL = 4
HEADS = 4
ROWS = MEM * CAP
K = 128
WIDTH = HEADS * K


def mm(a, b):
    return jnp.dot(a, b, preferred_element_type=F32)


def mm_nt(a, b):
    return lax.dot_general(a, b, (((1,), (1,)), ((), ())), preferred_element_type=F32)


def split(x):
    hi = x.astype(BF16)
    return hi, (x - hi.astype(F32)).astype(BF16)


def iota(shape, axis):
    return lax.broadcasted_iota(jnp.int32, shape, axis)


def ones_where(mask):
    return mask.astype(F32).astype(BF16)


def aligned(index, size):
    return pl.ds(pl.multiple_of(index * size, size), size)


def unit(x):
    return x * lax.rsqrt(jnp.sum(x * x, axis=1, keepdims=True) + 1e-06)


def level_rows(x, size):
    return jnp.concatenate(
        [x[at + size : at + 2 * size] for at in range(0, x.shape[0], 2 * size)], axis=0
    )


def spread_rows(x, size):
    gap = jnp.zeros((size, x.shape[1]), x.dtype)
    parts = []
    for at in range(0, x.shape[0], size):
        parts += [gap, x[at : at + size]]
    return jnp.concatenate(parts, axis=0)


def unit_lower_inverses(low, inverse, beside):
    beside = list(beside)
    side = low[0].shape[0]
    apart = iota((side, side), 0) ^ iota((side, side), 1)
    size = 2
    while size < side:
        whole = size < 16
        pick = (lambda x: x) if whole else (lambda x: level_rows(x, size))
        put = (lambda x: x) if whole else (lambda x: spread_rows(x, size))
        near = pick(apart)
        here = (near >= size) & (near < 2 * size)
        mid_way = [
            jnp.where(here, mm(pick(a), x), 0.0).astype(BF16) for a, x in zip(low, inverse)
        ]
        if beside:
            beside.pop(0)()
        update = [
            put(mm(pick(x), put(y)).astype(BF16)) for x, y in zip(inverse, mid_way)
        ]
        inverse = [x - u for x, u in zip(inverse, update)]
        size *= 2
    for work in beside:
        work()
    return inverse


def three_pass(a, b):
    a_hi, a_lo = a
    b_hi, b_lo = b
    return mm(
        jnp.concatenate([a_hi, a_lo, a_hi], axis=1), jnp.concatenate([b_hi, b_hi, b_lo], axis=0)
    )


def layer_kernel(
    rate_ref, routes_hbm, tok_ref, wq_ref, wk_ref, wv_ref, wb_hbm, wd_hbm, gain_hbm, wo_ref,
    out_ref,
    routes_ref, wb_ref, wd_ref, gain_ref, tok, outgoing, counts, cnt, xbuf, wq, wk, wv, gates, kv, logits_s, fades, total_ts, keys_s, solved_hi,
    solved_lo, mw, maps, states, entering, base, reach, reply, returned, picked, partner, wo,
    w_other,
    load_sem, wkv_sem, own_sem, x_send, x_recv, c_send, c_recv, f_send, f_recv,
    map_send, map_recv, state_send, state_recv, ret_send, ret_recv, pair_send, pair_recv,
):
    c = lax.axis_index("ctx")
    z = lax.axis_index("mem")
    half = lax.axis_index("half")
    other = {"half": 1 - half}
    mine = aligned(half, DH)
    heads = range(HEADS)
    own_stage = lax.rem(c // 4 + 4 - lax.rem(c, 4) + 2 * half, LOCAL)
    own_pair = own_stage * HEADS + lax.rem(c, 4)

    def owner(m, h):
        return lax.rem(m + h + 2 * half, LOCAL) * 4 + h

    tok_load = pltpu.make_async_copy(tok_ref.at[:, mine], tok, load_sem.at[0])
    routes_load = pltpu.make_async_copy(routes_hbm, routes_ref, load_sem.at[3])
    routes_load.start()
    tok_load.start()
    small_loads = [
        pltpu.make_async_copy(wb_hbm, wb_ref, load_sem.at[4]),
        pltpu.make_async_copy(wd_hbm, wd_ref, load_sem.at[5]),
        pltpu.make_async_copy(gain_hbm, gain_ref, load_sem.at[6]),
    ]
    for load in small_loads:
        load.start()
    barrier = pltpu.get_barrier_semaphore()
    for d in range(1, MEM):
        pl.semaphore_signal(
            barrier, inc=1, device_id={"mem": lax.rem(z + d, MEM)}, device_id_type=MESH
        )
    pl.semaphore_signal(barrier, inc=1, device_id=other, device_id_type=MESH)
    for d in range(1, CTX):
        pl.semaphore_signal(
            barrier, inc=1, device_id={"ctx": lax.rem(c + d, CTX)}, device_id_type=MESH
        )

    def weights(m):
        return (
            pltpu.make_async_copy(wk_ref.at[m], wk.at[m], wkv_sem.at[0, m]),
            pltpu.make_async_copy(wv_ref.at[m], wv.at[m], wkv_sem.at[1, m]),
        )

    routes_load.wait()
    route = routes_ref[...]
    member = (iota((MEM * LOCAL, TOK), 0) == route).astype(F32)
    upper_tok = ones_where(iota((TOK, TOK), 0) <= iota((TOK, TOK), 1))
    place = jnp.sum(mm(member.astype(BF16), upper_tok) * member, axis=0, keepdims=True)
    slots = route * CAP + place.astype(jnp.int32) - 1
    totals = jnp.sum(member, axis=1, keepdims=True)
    counts[...] = jnp.zeros_like(counts)
    for to in range(MEM):
        counts[to, 0:LOCAL, :] = jnp.broadcast_to(
            totals[to * LOCAL : (to + 1) * LOCAL], (LOCAL, 128)
        )
    tok_load.wait()

    def x_copy(d, m):
        to = lax.rem(z + d, MEM)
        return pltpu.make_async_remote_copy(
            outgoing.at[m, to], xbuf.at[m, aligned(z, CAP), mine], x_send.at[d, m],
            x_recv.at[d, m], device_id={"mem": to}, device_id_type=MESH,
        )

    def x_arrival(d, m):
        src = lax.rem(z + MEM - d, MEM)
        return pltpu.make_async_remote_copy(
            outgoing.at[m, z], xbuf.at[m, aligned(src, CAP), mine], x_send.at[d, m],
            x_recv.at[d, m], device_id={"mem": src}, device_id_type=MESH,
        )

    def own_copy(m):
        return pltpu.make_async_copy(
            outgoing.at[m, z], xbuf.at[m, aligned(z, CAP), mine], own_sem.at[m]
        )

    def forward(d, m):
        src = lax.rem(z + MEM - d, MEM)
        landed = xbuf.at[m, aligned(src, CAP), mine]
        return pltpu.make_async_remote_copy(
            landed if d else outgoing.at[m, z], landed, f_send.at[d, m], f_recv.at[d, m],
            device_id=other, device_id_type=MESH,
        )

    def forward_arrival(d, m):
        src = lax.rem(z + MEM - d, MEM)
        landed = xbuf.at[m, aligned(src, CAP), aligned(1 - half, DH)]
        return pltpu.make_async_remote_copy(
            landed, landed, f_send.at[d, m], f_recv.at[d, m],
            device_id=other, device_id_type=MESH,
        )

    def count_copy(d):
        to = lax.rem(z + d, MEM)
        return pltpu.make_async_remote_copy(
            counts.at[to], cnt.at[z], c_send.at[d], c_recv.at[d],
            device_id={"mem": to}, device_id_type=MESH,
        )

    def gather(m):
        at = iota((ROWS, TOK), 0)
        slot = (at // CAP * LOCAL + m) * CAP + at % CAP
        rows = mm(ones_where(slot == slots), tok[...]).astype(BF16)
        outgoing[m] = rows.reshape(MEM, CAP, DH)

    def launch(m):
        for d in (1, 3, 2):
            x_copy(d, m).start()
        forward(0, m).start()
        own_copy(m).start()

    gather(0)
    pl.semaphore_wait(barrier, CTX - 1 + MEM)
    for d in range(1, MEM):
        count_copy(d).start()
    launch(0)
    for copy in weights(0):
        copy.start()
    cnt[z] = counts[z]

    @pl.loop(1, LOCAL)
    def _(m):
        gather(m)
        launch(m)
        for copy in weights(m):
            copy.start()

    wq_load = pltpu.make_async_copy(wq_ref, wq, load_sem.at[1])
    wq_load.start()
    wo_load = pltpu.make_async_copy(wo_ref, wo, load_sem.at[2])
    wo_load.start()

    def pass_on(m):
        for d in (1, 3, 2):
            x_arrival(d, m).wait_recv()
            forward(d, m).start()

    pass_on(0)
    for d in range(1, MEM):
        src = lax.rem(z + MEM - d, MEM)
        pltpu.make_async_remote_copy(
            counts.at[z], cnt.at[src], c_send.at[d], c_recv.at[d],
            device_id={"mem": src}, device_id_type=MESH,
        ).wait_recv()

    def map_copy(m, h):
        p = m * HEADS + h
        return pltpu.make_async_remote_copy(
            mw.at[p], maps.at[c], map_send.at[p], map_recv.at[c],
            device_id={"ctx": owner(m, h)}, device_id_type=MESH,
        )

    gates[...] = jnp.zeros_like(gates)
    for load in small_loads:
        load.wait()
    square = iota((K, K), 0), iota((K, K), 1)

    def lower_times(matrix, right):
        first, below, second = matrix
        return jnp.concatenate(
            [mm(first, right[:K]), mm(jnp.concatenate([below, second], axis=1), right)], axis=0
        )

    def lower_times_exact(matrix, right):
        first, below, second = matrix
        r_hi, r_lo = right
        return jnp.concatenate(
            [
                three_pass(first, (r_hi[:K], r_lo[:K])),
                three_pass(
                    tuple(jnp.concatenate([below[i], second[i]], axis=1) for i in range(2)), right
                ),
            ],
            axis=0,
        )

    def wait_tokens(m):
        for copy in weights(m):
            copy.wait()
        own_copy(m).wait()
        for d in range(MEM):
            forward_arrival(d, m).wait_recv()

    def projections(m):
        def gate_part():
            gates[0:HEADS, :] = wb_ref[m]
            gates[HEADS : 2 * HEADS, :] = wd_ref[m]
            logits_s[...] = mm_nt(gates[...], xbuf[m])

        def part(w, at, to):
            def run():
                kv[:, to : to + 2 * K] = mm(xbuf[m], w[m, :, at : at + 2 * K])

            return run

        return [gate_part] + [
            part(w, at, first + at) for w, first in ((wk, 0), (wv, WIDTH)) for at in (0, 2 * K)
        ]

    def make_maps(m, following):
        if following is not None:
            pass_on(following)
        logits = logits_s[...]
        keys_all = kv[:, :WIDTH]
        values_all = kv[:, WIDTH:]

        lane = iota((1, 128), 1)
        cnt_of = [cnt[src, pl.ds(m, 1), :] for src in range(MEM)]
        cnt_row = jnp.concatenate(
            [
                jnp.where(lane < CAP, cnt_of[0], cnt_of[1]),
                jnp.where(lane < CAP, cnt_of[2], cnt_of[3]),
            ],
            axis=1,
        )
        live = ((iota((1, ROWS), 1) & (CAP - 1)).astype(F32) < cnt_row).astype(F32)
        gate = iota((16, 1), 0)
        rate = jnp.zeros((16, 1), F32)
        for h in heads:
            rate = jnp.where(gate == HEADS + h, rate_ref[m, h], rate)
        strength = jax.nn.sigmoid(logits) * live
        soft = jnp.maximum(logits, 0.0) + jnp.log1p(jnp.exp(-jnp.abs(logits)))
        forget = -rate * soft * live
        upper = ones_where(iota((ROWS, ROWS), 0) <= iota((ROWS, ROWS), 1))
        hi, mid = split(forget)
        low = (forget - hi.astype(F32) - mid.astype(F32)).astype(BF16)
        total_t = mm(hi, upper) + mm(mid, upper) + mm(low, upper)
        both_t = jnp.where(gate < HEADS, strength, total_t)
        total_ts[m] = both_t
        b_hi, b_mid = split(both_t)
        b_low = (both_t - b_hi.astype(F32) - b_mid.astype(F32)).astype(BF16)
        at_gate = iota((48, 2 * WIDTH), 0) & 15
        wide = lax.dot_general(
            jnp.concatenate([b_hi, b_mid, b_low], axis=0),
            ones_where(at_gate == iota((48, 2 * WIDTH), 1) // K),
            (((0,), (0,)), ((), ())),
            preferred_element_type=F32,
        )
        fades[m] = wide[:, WIDTH:]

        keys, corner, target = [None] * HEADS, [None] * HEADS, [None] * HEADS
        blocks, inverse = [None] * (2 * HEADS), [None] * (2 * HEADS)
        strict = square[0] > square[1]
        pair = (square[0] ^ square[1]) == 1
        eye = ones_where(square[0] == square[1])
        for h in heads:
            at = slice(h * K, (h + 1) * K)
            k = unit(keys_all[:, at])
            keys[h] = k
            k_hi, k_lo = split(k)
            keys_s[m, h, :, :K] = k_hi
            keys_s[m, h, :, K:] = k_lo
            gram = mm_nt(
                jnp.concatenate([k_hi, k_lo], axis=1), jnp.concatenate([k_hi, k_hi], axis=1)
            ) + mm_nt(k_hi, k_lo)
            beta = wide[:, at]
            g_col = wide[:, WIDTH + h * K : WIDTH + (h + 1) * K]
            g_row = both_t[HEADS + h : HEADS + h + 1, :]
            for b in range(2):
                part = slice(b * K, (b + 1) * K)
                gap = jnp.minimum(g_col[part] - g_row[:, part], 0.0)
                mix = jnp.where(strict, gram[part, part] * jnp.exp(gap) * beta[part], 0.0)
                blocks[2 * h + b] = split(mix)
                inverse[2 * h + b] = jnp.where(pair, -mix, 0.0).astype(BF16) + eye
            corner[h] = split(gram[K:, :K] * jnp.exp(g_col[K:] - g_row[:, :K]) * beta[K:])
            target[h] = jnp.concatenate(
                [(beta * jnp.exp(g_col)) * k, beta * values_all[:, at]], axis=1
            )
        beside = []
        if following is not None:
            wait_tokens(following)
            beside = projections(following)
        inverse = unit_lower_inverses([b[0] for b in blocks], inverse, beside)
        cross = [mm(corner[h][0], inverse[2 * h]).astype(BF16) for h in heads]
        cross = [mm(inverse[2 * h + 1], cross[h]).astype(BF16) for h in heads]
        inverse = [
            (inverse[2 * h] - eye, -cross[h], inverse[2 * h + 1] - eye) for h in heads
        ]
        shift = [lower_times(inverse[h], target[h].astype(BF16)) for h in heads]
        guess = [target[h] + shift[h] for h in heads]
        rest = [None] * HEADS
        for h in heads:
            mix = (blocks[2 * h], corner[h], blocks[2 * h + 1])
            rest[h] = -(shift[h] + lower_times_exact(mix, split(guess[h])))
        solved = [
            guess[h] + (rest[h] + lower_times(inverse[h], rest[h].astype(BF16))) for h in heads
        ]
        diagonal = square[0] == square[1]
        for h in heads:
            y = split(solved[h])
            solved_hi[m, h], solved_lo[m, h] = y
            g_col = fades[m, :, h * K : (h + 1) * K]
            g_last = g_col[ROWS - 1 : ROWS, :]
            out = three_pass(split((keys[h] * jnp.exp(g_last - g_col)).T), y)
            p = m * HEADS + h
            mw[p, :, :K] = (jnp.where(diagonal, jnp.exp(g_last), 0.0) - out[:, :K]).astype(BF16)
            mw[p, :, K:] = out[:, K:].astype(BF16)
        for turn in heads:
            h = lax.rem(c + turn, HEADS)

            @pl.when((m * HEADS + h != own_pair) & (c < CTX - 1))
            def _():
                map_copy(m, h).start()

    def state_copy(to):
        return pltpu.make_async_remote_copy(
            states.at[to], entering.at[own_pair], state_send.at[to], state_recv.at[own_pair],
            device_id={"ctx": to}, device_id_type=MESH,
        )

    def run_pair():
        maps[c] = mw[own_pair]
        for j in range(CTX - 1):

            @pl.when(c != j)
            def _():
                pltpu.make_async_remote_copy(
                    mw.at[j], maps.at[j], map_send.at[j], map_recv.at[j],
                    device_id={"ctx": j}, device_id_type=MESH,
                ).wait_recv()

        pairs = []
        for j in range(0, CTX - 2, 2):
            joined = mm(maps[j + 1, :, :K], maps[j])
            m_hi, m_lo = split(joined[:, :K])
            pairs.append(
                (
                    jnp.concatenate([m_hi, m_lo, m_hi], axis=1),
                    joined[:, K:] + maps[j + 1, :, K:].astype(F32),
                )
            )
        states[1] = maps[0, :, K:]
        state = pairs[0][1]
        even = [state]
        for step, add in pairs[1:]:
            s_hi, s_lo = split(state)
            state = add + mm(step, jnp.concatenate([s_hi, s_hi, s_lo], axis=0))
            even.append(state)
        for n, state in enumerate(even):
            j = 2 * n + 2
            s_hi, s_lo = split(state)
            states[j] = s_hi
            step = maps[j, :, :K]
            states[j + 1] = (
                maps[j, :, K:].astype(F32)
                + mm(
                    jnp.concatenate([step, step], axis=1), jnp.concatenate([s_hi, s_lo], axis=0)
                )
            ).astype(BF16)

        @pl.loop(1, CTX)
        def _(turn):
            to = lax.rem(c + turn, CTX)

            @pl.when(to > 0)
            def _():
                state_copy(to).start()

        @pl.when(c > 0)
        def _():
            entering[own_pair] = states[c]

    @pl.when(c == 0)
    def _():
        entering[...] = jnp.zeros_like(entering)

    wait_tokens(0)
    for work in projections(0):
        work()

    @pl.loop(0, LOCAL - 1)
    def _(m):
        make_maps(m, m + 1)

    @pl.when(own_stage == 0)
    def _():
        run_pair()

    make_maps(LOCAL - 1, None)

    w_copy = pltpu.make_async_remote_copy(
        wo_ref, w_other, pair_send.at[0], pair_recv.at[0], device_id=other, device_id_type=MESH
    )
    w_copy.start()
    wq_load.wait()

    def local_output(m):
        query_all = mm(xbuf[m], wq[...])
        lower = square[0] >= square[1]
        for h in heads:
            at = slice(h * K, (h + 1) * K)
            q = unit(query_all[:, at])
            q_hi, q_lo = split(q)
            k_hi, k_lo = keys_s[m, h, :, :K], keys_s[m, h, :, K:]
            gram = mm_nt(
                jnp.concatenate([q_hi, q_lo], axis=1), jnp.concatenate([k_hi, k_hi], axis=1)
            ) + mm_nt(q_hi, k_lo)
            g_col = fades[m, :, at]
            g_row = total_ts[m, HEADS + h : HEADS + h + 1, :]
            parts = []
            for b in range(2):
                part = slice(b * K, (b + 1) * K)
                gap = jnp.minimum(g_col[part] - g_row[:, part], 0.0)
                parts.append(split(jnp.where(lower, gram[part, part] * jnp.exp(gap), 0.0)))
            below = split(gram[K:, :K] * jnp.exp(g_col[K:] - g_row[:, :K]))
            out = lower_times_exact(
                (parts[0], below, parts[1]), (solved_hi[m, h], solved_lo[m, h])
            )
            base[m, :, h * K : (h + 1) * K] = out[:, K:]
            r_hi, r_lo = split(q * jnp.exp(g_col) - out[:, :K])
            reach[m, :, 2 * h * K : (2 * h + 1) * K] = r_hi
            reach[m, :, (2 * h + 1) * K : (2 * h + 2) * K] = r_lo

    def ret_copy(d, m):
        to = lax.rem(z + d, MEM)
        return pltpu.make_async_remote_copy(
            reply.at[m, to], returned.at[z, m], ret_send.at[d, m], ret_recv.at[d, m],
            device_id={"mem": to}, device_id_type=MESH,
        )

    def send_outputs(m):
        for h in heads:
            p = m * HEADS + h

            @pl.when((c > 0) & (p != own_pair))
            def _():
                pltpu.make_async_remote_copy(
                    states.at[1], entering.at[p], state_send.at[1], state_recv.at[p],
                    device_id={"ctx": owner(m, h)}, device_id_type=MESH,
                ).wait_recv()

        for h in heads:
            at = slice(h * K, (h + 1) * K)
            s = entering[m * HEADS + h]
            heads_out = base[m, :, at] + mm(
                reach[m, :, 2 * h * K : (2 * h + 2) * K], jnp.concatenate([s, s], axis=0)
            )
            scale = lax.rsqrt(jnp.mean(heads_out * heads_out, axis=1, keepdims=True) + 1e-05)
            normed = (heads_out * scale * gain_ref[:, at]).astype(BF16)
            reply[m, :, :, at] = normed.reshape(MEM, CAP, K)
        for d in (2, 1, 3):
            ret_copy(d, m).start()

    @pl.loop(0, LOCAL - 1)
    def _(m):
        @pl.when((m == 0) & (own_stage == 1))
        def _():
            run_pair()

        local_output(m)

    @pl.when(own_stage == 2)
    def _():
        run_pair()

    send_outputs(0)
    local_output(LOCAL - 1)

    @pl.loop(1, LOCAL)
    def _(m):
        @pl.when((m == 2) & (own_stage == LOCAL - 1))
        def _():
            run_pair()

        send_outputs(m)

    column = jnp.broadcast_to(slots.astype(F32), (128, TOK)).T[:, 0:1].astype(jnp.int32)

    def pick(src, rows):
        chosen = ones_where(iota((TOK, ROWS), 1) + src * ROWS == column)
        return mm(chosen, rows)

    own_rows = jnp.concatenate([reply[m, z] for m in range(LOCAL)], axis=0)
    total = pick(z, own_rows)
    for d in (1, 3, 2):
        src = lax.rem(z + MEM - d, MEM)
        for m in range(LOCAL):
            pltpu.make_async_remote_copy(
                reply.at[m, z], returned.at[src, m], ret_send.at[d, m], ret_recv.at[d, m],
                device_id={"mem": src}, device_id_type=MESH,
            ).wait_recv()
        total = total + pick(src, returned[src].reshape(ROWS, WIDTH))
    picked[...] = total.astype(BF16)
    swap = pltpu.make_async_remote_copy(
        picked.at[aligned(1 - half, TOK // 2)], partner, pair_send.at[1], pair_recv.at[1],
        device_id=other, device_id_type=MESH,
    )
    swap.start()
    wo_load.wait()
    mixed = mm(picked[aligned(half, TOK // 2), :], wo[...])
    w_copy.wait()
    swap.wait()
    out_ref[...] = (mixed + mm(partner[...], w_other[...])).astype(BF16)

    for d in range(1, MEM):
        count_copy(d).wait_send()

    @pl.loop(0, LOCAL)
    def _(m):
        for d in range(1, MEM):
            x_copy(d, m).wait_send()
            ret_copy(d, m).wait_send()
        for d in range(MEM):
            forward(d, m).wait_send()
        for h in heads:

            @pl.when((m * HEADS + h != own_pair) & (c < CTX - 1))
            def _():
                map_copy(m, h).wait_send()

    @pl.loop(1, CTX)
    def _(j):
        @pl.when(c != j)
        def _():
            state_copy(j).wait_send()


def per_device(
    tokens, routes, w_query, w_key, w_value, w_beta, w_decay, decay_rate, norm_gain, w_out
):
    dma = pltpu.SemaphoreType.DMA
    vmem = pltpu.VMEM
    in_vmem = pl.BlockSpec(memory_space=pltpu.VMEM)
    in_place = pl.BlockSpec(memory_space=pl.ANY)
    return pl.pallas_call(
        layer_kernel,
        name="layer",
        out_shape=pltpu.VMEM((TOK // 2, D), BF16),
        in_specs=[
            pl.BlockSpec(memory_space=pltpu.SMEM), in_place, in_place, in_place, in_place,
            in_place, in_place, in_place, in_place, in_place,
        ],
        out_specs=in_vmem,
        scratch_shapes=[
            vmem((1, TOK), jnp.int32),
            vmem((LOCAL, HEADS, D), BF16),
            vmem((LOCAL, HEADS, D), BF16),
            vmem((1, WIDTH), F32),
            vmem((TOK, DH), BF16),
            vmem((LOCAL, MEM, CAP, DH), BF16),
            vmem((MEM, 8, 128), F32),
            vmem((MEM, 8, 128), F32),
            vmem((LOCAL, ROWS, D), BF16),
            vmem((D, WIDTH), BF16),
            vmem((LOCAL, D, WIDTH), BF16),
            vmem((LOCAL, D, WIDTH), BF16),
            vmem((16, D), BF16),
            vmem((ROWS, 2 * WIDTH), F32),
            vmem((16, ROWS), F32),
            vmem((LOCAL, ROWS, WIDTH), F32),
            vmem((LOCAL, 16, ROWS), F32),
            vmem((LOCAL, HEADS, ROWS, 2 * K), BF16),
            vmem((LOCAL, HEADS, ROWS, 2 * K), BF16),
            vmem((LOCAL, HEADS, ROWS, 2 * K), BF16),
            vmem((CTX, K, 2 * K), BF16),
            vmem((CTX, K, 2 * K), BF16),
            vmem((CTX, K, K), BF16),
            vmem((CTX, K, K), BF16),
            vmem((LOCAL, ROWS, WIDTH), F32),
            vmem((LOCAL, ROWS, 2 * WIDTH), BF16),
            vmem((LOCAL, MEM, CAP, WIDTH), BF16),
            vmem((MEM, LOCAL, CAP, WIDTH), BF16),
            vmem((TOK, WIDTH), BF16),
            vmem((TOK // 2, WIDTH), BF16),
            vmem((WIDTH, D), BF16),
            vmem((WIDTH, D), BF16),
            dma((7,)), dma((2, LOCAL)), dma((LOCAL,)),
            dma((MEM, LOCAL)), dma((MEM, LOCAL)), dma((MEM,)), dma((MEM,)),
            dma((MEM, LOCAL)), dma((MEM, LOCAL)),
            dma((CTX,)), dma((CTX,)), dma((CTX,)), dma((CTX,)),
            dma((MEM, LOCAL)), dma((MEM, LOCAL)), dma((2,)), dma((2,)),
        ],
        compiler_params=pltpu.CompilerParams(
            collective_id=0, has_side_effects=True, vmem_limit_bytes=58 * 1024 * 1024
        ),
    )(
        decay_rate,
        routes.reshape(1, TOK),
        tokens,
        w_query,
        w_key,
        w_value,
        jnp.swapaxes(w_beta, 1, 2),
        jnp.swapaxes(w_decay, 1, 2),
        norm_gain.reshape(1, WIDTH),
        w_out,
    )


def solution(mesh):
    in_specs = (
        P(("ctx", "mem"), None),
        P(("ctx", "mem"), None),
        P(None, "half"),
        P("mem", None, "half"),
        P("mem", None, "half"),
        P("mem", None, "half"),
        P("mem", None, "half"),
        P("mem", "half"),
        P("half"),
        P("half", None),
    )
    out_specs = P(("ctx", "mem", "half"), None)
    return jax.shard_map(
        per_device, mesh=mesh, in_specs=in_specs, out_specs=out_specs, check_vma=False
    )
```

```python
import jax
import jax.numpy as jnp
from jax import lax
from jax.experimental import pallas as pl
from jax.experimental.pallas import tpu as pltpu
from jax.sharding import PartitionSpec as P

MESH = pl.DeviceIdType.MESH
F32 = jnp.float32
BF16 = jnp.bfloat16
CTX, MEM = 16, 4
TOK = 512
D = 2048
DH = D // 2
CAP = 64
LOCAL = 4
HEADS = 4
ROWS = MEM * CAP
K = 128
WIDTH = HEADS * K


def mm(a, b):
    return jnp.dot(a, b, preferred_element_type=F32)


def mm_nt(a, b):
    return lax.dot_general(a, b, (((1,), (1,)), ((), ())), preferred_element_type=F32)


def split(x):
    hi = x.astype(BF16)
    return hi, (x - hi.astype(F32)).astype(BF16)


def iota(shape, axis):
    return lax.broadcasted_iota(jnp.int32, shape, axis)


def ones_where(mask):
    return mask.astype(F32).astype(BF16)


def aligned(index, size):
    return pl.ds(pl.multiple_of(index * size, size), size)


def unit(x):
    return x * lax.rsqrt(jnp.sum(x * x, axis=1, keepdims=True) + 1e-06)


def level_rows(x, size):
    return jnp.concatenate(
        [x[at + size : at + 2 * size] for at in range(0, x.shape[0], 2 * size)], axis=0
    )


def spread_rows(x, size):
    gap = jnp.zeros((size, x.shape[1]), x.dtype)
    parts = []
    for at in range(0, x.shape[0], size):
        parts += [gap, x[at : at + size]]
    return jnp.concatenate(parts, axis=0)


def unit_lower_inverses(low, inverse, beside):
    beside = list(beside)
    side = low[0].shape[0]
    apart = iota((side, side), 0) ^ iota((side, side), 1)
    size = 2
    while size < side:
        whole = size < 16
        pick = (lambda x: x) if whole else (lambda x: level_rows(x, size))
        put = (lambda x: x) if whole else (lambda x: spread_rows(x, size))
        near = pick(apart)
        here = (near >= size) & (near < 2 * size)
        mid_way = [
            jnp.where(here, mm(pick(a), x), 0.0).astype(BF16) for a, x in zip(low, inverse)
        ]
        if beside:
            beside.pop(0)()
        update = [
            put(mm(pick(x), put(y)).astype(BF16)) for x, y in zip(inverse, mid_way)
        ]
        inverse = [x - u for x, u in zip(inverse, update)]
        size *= 2
    for work in beside:
        work()
    return inverse


def three_pass(a, b):
    a_hi, a_lo = a
    b_hi, b_lo = b
    return mm(
        jnp.concatenate([a_hi, a_lo, a_hi], axis=1), jnp.concatenate([b_hi, b_hi, b_lo], axis=0)
    )


def layer_kernel(
    rate_hbm, routes_hbm, tok_ref, wq_ref, wk_ref, wv_ref, wb_hbm, wd_hbm, gain_hbm, wo_ref,
    out_ref,
    rate_ref, routes_ref, wb_ref, wd_ref, gain_ref, tok, outgoing, counts, cnt, xbuf, wq, wk, wv, gates, kv, logits_s, fades, total_ts, keys_s, solved_hi,
    solved_lo, mw, maps, states, entering, base, reach, reply, returned, picked, partner, wo,
    w_other,
    load_sem, wkv_sem, own_sem, x_send, x_recv, c_send, c_recv, f_send, f_recv,
    map_send, map_recv, state_send, state_recv, ret_send, ret_recv, pair_send, pair_recv,
):
    c = lax.axis_index("ctx")
    z = lax.axis_index("mem")
    half = lax.axis_index("half")
    other = {"half": 1 - half}
    mine = aligned(half, DH)
    heads = range(HEADS)
    own_stage = lax.rem(c // 4 + 4 - lax.rem(c, 4) + 2 * half, LOCAL)
    own_pair = own_stage * HEADS + lax.rem(c, 4)

    def owner(m, h):
        return lax.rem(m + h + 2 * half, LOCAL) * 4 + h

    tok_load = pltpu.make_async_copy(tok_ref.at[:, mine], tok, load_sem.at[0])
    routes_load = pltpu.make_async_copy(routes_hbm, routes_ref, load_sem.at[3])
    routes_load.start()
    tok_load.start()
    small_loads = [
        pltpu.make_async_copy(wb_hbm, wb_ref, load_sem.at[4]),
        pltpu.make_async_copy(wd_hbm, wd_ref, load_sem.at[5]),
        pltpu.make_async_copy(gain_hbm, gain_ref, load_sem.at[6]),
        pltpu.make_async_copy(rate_hbm, rate_ref, load_sem.at[7]),
    ]
    for load in small_loads:
        load.start()
    barrier = pltpu.get_barrier_semaphore()
    for d in range(1, MEM):
        pl.semaphore_signal(
            barrier, inc=1, device_id={"mem": lax.rem(z + d, MEM)}, device_id_type=MESH
        )
    pl.semaphore_signal(barrier, inc=1, device_id=other, device_id_type=MESH)
    for d in range(1, CTX):
        pl.semaphore_signal(
            barrier, inc=1, device_id={"ctx": lax.rem(c + d, CTX)}, device_id_type=MESH
        )

    def weights(m):
        return (
            pltpu.make_async_copy(wk_ref.at[m], wk.at[m], wkv_sem.at[0, m]),
            pltpu.make_async_copy(wv_ref.at[m], wv.at[m], wkv_sem.at[1, m]),
        )

    routes_load.wait()
    route = routes_ref[...]
    member = (iota((MEM * LOCAL, TOK), 0) == route).astype(F32)
    upper_tok = ones_where(iota((TOK, TOK), 0) <= iota((TOK, TOK), 1))
    place = jnp.sum(mm(member.astype(BF16), upper_tok) * member, axis=0, keepdims=True)
    slots = route * CAP + place.astype(jnp.int32) - 1
    totals = jnp.sum(member, axis=1, keepdims=True)
    counts[...] = jnp.zeros_like(counts)
    for to in range(MEM):
        counts[to, 0:LOCAL, :] = jnp.broadcast_to(
            totals[to * LOCAL : (to + 1) * LOCAL], (LOCAL, 128)
        )
    tok_load.wait()

    def x_copy(d, m):
        to = lax.rem(z + d, MEM)
        return pltpu.make_async_remote_copy(
            outgoing.at[m, to], xbuf.at[m, aligned(z, CAP), mine], x_send.at[d, m],
            x_recv.at[d, m], device_id={"mem": to}, device_id_type=MESH,
        )

    def x_arrival(d, m):
        src = lax.rem(z + MEM - d, MEM)
        return pltpu.make_async_remote_copy(
            outgoing.at[m, z], xbuf.at[m, aligned(src, CAP), mine], x_send.at[d, m],
            x_recv.at[d, m], device_id={"mem": src}, device_id_type=MESH,
        )

    def own_copy(m):
        return pltpu.make_async_copy(
            outgoing.at[m, z], xbuf.at[m, aligned(z, CAP), mine], own_sem.at[m]
        )

    def forward(d, m):
        src = lax.rem(z + MEM - d, MEM)
        landed = xbuf.at[m, aligned(src, CAP), mine]
        return pltpu.make_async_remote_copy(
            landed if d else outgoing.at[m, z], landed, f_send.at[d, m], f_recv.at[d, m],
            device_id=other, device_id_type=MESH,
        )

    def forward_arrival(d, m):
        src = lax.rem(z + MEM - d, MEM)
        landed = xbuf.at[m, aligned(src, CAP), aligned(1 - half, DH)]
        return pltpu.make_async_remote_copy(
            landed, landed, f_send.at[d, m], f_recv.at[d, m],
            device_id=other, device_id_type=MESH,
        )

    def count_copy(d):
        to = lax.rem(z + d, MEM)
        return pltpu.make_async_remote_copy(
            counts.at[to], cnt.at[z], c_send.at[d], c_recv.at[d],
            device_id={"mem": to}, device_id_type=MESH,
        )

    def gather(m):
        at = iota((ROWS, TOK), 0)
        slot = (at // CAP * LOCAL + m) * CAP + at % CAP
        rows = mm(ones_where(slot == slots), tok[...]).astype(BF16)
        outgoing[m] = rows.reshape(MEM, CAP, DH)

    def launch(m):
        for d in (1, 3, 2):
            x_copy(d, m).start()
        forward(0, m).start()
        own_copy(m).start()

    gather(0)
    pl.semaphore_wait(barrier, CTX - 1 + MEM)
    for d in range(1, MEM):
        count_copy(d).start()
    launch(0)
    for copy in weights(0):
        copy.start()
    cnt[z] = counts[z]

    @pl.loop(1, LOCAL)
    def _(m):
        gather(m)
        launch(m)
        for copy in weights(m):
            copy.start()

    wq_load = pltpu.make_async_copy(wq_ref, wq, load_sem.at[1])
    wq_load.start()
    wo_load = pltpu.make_async_copy(wo_ref, wo, load_sem.at[2])
    wo_load.start()

    def pass_on(m):
        for d in (1, 3, 2):
            x_arrival(d, m).wait_recv()
            forward(d, m).start()

    pass_on(0)
    for d in range(1, MEM):
        src = lax.rem(z + MEM - d, MEM)
        pltpu.make_async_remote_copy(
            counts.at[z], cnt.at[src], c_send.at[d], c_recv.at[d],
            device_id={"mem": src}, device_id_type=MESH,
        ).wait_recv()

    def map_copy(m, h):
        p = m * HEADS + h
        return pltpu.make_async_remote_copy(
            mw.at[p], maps.at[c], map_send.at[p], map_recv.at[c],
            device_id={"ctx": owner(m, h)}, device_id_type=MESH,
        )

    gates[...] = jnp.zeros_like(gates)
    for load in small_loads:
        load.wait()
    square = iota((K, K), 0), iota((K, K), 1)

    def lower_times(matrix, right):
        first, below, second = matrix
        return jnp.concatenate(
            [mm(first, right[:K]), mm(jnp.concatenate([below, second], axis=1), right)], axis=0
        )

    def lower_times_exact(matrix, right):
        first, below, second = matrix
        r_hi, r_lo = right
        return jnp.concatenate(
            [
                three_pass(first, (r_hi[:K], r_lo[:K])),
                three_pass(
                    tuple(jnp.concatenate([below[i], second[i]], axis=1) for i in range(2)), right
                ),
            ],
            axis=0,
        )

    def wait_tokens(m):
        for copy in weights(m):
            copy.wait()
        own_copy(m).wait()
        for d in range(MEM):
            forward_arrival(d, m).wait_recv()

    def projections(m):
        def gate_part():
            gates[0:HEADS, :] = wb_ref[m]
            gates[HEADS : 2 * HEADS, :] = wd_ref[m]
            logits_s[...] = mm_nt(gates[...], xbuf[m])

        def part(w, at, to):
            def run():
                kv[:, to : to + 2 * K] = mm(xbuf[m], w[m, :, at : at + 2 * K])

            return run

        return [gate_part] + [
            part(w, at, first + at) for w, first in ((wk, 0), (wv, WIDTH)) for at in (0, 2 * K)
        ]

    def make_maps(m, following):
        if following is not None:
            pass_on(following)
        logits = logits_s[...]
        keys_all = kv[:, :WIDTH]
        values_all = kv[:, WIDTH:]

        lane = iota((1, 128), 1)
        cnt_of = [cnt[src, pl.ds(m, 1), :] for src in range(MEM)]
        cnt_row = jnp.concatenate(
            [
                jnp.where(lane < CAP, cnt_of[0], cnt_of[1]),
                jnp.where(lane < CAP, cnt_of[2], cnt_of[3]),
            ],
            axis=1,
        )
        live = ((iota((1, ROWS), 1) & (CAP - 1)).astype(F32) < cnt_row).astype(F32)
        gate = iota((16, 1), 0)
        own_gate = iota((16, HEADS), 0) == iota((16, HEADS), 1) + HEADS
        rate = jnp.sum(
            jnp.where(own_gate, rate_ref[pl.ds(m, 1), :], 0.0), axis=1, keepdims=True
        )
        strength = jax.nn.sigmoid(logits) * live
        soft = jnp.maximum(logits, 0.0) + jnp.log1p(jnp.exp(-jnp.abs(logits)))
        forget = -rate * soft * live
        upper = ones_where(iota((ROWS, ROWS), 0) <= iota((ROWS, ROWS), 1))
        hi, mid = split(forget)
        low = (forget - hi.astype(F32) - mid.astype(F32)).astype(BF16)
        total_t = mm(hi, upper) + mm(mid, upper) + mm(low, upper)
        both_t = jnp.where(gate < HEADS, strength, total_t)
        total_ts[m] = both_t
        b_hi, b_mid = split(both_t)
        b_low = (both_t - b_hi.astype(F32) - b_mid.astype(F32)).astype(BF16)
        at_gate = iota((48, 2 * WIDTH), 0) & 15
        wide = lax.dot_general(
            jnp.concatenate([b_hi, b_mid, b_low], axis=0),
            ones_where(at_gate == iota((48, 2 * WIDTH), 1) // K),
            (((0,), (0,)), ((), ())),
            preferred_element_type=F32,
        )
        fades[m] = wide[:, WIDTH:]

        keys, corner, target = [None] * HEADS, [None] * HEADS, [None] * HEADS
        blocks, inverse = [None] * (2 * HEADS), [None] * (2 * HEADS)
        strict = square[0] > square[1]
        pair = (square[0] ^ square[1]) == 1
        eye = ones_where(square[0] == square[1])
        for h in heads:
            at = slice(h * K, (h + 1) * K)
            k = unit(keys_all[:, at])
            keys[h] = k
            k_hi, k_lo = split(k)
            keys_s[m, h, :, :K] = k_hi
            keys_s[m, h, :, K:] = k_lo
            gram = mm_nt(
                jnp.concatenate([k_hi, k_lo], axis=1), jnp.concatenate([k_hi, k_hi], axis=1)
            ) + mm_nt(k_hi, k_lo)
            beta = wide[:, at]
            g_col = wide[:, WIDTH + h * K : WIDTH + (h + 1) * K]
            g_row = both_t[HEADS + h : HEADS + h + 1, :]
            for b in range(2):
                part = slice(b * K, (b + 1) * K)
                gap = jnp.minimum(g_col[part] - g_row[:, part], 0.0)
                mix = jnp.where(strict, gram[part, part] * jnp.exp(gap) * beta[part], 0.0)
                blocks[2 * h + b] = split(mix)
                inverse[2 * h + b] = jnp.where(pair, -mix, 0.0).astype(BF16) + eye
            corner[h] = split(gram[K:, :K] * jnp.exp(g_col[K:] - g_row[:, :K]) * beta[K:])
            target[h] = jnp.concatenate(
                [(beta * jnp.exp(g_col)) * k, beta * values_all[:, at]], axis=1
            )
        beside = []
        if following is not None:
            wait_tokens(following)
            beside = projections(following)
        inverse = unit_lower_inverses([b[0] for b in blocks], inverse, beside)
        cross = [mm(corner[h][0], inverse[2 * h]).astype(BF16) for h in heads]
        cross = [mm(inverse[2 * h + 1], cross[h]).astype(BF16) for h in heads]
        inverse = [
            (inverse[2 * h] - eye, -cross[h], inverse[2 * h + 1] - eye) for h in heads
        ]
        shift = [lower_times(inverse[h], target[h].astype(BF16)) for h in heads]
        guess = [target[h] + shift[h] for h in heads]
        rest = [None] * HEADS
        for h in heads:
            mix = (blocks[2 * h], corner[h], blocks[2 * h + 1])
            rest[h] = -(shift[h] + lower_times_exact(mix, split(guess[h])))
        solved = [
            guess[h] + (rest[h] + lower_times(inverse[h], rest[h].astype(BF16))) for h in heads
        ]
        diagonal = square[0] == square[1]
        for h in heads:
            y = split(solved[h])
            solved_hi[m, h], solved_lo[m, h] = y
            g_col = fades[m, :, h * K : (h + 1) * K]
            g_last = g_col[ROWS - 1 : ROWS, :]
            out = three_pass(split((keys[h] * jnp.exp(g_last - g_col)).T), y)
            p = m * HEADS + h
            mw[p, :, :K] = (jnp.where(diagonal, jnp.exp(g_last), 0.0) - out[:, :K]).astype(BF16)
            mw[p, :, K:] = out[:, K:].astype(BF16)
        for turn in heads:
            h = lax.rem(c + turn, HEADS)

            @pl.when((m * HEADS + h != own_pair) & (c < CTX - 1))
            def _():
                map_copy(m, h).start()

    def state_copy(to):
        return pltpu.make_async_remote_copy(
            states.at[to], entering.at[own_pair], state_send.at[to], state_recv.at[own_pair],
            device_id={"ctx": to}, device_id_type=MESH,
        )

    def run_pair():
        maps[c] = mw[own_pair]
        for j in range(CTX - 1):

            @pl.when(c != j)
            def _():
                pltpu.make_async_remote_copy(
                    mw.at[j], maps.at[j], map_send.at[j], map_recv.at[j],
                    device_id={"ctx": j}, device_id_type=MESH,
                ).wait_recv()

        pairs = []
        for j in range(0, CTX - 2, 2):
            joined = mm(maps[j + 1, :, :K], maps[j])
            m_hi, m_lo = split(joined[:, :K])
            pairs.append(
                (
                    jnp.concatenate([m_hi, m_lo, m_hi], axis=1),
                    joined[:, K:] + maps[j + 1, :, K:].astype(F32),
                )
            )
        states[1] = maps[0, :, K:]
        state = pairs[0][1]
        even = [state]
        for step, add in pairs[1:]:
            s_hi, s_lo = split(state)
            state = add + mm(step, jnp.concatenate([s_hi, s_hi, s_lo], axis=0))
            even.append(state)
        for n, state in enumerate(even):
            j = 2 * n + 2
            s_hi, s_lo = split(state)
            states[j] = s_hi
            step = maps[j, :, :K]
            states[j + 1] = (
                maps[j, :, K:].astype(F32)
                + mm(
                    jnp.concatenate([step, step], axis=1), jnp.concatenate([s_hi, s_lo], axis=0)
                )
            ).astype(BF16)

        @pl.loop(1, CTX)
        def _(turn):
            to = lax.rem(c + turn, CTX)

            @pl.when(to > 0)
            def _():
                state_copy(to).start()

        @pl.when(c > 0)
        def _():
            entering[own_pair] = states[c]

    @pl.when(c == 0)
    def _():
        entering[...] = jnp.zeros_like(entering)

    wait_tokens(0)
    for work in projections(0):
        work()

    @pl.loop(0, LOCAL - 1)
    def _(m):
        make_maps(m, m + 1)

    @pl.when(own_stage == 0)
    def _():
        run_pair()

    make_maps(LOCAL - 1, None)

    w_copy = pltpu.make_async_remote_copy(
        wo_ref, w_other, pair_send.at[0], pair_recv.at[0], device_id=other, device_id_type=MESH
    )
    w_copy.start()
    wq_load.wait()

    def local_output(m):
        query_all = mm(xbuf[m], wq[...])
        lower = square[0] >= square[1]
        for h in heads:
            at = slice(h * K, (h + 1) * K)
            q = unit(query_all[:, at])
            q_hi, q_lo = split(q)
            k_hi, k_lo = keys_s[m, h, :, :K], keys_s[m, h, :, K:]
            gram = mm_nt(
                jnp.concatenate([q_hi, q_lo], axis=1), jnp.concatenate([k_hi, k_hi], axis=1)
            ) + mm_nt(q_hi, k_lo)
            g_col = fades[m, :, at]
            g_row = total_ts[m, HEADS + h : HEADS + h + 1, :]
            parts = []
            for b in range(2):
                part = slice(b * K, (b + 1) * K)
                gap = jnp.minimum(g_col[part] - g_row[:, part], 0.0)
                parts.append(split(jnp.where(lower, gram[part, part] * jnp.exp(gap), 0.0)))
            below = split(gram[K:, :K] * jnp.exp(g_col[K:] - g_row[:, :K]))
            out = lower_times_exact(
                (parts[0], below, parts[1]), (solved_hi[m, h], solved_lo[m, h])
            )
            base[m, :, h * K : (h + 1) * K] = out[:, K:]
            r_hi, r_lo = split(q * jnp.exp(g_col) - out[:, :K])
            reach[m, :, 2 * h * K : (2 * h + 1) * K] = r_hi
            reach[m, :, (2 * h + 1) * K : (2 * h + 2) * K] = r_lo

    def ret_copy(d, m):
        to = lax.rem(z + d, MEM)
        return pltpu.make_async_remote_copy(
            reply.at[m, to], returned.at[z, m], ret_send.at[d, m], ret_recv.at[d, m],
            device_id={"mem": to}, device_id_type=MESH,
        )

    def send_outputs(m):
        for h in heads:
            p = m * HEADS + h

            @pl.when((c > 0) & (p != own_pair))
            def _():
                pltpu.make_async_remote_copy(
                    states.at[1], entering.at[p], state_send.at[1], state_recv.at[p],
                    device_id={"ctx": owner(m, h)}, device_id_type=MESH,
                ).wait_recv()

        for h in heads:
            at = slice(h * K, (h + 1) * K)
            s = entering[m * HEADS + h]
            heads_out = base[m, :, at] + mm(
                reach[m, :, 2 * h * K : (2 * h + 2) * K], jnp.concatenate([s, s], axis=0)
            )
            scale = lax.rsqrt(jnp.mean(heads_out * heads_out, axis=1, keepdims=True) + 1e-05)
            normed = (heads_out * scale * gain_ref[:, at]).astype(BF16)
            reply[m, :, :, at] = normed.reshape(MEM, CAP, K)
        for d in (1, 3, 2):
            ret_copy(d, m).start()

    @pl.loop(0, LOCAL - 1)
    def _(m):
        @pl.when((m == 0) & (own_stage == 1))
        def _():
            run_pair()

        local_output(m)

    @pl.when(own_stage == 2)
    def _():
        run_pair()

    send_outputs(0)
    local_output(LOCAL - 1)

    @pl.loop(1, LOCAL)
    def _(m):
        @pl.when((m == 1) & (own_stage == LOCAL - 1))
        def _():
            run_pair()

        send_outputs(m)

    for d in range(1, MEM):
        count_copy(d).wait_send()

    @pl.loop(0, LOCAL)
    def _(m):
        for d in range(1, MEM):
            x_copy(d, m).wait_send()
        for d in range(MEM):
            forward(d, m).wait_send()
        for h in heads:

            @pl.when((m * HEADS + h != own_pair) & (c < CTX - 1))
            def _():
                map_copy(m, h).wait_send()

    @pl.loop(1, CTX)
    def _(j):
        @pl.when(c != j)
        def _():
            state_copy(j).wait_send()

    column = jnp.broadcast_to(slots.astype(F32), (128, TOK)).T[:, 0:1].astype(jnp.int32)

    source = [lax.rem(z + MEM - d, MEM) for d in range(MEM)]
    chosen = [
        ones_where(iota((TOK, ROWS), 1) + src * ROWS == column) for src in source
    ]
    total = mm(chosen[0], jnp.concatenate([reply[m, z] for m in range(LOCAL)], axis=0))
    for d in (1, 3, 2):
        for m in range(LOCAL):
            pltpu.make_async_remote_copy(
                reply.at[m, z], returned.at[source[d], m], ret_send.at[d, m], ret_recv.at[d, m],
                device_id={"mem": source[d]}, device_id_type=MESH,
            ).wait_recv()
        total = total + mm(chosen[d], returned[source[d]].reshape(ROWS, WIDTH))
    picked[...] = total.astype(BF16)
    swap = pltpu.make_async_remote_copy(
        picked.at[aligned(1 - half, TOK // 2)], partner, pair_send.at[1], pair_recv.at[1],
        device_id=other, device_id_type=MESH,
    )
    swap.start()
    wo_load.wait()
    mixed = mm(picked[aligned(half, TOK // 2), :], wo[...])
    w_copy.wait()
    swap.wait()
    out_ref[...] = (mixed + mm(partner[...], w_other[...])).astype(BF16)

    @pl.loop(0, LOCAL)
    def _(m):
        for d in range(1, MEM):
            ret_copy(d, m).wait_send()


def per_device(
    tokens, routes, w_query, w_key, w_value, w_beta, w_decay, decay_rate, norm_gain, w_out
):
    dma = pltpu.SemaphoreType.DMA
    vmem = pltpu.VMEM
    in_vmem = pl.BlockSpec(memory_space=pltpu.VMEM)
    in_place = pl.BlockSpec(memory_space=pl.ANY)
    return pl.pallas_call(
        layer_kernel,
        name="layer",
        out_shape=pltpu.VMEM((TOK // 2, D), BF16),
        in_specs=[
            in_place, in_place, in_place, in_place, in_place,
            in_place, in_place, in_place, in_place, in_place,
        ],
        out_specs=in_vmem,
        scratch_shapes=[
            vmem((LOCAL, HEADS), F32),
            vmem((1, TOK), jnp.int32),
            vmem((LOCAL, HEADS, D), BF16),
            vmem((LOCAL, HEADS, D), BF16),
            vmem((1, WIDTH), F32),
            vmem((TOK, DH), BF16),
            vmem((LOCAL, MEM, CAP, DH), BF16),
            vmem((MEM, 8, 128), F32),
            vmem((MEM, 8, 128), F32),
            vmem((LOCAL, ROWS, D), BF16),
            vmem((D, WIDTH), BF16),
            vmem((LOCAL, D, WIDTH), BF16),
            vmem((LOCAL, D, WIDTH), BF16),
            vmem((16, D), BF16),
            vmem((ROWS, 2 * WIDTH), F32),
            vmem((16, ROWS), F32),
            vmem((LOCAL, ROWS, WIDTH), F32),
            vmem((LOCAL, 16, ROWS), F32),
            vmem((LOCAL, HEADS, ROWS, 2 * K), BF16),
            vmem((LOCAL, HEADS, ROWS, 2 * K), BF16),
            vmem((LOCAL, HEADS, ROWS, 2 * K), BF16),
            vmem((CTX, K, 2 * K), BF16),
            vmem((CTX, K, 2 * K), BF16),
            vmem((CTX, K, K), BF16),
            vmem((CTX, K, K), BF16),
            vmem((LOCAL, ROWS, WIDTH), F32),
            vmem((LOCAL, ROWS, 2 * WIDTH), BF16),
            vmem((LOCAL, MEM, CAP, WIDTH), BF16),
            vmem((MEM, LOCAL, CAP, WIDTH), BF16),
            vmem((TOK, WIDTH), BF16),
            vmem((TOK // 2, WIDTH), BF16),
            vmem((WIDTH, D), BF16),
            vmem((WIDTH, D), BF16),
            dma((8,)), dma((2, LOCAL)), dma((LOCAL,)),
            dma((MEM, LOCAL)), dma((MEM, LOCAL)), dma((MEM,)), dma((MEM,)),
            dma((MEM, LOCAL)), dma((MEM, LOCAL)),
            dma((CTX,)), dma((CTX,)), dma((CTX,)), dma((CTX,)),
            dma((MEM, LOCAL)), dma((MEM, LOCAL)), dma((2,)), dma((2,)),
        ],
        compiler_params=pltpu.CompilerParams(
            collective_id=0, has_side_effects=True, vmem_limit_bytes=58 * 1024 * 1024
        ),
    )(
        decay_rate,
        routes.reshape(1, TOK),
        tokens,
        w_query,
        w_key,
        w_value,
        jnp.swapaxes(w_beta, 1, 2),
        jnp.swapaxes(w_decay, 1, 2),
        norm_gain.reshape(1, WIDTH),
        w_out,
    )


def solution(mesh):
    in_specs = (
        P(("ctx", "mem"), None),
        P(("ctx", "mem"), None),
        P(None, "half"),
        P("mem", None, "half"),
        P("mem", None, "half"),
        P("mem", None, "half"),
        P("mem", None, "half"),
        P("mem", "half"),
        P("half"),
        P("half", None),
    )
    out_specs = P(("ctx", "mem", "half"), None)
    return jax.shard_map(
        per_device, mesh=mesh, in_specs=in_specs, out_specs=out_specs, check_vma=False
    )
```

```python
import jax
import jax.numpy as jnp
from jax import lax
from jax.experimental import pallas as pl
from jax.experimental.pallas import tpu as pltpu
from jax.sharding import PartitionSpec as P

MESH = pl.DeviceIdType.MESH
F32 = jnp.float32
BF16 = jnp.bfloat16
CTX, MEM = 16, 4
TOK = 512
D = 2048
DH = D // 2
CAP = 64
LOCAL = 4
HEADS = 4
ROWS = MEM * CAP
K = 128
WIDTH = HEADS * K


def mm(a, b):
    return jnp.dot(a, b, preferred_element_type=F32)


def mm_nt(a, b):
    return lax.dot_general(a, b, (((1,), (1,)), ((), ())), preferred_element_type=F32)


def split(x):
    hi = x.astype(BF16)
    return hi, (x - hi.astype(F32)).astype(BF16)


def iota(shape, axis):
    return lax.broadcasted_iota(jnp.int32, shape, axis)


def ones_where(mask):
    return mask.astype(F32).astype(BF16)


def aligned(index, size):
    return pl.ds(pl.multiple_of(index * size, size), size)


def unit(x):
    return x * lax.rsqrt(jnp.sum(x * x, axis=1, keepdims=True) + 1e-06)


def level_rows(x, size):
    return jnp.concatenate(
        [x[at + size : at + 2 * size] for at in range(0, x.shape[0], 2 * size)], axis=0
    )


def spread_rows(x, size):
    gap = jnp.zeros((size, x.shape[1]), x.dtype)
    parts = []
    for at in range(0, x.shape[0], size):
        parts += [gap, x[at : at + size]]
    return jnp.concatenate(parts, axis=0)


def unit_lower_inverses(low, inverse, beside):
    beside = list(beside)
    side = low[0].shape[0]
    apart = iota((side, side), 0) ^ iota((side, side), 1)
    size = 2
    while size < side:
        whole = size < 16
        pick = (lambda x: x) if whole else (lambda x: level_rows(x, size))
        put = (lambda x: x) if whole else (lambda x: spread_rows(x, size))
        near = pick(apart)
        here = (near >= size) & (near < 2 * size)
        mid_way = [
            jnp.where(here, mm(pick(a), x), 0.0).astype(BF16) for a, x in zip(low, inverse)
        ]
        if beside:
            beside.pop(0)()
        update = [
            put(mm(pick(x), put(y)).astype(BF16)) for x, y in zip(inverse, mid_way)
        ]
        inverse = [x - u for x, u in zip(inverse, update)]
        size *= 2
    for work in beside:
        work()
    return inverse


def three_pass(a, b):
    a_hi, a_lo = a
    b_hi, b_lo = b
    return mm(
        jnp.concatenate([a_hi, a_lo, a_hi], axis=1), jnp.concatenate([b_hi, b_hi, b_lo], axis=0)
    )


def layer_kernel(
    rate_hbm, routes_hbm, tok_ref, wq_ref, wk_ref, wv_ref, wb_hbm, wd_hbm, gain_hbm, wo_ref,
    out_ref,
    upper_s, select_s, rate_ref, routes_ref, wb_ref, wd_ref, gain_ref, tok, outgoing, counts, cnt, xbuf, wq, wk, wv, gates, kv, logits_s, fades, total_ts, keys_s, solved_hi,
    solved_lo, mw, maps, states, entering, base, reach, reply, returned, picked, partner, wo,
    w_other,
    load_sem, wkv_sem, own_sem, x_send, x_recv, c_send, c_recv, f_send, f_recv,
    map_send, map_recv, state_send, state_recv, ret_send, ret_recv, pair_send, pair_recv,
):
    c = lax.axis_index("ctx")
    z = lax.axis_index("mem")
    half = lax.axis_index("half")
    other = {"half": 1 - half}
    mine = aligned(half, DH)
    heads = range(HEADS)
    own_stage = lax.rem(c // 4 + 4 - lax.rem(c, 4) + 2 * half, LOCAL)
    own_pair = own_stage * HEADS + lax.rem(c, 4)

    def owner(m, h):
        return lax.rem(m + h + 2 * half, LOCAL) * 4 + h

    tok_load = pltpu.make_async_copy(tok_ref.at[:, mine], tok, load_sem.at[0])
    routes_load = pltpu.make_async_copy(routes_hbm, routes_ref, load_sem.at[3])
    routes_load.start()
    tok_load.start()
    small_loads = [
        pltpu.make_async_copy(wb_hbm, wb_ref, load_sem.at[4]),
        pltpu.make_async_copy(wd_hbm, wd_ref, load_sem.at[5]),
        pltpu.make_async_copy(gain_hbm, gain_ref, load_sem.at[6]),
        pltpu.make_async_copy(rate_hbm, rate_ref, load_sem.at[7]),
    ]
    for load in small_loads:
        load.start()
    barrier = pltpu.get_barrier_semaphore()
    for d in range(1, MEM):
        pl.semaphore_signal(
            barrier, inc=1, device_id={"mem": lax.rem(z + d, MEM)}, device_id_type=MESH
        )
    pl.semaphore_signal(barrier, inc=1, device_id=other, device_id_type=MESH)
    for d in range(1, CTX):
        pl.semaphore_signal(
            barrier, inc=1, device_id={"ctx": lax.rem(c + d, CTX)}, device_id_type=MESH
        )

    def weights(m):
        return (
            pltpu.make_async_copy(wk_ref.at[m], wk.at[m], wkv_sem.at[0, m]),
            pltpu.make_async_copy(wv_ref.at[m], wv.at[m], wkv_sem.at[1, m]),
        )

    routes_load.wait()
    route = routes_ref[...]
    member = (iota((MEM * LOCAL, TOK), 0) == route).astype(F32)
    upper_tok = ones_where(iota((TOK, TOK), 0) <= iota((TOK, TOK), 1))
    place = jnp.sum(mm(member.astype(BF16), upper_tok) * member, axis=0, keepdims=True)
    slots = route * CAP + place.astype(jnp.int32) - 1
    totals = jnp.sum(member, axis=1, keepdims=True)
    counts[...] = jnp.zeros_like(counts)
    for to in range(MEM):
        counts[to, 0:LOCAL, :] = jnp.broadcast_to(
            totals[to * LOCAL : (to + 1) * LOCAL], (LOCAL, 128)
        )
    tok_load.wait()

    def x_copy(d, m):
        to = lax.rem(z + d, MEM)
        return pltpu.make_async_remote_copy(
            outgoing.at[m, to], xbuf.at[m, aligned(z, CAP), mine], x_send.at[d, m],
            x_recv.at[d, m], device_id={"mem": to}, device_id_type=MESH,
        )

    def x_arrival(d, m):
        src = lax.rem(z + MEM - d, MEM)
        return pltpu.make_async_remote_copy(
            outgoing.at[m, z], xbuf.at[m, aligned(src, CAP), mine], x_send.at[d, m],
            x_recv.at[d, m], device_id={"mem": src}, device_id_type=MESH,
        )

    def own_copy(m):
        return pltpu.make_async_copy(
            outgoing.at[m, z], xbuf.at[m, aligned(z, CAP), mine], own_sem.at[m]
        )

    def forward(d, m):
        src = lax.rem(z + MEM - d, MEM)
        landed = xbuf.at[m, aligned(src, CAP), mine]
        return pltpu.make_async_remote_copy(
            landed if d else outgoing.at[m, z], landed, f_send.at[d, m], f_recv.at[d, m],
            device_id=other, device_id_type=MESH,
        )

    def forward_arrival(d, m):
        src = lax.rem(z + MEM - d, MEM)
        landed = xbuf.at[m, aligned(src, CAP), aligned(1 - half, DH)]
        return pltpu.make_async_remote_copy(
            landed, landed, f_send.at[d, m], f_recv.at[d, m],
            device_id=other, device_id_type=MESH,
        )

    def count_copy(d):
        to = lax.rem(z + d, MEM)
        return pltpu.make_async_remote_copy(
            counts.at[to], cnt.at[z], c_send.at[d], c_recv.at[d],
            device_id={"mem": to}, device_id_type=MESH,
        )

    def gather(m):
        at = iota((ROWS, TOK), 0)
        slot = (at // CAP * LOCAL + m) * CAP + at % CAP
        rows = mm(ones_where(slot == slots), tok[...]).astype(BF16)
        outgoing[m] = rows.reshape(MEM, CAP, DH)

    def launch(m):
        for d in (1, 3, 2):
            x_copy(d, m).start()
        forward(0, m).start()
        own_copy(m).start()

    gather(0)
    pl.semaphore_wait(barrier, CTX - 1 + MEM)
    for d in range(1, MEM):
        count_copy(d).start()
    launch(0)
    for copy in weights(0):
        copy.start()
    cnt[z] = counts[z]

    @pl.loop(1, LOCAL)
    def _(m):
        gather(m)
        launch(m)
        for copy in weights(m):
            copy.start()

    wq_load = pltpu.make_async_copy(wq_ref, wq, load_sem.at[1])
    wq_load.start()
    wo_load = pltpu.make_async_copy(wo_ref, wo, load_sem.at[2])
    wo_load.start()

    def pass_on(m):
        for d in (1, 3, 2):
            x_arrival(d, m).wait_recv()
            forward(d, m).start()

    gates[...] = jnp.zeros_like(gates)
    upper_s[...] = ones_where(iota((ROWS, ROWS), 0) <= iota((ROWS, ROWS), 1))
    at_gate = iota((48, 2 * WIDTH), 0) & 15
    select_s[...] = ones_where(at_gate == iota((48, 2 * WIDTH), 1) // K)

    pass_on(0)
    for d in range(1, MEM):
        src = lax.rem(z + MEM - d, MEM)
        pltpu.make_async_remote_copy(
            counts.at[z], cnt.at[src], c_send.at[d], c_recv.at[d],
            device_id={"mem": src}, device_id_type=MESH,
        ).wait_recv()

    def map_copy(m, h):
        p = m * HEADS + h
        return pltpu.make_async_remote_copy(
            mw.at[p], maps.at[c], map_send.at[p], map_recv.at[c],
            device_id={"ctx": owner(m, h)}, device_id_type=MESH,
        )

    for load in small_loads:
        load.wait()
    square = iota((K, K), 0), iota((K, K), 1)

    def lower_times(matrix, right):
        first, below, second = matrix
        return jnp.concatenate(
            [mm(first, right[:K]), mm(jnp.concatenate([below, second], axis=1), right)], axis=0
        )

    def lower_times_exact(matrix, right):
        first, below, second = matrix
        r_hi, r_lo = right
        return jnp.concatenate(
            [
                three_pass(first, (r_hi[:K], r_lo[:K])),
                three_pass(
                    tuple(jnp.concatenate([below[i], second[i]], axis=1) for i in range(2)), right
                ),
            ],
            axis=0,
        )

    def wait_loads(m):
        for copy in weights(m):
            copy.wait()
        own_copy(m).wait()

    def wait_tokens(m):
        for d in range(MEM):
            forward_arrival(d, m).wait_recv()

    def projections(m):
        def gate_part():
            gates[0:HEADS, :] = wb_ref[m]
            gates[HEADS : 2 * HEADS, :] = wd_ref[m]
            logits_s[...] = mm_nt(gates[...], xbuf[m])

        def part(w, at, to):
            def run():
                kv[:, to : to + 2 * K] = mm(xbuf[m], w[m, :, at : at + 2 * K])

            return run

        return [gate_part] + [
            part(w, at, first + at) for w, first in ((wk, 0), (wv, WIDTH)) for at in (0, 2 * K)
        ]

    def make_maps(m, following):
        if following is not None:
            pass_on(following)
        logits = logits_s[...]
        keys_all = kv[:, :WIDTH]
        values_all = kv[:, WIDTH:]

        lane = iota((1, 128), 1)
        cnt_of = [cnt[src, pl.ds(m, 1), :] for src in range(MEM)]
        cnt_row = jnp.concatenate(
            [
                jnp.where(lane < CAP, cnt_of[0], cnt_of[1]),
                jnp.where(lane < CAP, cnt_of[2], cnt_of[3]),
            ],
            axis=1,
        )
        live = ((iota((1, ROWS), 1) & (CAP - 1)).astype(F32) < cnt_row).astype(F32)
        gate = iota((16, 1), 0)
        own_gate = iota((16, HEADS), 0) == iota((16, HEADS), 1) + HEADS
        rate = jnp.sum(
            jnp.where(own_gate, rate_ref[pl.ds(m, 1), :], 0.0), axis=1, keepdims=True
        )
        strength = jax.nn.sigmoid(logits) * live
        soft = jnp.maximum(logits, 0.0) + jnp.log1p(jnp.exp(-jnp.abs(logits)))
        forget = -rate * soft * live
        upper = upper_s[...]
        hi, mid = split(forget)
        low = (forget - hi.astype(F32) - mid.astype(F32)).astype(BF16)
        total_t = mm(hi, upper) + mm(mid, upper) + mm(low, upper)
        both_t = jnp.where(gate < HEADS, strength, total_t)
        total_ts[m] = both_t
        b_hi, b_mid = split(both_t)
        b_low = (both_t - b_hi.astype(F32) - b_mid.astype(F32)).astype(BF16)
        wide = lax.dot_general(
            jnp.concatenate([b_hi, b_mid, b_low], axis=0),
            select_s[...],
            (((0,), (0,)), ((), ())),
            preferred_element_type=F32,
        )
        fades[m] = wide[:, WIDTH:]

        keys, corner, target = [None] * HEADS, [None] * HEADS, [None] * HEADS
        blocks, inverse = [None] * (2 * HEADS), [None] * (2 * HEADS)
        strict = square[0] > square[1]
        pair = (square[0] ^ square[1]) == 1
        eye = ones_where(square[0] == square[1])
        for h in heads:
            at = slice(h * K, (h + 1) * K)
            k = unit(keys_all[:, at])
            keys[h] = k
            k_hi, k_lo = split(k)
            keys_s[m, h, :, :K] = k_hi
            keys_s[m, h, :, K:] = k_lo
            gram = mm_nt(
                jnp.concatenate([k_hi, k_lo], axis=1), jnp.concatenate([k_hi, k_hi], axis=1)
            ) + mm_nt(k_hi, k_lo)
            beta = wide[:, at]
            g_col = wide[:, WIDTH + h * K : WIDTH + (h + 1) * K]
            g_row = both_t[HEADS + h : HEADS + h + 1, :]
            for b in range(2):
                part = slice(b * K, (b + 1) * K)
                gap = jnp.minimum(g_col[part] - g_row[:, part], 0.0)
                mix = jnp.where(strict, gram[part, part] * jnp.exp(gap) * beta[part], 0.0)
                blocks[2 * h + b] = split(mix)
                inverse[2 * h + b] = jnp.where(pair, -mix, 0.0).astype(BF16) + eye
            corner[h] = split(gram[K:, :K] * jnp.exp(g_col[K:] - g_row[:, :K]) * beta[K:])
            target[h] = jnp.concatenate(
                [(beta * jnp.exp(g_col)) * k, beta * values_all[:, at]], axis=1
            )
        beside = []
        if following is not None:
            wait_tokens(following)
            beside = projections(following)
        inverse = unit_lower_inverses([b[0] for b in blocks], inverse, beside)
        cross = [mm(corner[h][0], inverse[2 * h]).astype(BF16) for h in heads]
        cross = [mm(inverse[2 * h + 1], cross[h]).astype(BF16) for h in heads]
        inverse = [
            (inverse[2 * h] - eye, -cross[h], inverse[2 * h + 1] - eye) for h in heads
        ]
        shift = [lower_times(inverse[h], target[h].astype(BF16)) for h in heads]
        guess = [target[h] + shift[h] for h in heads]
        rest = [None] * HEADS
        for h in heads:
            mix = (blocks[2 * h], corner[h], blocks[2 * h + 1])
            rest[h] = -(shift[h] + lower_times_exact(mix, split(guess[h])))
        solved = [
            guess[h] + (rest[h] + lower_times(inverse[h], rest[h].astype(BF16))) for h in heads
        ]
        diagonal = square[0] == square[1]
        for h in heads:
            y = split(solved[h])
            solved_hi[m, h], solved_lo[m, h] = y
            g_col = fades[m, :, h * K : (h + 1) * K]
            g_last = g_col[ROWS - 1 : ROWS, :]
            out = three_pass(split((keys[h] * jnp.exp(g_last - g_col)).T), y)
            p = m * HEADS + h
            mw[p, :, :K] = (jnp.where(diagonal, jnp.exp(g_last), 0.0) - out[:, :K]).astype(BF16)
            mw[p, :, K:] = out[:, K:].astype(BF16)
        for turn in heads:
            h = lax.rem(c + turn, HEADS)

            @pl.when((m * HEADS + h != own_pair) & (c < CTX - 1))
            def _():
                map_copy(m, h).start()

    def state_copy(to):
        return pltpu.make_async_remote_copy(
            states.at[to], entering.at[own_pair], state_send.at[to], state_recv.at[own_pair],
            device_id={"ctx": to}, device_id_type=MESH,
        )

    def run_pair():
        maps[c] = mw[own_pair]
        for j in range(CTX - 1):

            @pl.when(c != j)
            def _():
                pltpu.make_async_remote_copy(
                    mw.at[j], maps.at[j], map_send.at[j], map_recv.at[j],
                    device_id={"ctx": j}, device_id_type=MESH,
                ).wait_recv()

        pairs = []
        for j in range(0, CTX - 2, 2):
            joined = mm(maps[j + 1, :, :K], maps[j])
            m_hi, m_lo = split(joined[:, :K])
            pairs.append(
                (
                    jnp.concatenate([m_hi, m_lo, m_hi], axis=1),
                    joined[:, K:] + maps[j + 1, :, K:].astype(F32),
                )
            )
        states[1] = maps[0, :, K:]
        state = pairs[0][1]
        even = [state]
        for step, add in pairs[1:]:
            s_hi, s_lo = split(state)
            state = add + mm(step, jnp.concatenate([s_hi, s_hi, s_lo], axis=0))
            even.append(state)
        for n, state in enumerate(even):
            j = 2 * n + 2
            s_hi, s_lo = split(state)
            states[j] = s_hi
            step = maps[j, :, :K]
            states[j + 1] = (
                maps[j, :, K:].astype(F32)
                + mm(
                    jnp.concatenate([step, step], axis=1), jnp.concatenate([s_hi, s_lo], axis=0)
                )
            ).astype(BF16)

        @pl.loop(1, CTX)
        def _(turn):
            to = lax.rem(c + turn, CTX)

            @pl.when(to > 0)
            def _():
                state_copy(to).start()

        @pl.when(c > 0)
        def _():
            entering[own_pair] = states[c]

    @pl.when(c == 0)
    def _():
        entering[...] = jnp.zeros_like(entering)

    wait_loads(0)
    wait_tokens(0)
    for work in projections(0):
        work()

    @pl.loop(1, LOCAL)
    def _(m):
        wait_loads(m)

    @pl.loop(0, LOCAL - 1)
    def _(m):
        make_maps(m, m + 1)

    @pl.when(own_stage == 0)
    def _():
        run_pair()

    make_maps(LOCAL - 1, None)

    w_copy = pltpu.make_async_remote_copy(
        wo_ref, w_other, pair_send.at[0], pair_recv.at[0], device_id=other, device_id_type=MESH
    )
    w_copy.start()
    wq_load.wait()

    def local_output(m):
        query_all = mm(xbuf[m], wq[...])
        lower = square[0] >= square[1]
        for h in heads:
            at = slice(h * K, (h + 1) * K)
            q = unit(query_all[:, at])
            q_hi, q_lo = split(q)
            k_hi, k_lo = keys_s[m, h, :, :K], keys_s[m, h, :, K:]
            gram = mm_nt(
                jnp.concatenate([q_hi, q_lo], axis=1), jnp.concatenate([k_hi, k_hi], axis=1)
            ) + mm_nt(q_hi, k_lo)
            g_col = fades[m, :, at]
            g_row = total_ts[m, HEADS + h : HEADS + h + 1, :]
            parts = []
            for b in range(2):
                part = slice(b * K, (b + 1) * K)
                gap = jnp.minimum(g_col[part] - g_row[:, part], 0.0)
                parts.append(split(jnp.where(lower, gram[part, part] * jnp.exp(gap), 0.0)))
            below = split(gram[K:, :K] * jnp.exp(g_col[K:] - g_row[:, :K]))
            out = lower_times_exact(
                (parts[0], below, parts[1]), (solved_hi[m, h], solved_lo[m, h])
            )
            base[m, :, h * K : (h + 1) * K] = out[:, K:]
            r_hi, r_lo = split(q * jnp.exp(g_col) - out[:, :K])
            reach[m, :, 2 * h * K : (2 * h + 1) * K] = r_hi
            reach[m, :, (2 * h + 1) * K : (2 * h + 2) * K] = r_lo

    def ret_copy(d, m):
        to = lax.rem(z + d, MEM)
        return pltpu.make_async_remote_copy(
            reply.at[m, to], returned.at[z, m], ret_send.at[d, m], ret_recv.at[d, m],
            device_id={"mem": to}, device_id_type=MESH,
        )

    def send_outputs(m):
        for h in heads:
            p = m * HEADS + h

            @pl.when((c > 0) & (p != own_pair))
            def _():
                pltpu.make_async_remote_copy(
                    states.at[1], entering.at[p], state_send.at[1], state_recv.at[p],
                    device_id={"ctx": owner(m, h)}, device_id_type=MESH,
                ).wait_recv()

        for h in heads:
            at = slice(h * K, (h + 1) * K)
            s = entering[m * HEADS + h]
            heads_out = base[m, :, at] + mm(
                reach[m, :, 2 * h * K : (2 * h + 2) * K], jnp.concatenate([s, s], axis=0)
            )
            scale = lax.rsqrt(jnp.mean(heads_out * heads_out, axis=1, keepdims=True) + 1e-05)
            normed = (heads_out * scale * gain_ref[:, at]).astype(BF16)
            reply[m, :, :, at] = normed.reshape(MEM, CAP, K)
        for d in (1, 3, 2):
            ret_copy(d, m).start()

    @pl.loop(0, LOCAL - 1)
    def _(m):
        @pl.when((m == 0) & (own_stage == 1))
        def _():
            run_pair()

        local_output(m)

    @pl.when(own_stage == 2)
    def _():
        run_pair()

    send_outputs(0)
    local_output(LOCAL - 1)

    @pl.loop(1, LOCAL)
    def _(m):
        @pl.when((m == 1) & (own_stage == LOCAL - 1))
        def _():
            run_pair()

        send_outputs(m)

    for d in range(1, MEM):
        count_copy(d).wait_send()

    @pl.loop(0, LOCAL)
    def _(m):
        for d in range(1, MEM):
            x_copy(d, m).wait_send()
        for d in range(MEM):
            forward(d, m).wait_send()
        for h in heads:

            @pl.when((m * HEADS + h != own_pair) & (c < CTX - 1))
            def _():
                map_copy(m, h).wait_send()

    @pl.loop(1, CTX)
    def _(j):
        @pl.when(c != j)
        def _():
            state_copy(j).wait_send()

    column = jnp.broadcast_to(slots.astype(F32), (128, TOK)).T[:, 0:1].astype(jnp.int32)

    source = [lax.rem(z + MEM - d, MEM) for d in range(MEM)]
    chosen = [
        ones_where(iota((TOK, ROWS), 1) + src * ROWS == column) for src in source
    ]
    total = mm(chosen[0], jnp.concatenate([reply[m, z] for m in range(LOCAL)], axis=0))
    for d in (1, 3, 2):
        for m in range(LOCAL):
            pltpu.make_async_remote_copy(
                reply.at[m, z], returned.at[source[d], m], ret_send.at[d, m], ret_recv.at[d, m],
                device_id={"mem": source[d]}, device_id_type=MESH,
            ).wait_recv()
        total = total + mm(chosen[d], returned[source[d]].reshape(ROWS, WIDTH))
    picked[...] = total.astype(BF16)
    swap = pltpu.make_async_remote_copy(
        picked.at[aligned(1 - half, TOK // 2)], partner, pair_send.at[1], pair_recv.at[1],
        device_id=other, device_id_type=MESH,
    )
    swap.start()
    wo_load.wait()
    mixed = mm(picked[aligned(half, TOK // 2), :], wo[...])
    w_copy.wait()
    swap.wait()
    out_ref[...] = (mixed + mm(partner[...], w_other[...])).astype(BF16)

    @pl.loop(0, LOCAL)
    def _(m):
        for d in range(1, MEM):
            ret_copy(d, m).wait_send()


def per_device(
    tokens, routes, w_query, w_key, w_value, w_beta, w_decay, decay_rate, norm_gain, w_out
):
    dma = pltpu.SemaphoreType.DMA
    vmem = pltpu.VMEM
    in_vmem = pl.BlockSpec(memory_space=pltpu.VMEM)
    in_place = pl.BlockSpec(memory_space=pl.ANY)
    return pl.pallas_call(
        layer_kernel,
        name="layer",
        out_shape=pltpu.VMEM((TOK // 2, D), BF16),
        in_specs=[
            in_place, in_place, in_place, in_place, in_place,
            in_place, in_place, in_place, in_place, in_place,
        ],
        out_specs=in_vmem,
        scratch_shapes=[
            vmem((ROWS, ROWS), BF16),
            vmem((48, 2 * WIDTH), BF16),
            vmem((LOCAL, HEADS), F32),
            vmem((1, TOK), jnp.int32),
            vmem((LOCAL, HEADS, D), BF16),
            vmem((LOCAL, HEADS, D), BF16),
            vmem((1, WIDTH), F32),
            vmem((TOK, DH), BF16),
            vmem((LOCAL, MEM, CAP, DH), BF16),
            vmem((MEM, 8, 128), F32),
            vmem((MEM, 8, 128), F32),
            vmem((LOCAL, ROWS, D), BF16),
            vmem((D, WIDTH), BF16),
            vmem((LOCAL, D, WIDTH), BF16),
            vmem((LOCAL, D, WIDTH), BF16),
            vmem((16, D), BF16),
            vmem((ROWS, 2 * WIDTH), F32),
            vmem((16, ROWS), F32),
            vmem((LOCAL, ROWS, WIDTH), F32),
            vmem((LOCAL, 16, ROWS), F32),
            vmem((LOCAL, HEADS, ROWS, 2 * K), BF16),
            vmem((LOCAL, HEADS, ROWS, 2 * K), BF16),
            vmem((LOCAL, HEADS, ROWS, 2 * K), BF16),
            vmem((CTX, K, 2 * K), BF16),
            vmem((CTX, K, 2 * K), BF16),
            vmem((CTX, K, K), BF16),
            vmem((CTX, K, K), BF16),
            vmem((LOCAL, ROWS, WIDTH), F32),
            vmem((LOCAL, ROWS, 2 * WIDTH), BF16),
            vmem((LOCAL, MEM, CAP, WIDTH), BF16),
            vmem((MEM, LOCAL, CAP, WIDTH), BF16),
            vmem((TOK, WIDTH), BF16),
            vmem((TOK // 2, WIDTH), BF16),
            vmem((WIDTH, D), BF16),
            vmem((WIDTH, D), BF16),
            dma((8,)), dma((2, LOCAL)), dma((LOCAL,)),
            dma((MEM, LOCAL)), dma((MEM, LOCAL)), dma((MEM,)), dma((MEM,)),
            dma((MEM, LOCAL)), dma((MEM, LOCAL)),
            dma((CTX,)), dma((CTX,)), dma((CTX,)), dma((CTX,)),
            dma((MEM, LOCAL)), dma((MEM, LOCAL)), dma((2,)), dma((2,)),
        ],
        compiler_params=pltpu.CompilerParams(
            collective_id=0, has_side_effects=True, vmem_limit_bytes=58 * 1024 * 1024
        ),
    )(
        decay_rate,
        routes.reshape(1, TOK),
        tokens,
        w_query,
        w_key,
        w_value,
        jnp.swapaxes(w_beta, 1, 2),
        jnp.swapaxes(w_decay, 1, 2),
        norm_gain.reshape(1, WIDTH),
        w_out,
    )


def solution(mesh):
    in_specs = (
        P(("ctx", "mem"), None),
        P(("ctx", "mem"), None),
        P(None, "half"),
        P("mem", None, "half"),
        P("mem", None, "half"),
        P("mem", None, "half"),
        P("mem", None, "half"),
        P("mem", "half"),
        P("half"),
        P("half", None),
    )
    out_specs = P(("ctx", "mem", "half"), None)
    return jax.shard_map(
        per_device, mesh=mesh, in_specs=in_specs, out_specs=out_specs, check_vma=False
    )
```
